32 devices in a mesh: wide: 8 (over z, x), narrow: 4 (over y, core).
Axes of the slice: x: 2, y: 2, z: 4, core: 2. Of those that a mesh axis runs over, the one named last changes fastest.
Arguments:
- tokens: bfloat16 [8192, 768], P(('wide', 'narrow')), may hold values from -4 to 4
- lengths: int32 [8], P('wide'), may hold values from 512 to 1024, as said below
- input_weights: bfloat16 [3, 768, 768], P(None, None, 'narrow'), may hold values from -0.4375 to 0.4375
- output_weight: bfloat16 [768, 768], P('narrow'), may hold values from -0.21875 to 0.21875
- conv_taps: float32 [12, 33], P('narrow'), may hold values from -1 to 1
- first_gain: float32 [768], replicated, may hold values from 0.5 to 1.5
- first_bias: float32 [768], replicated, may hold values from -1.8 to 1.8
- up_weight: bfloat16 [768, 3072], replicated, may hold values from -0.21875 to 0.21875
- up_bias: float32 [3072], replicated, may hold values from -1.8 to 1.8
- down_weight: bfloat16 [3072, 768], replicated, may hold values from -0.109375 to 0.109375
- down_bias: float32 [768], replicated, may hold values from -1.8 to 1.8
- second_gain: float32 [768], replicated, may hold values from 0.5 to 1.5
- second_bias: float32 [768], replicated, may hold values from -1.8 to 1.8
- cotangent: bfloat16 [8192, 768], P(('wide', 'narrow')), may hold values from -6 to 6
Outputs:
- mixed: bfloat16 [8192, 768], P(('wide', 'narrow'))
- tokens_grad: bfloat16 [8192, 768], P(('wide', 'narrow'))
- input_weights_grad: float32 [3, 768, 768], P(None, None, 'narrow')
- output_weight_grad: float32 [768, 768], P('narrow')
- conv_taps_grad: float32 [12, 33], P('narrow')
- first_gain_grad: float32 [768], replicated
- first_bias_grad: float32 [768], replicated
- up_weight_grad: float32 [768, 3072], P(None, ('wide', 'narrow'))
- up_bias_grad: float32 [3072], P(('wide', 'narrow'))
- down_weight_grad: float32 [3072, 768], P(('wide', 'narrow'))
- down_bias_grad: float32 [768], replicated
- second_gain_grad: float32 [768], replicated
- second_bias_grad: float32 [768], replicated
The draws below stay inside these ranges and needn't reach their ends.
Inputs may be any that keep to these rules, and one draw needn't show every extreme that they name: `lengths`: the true length of each sequence; positions of its slot of 1024 past it are padding; some sequence fills its slot.
All inputs are finite; a program needn't handle non-finite values.
Results may differ from the reference program's by a relative error of at most 0.018.
The reference program's roundings to bfloat16 on the way count: a program that leaves them out, or rounds other values in their place, can miss the bound.
Values may be sent and summed in bfloat16 or wider, within the bound.
No kernel may reach another device: no remote copies, remote signals or barrier semaphores. Data moves between devices by JAX's collectives and lax.ppermute only.
A program may use at most 192 MiB of HBM per device.

```python
import jax
import jax.numpy as jnp
from jax import lax

D = 768
HEADS = 12
HEAD_DIM = 64
LANDMARKS = 64
NEWTON = 6
KW = 33
FF = 3072
SLOT = 1024
SEQ_DEV = 1
GROUP = 1024
TOKENS = 8192
SEQS = 8
N_WIDE = 8


def draw_tokens(key, part):
    slow_key, fast_key = jax.random.split(jax.random.fold_in(key, 11))
    slow_part = jax.random.normal(slow_key, (TOKENS // 8, D), jnp.float32)
    fast_part = jax.random.normal(fast_key, (TOKENS, D), jnp.float32)
    combined = 0.8 * jnp.repeat(slow_part, 8, axis=0) + 0.6 * fast_part
    return jnp.clip(combined, -4.0, 4.0).astype(jnp.bfloat16)


def draw_lengths(key, part):
    base_key, full_key, half_key = jax.random.split(jax.random.fold_in(key, 23), 3)
    drawn = jax.random.randint(base_key, (SEQS,), SLOT // 2, SLOT + 1, jnp.int32)
    full_at = jax.random.randint(full_key, (), 0, SEQS, jnp.int32)
    half_at = (full_at + 1 + jax.random.randint(half_key, (), 0, SEQS - 1, jnp.int32)) % SEQS
    drawn = drawn.at[full_at].set(SLOT)
    drawn = drawn.at[half_at].set(SLOT // 2)
    return drawn


def block_levels(rng, dims, cuts, smallest, top_value):
    level, own = 1.0, jax.random.fold_in(rng, 6)
    for dim, shards_of in cuts:
        heights = jnp.exp(jax.random.uniform(jax.random.fold_in(own, dim), (shards_of,), jnp.float32, smallest / len(cuts), top_value / len(cuts)))
        level = level * jnp.repeat(heights, dims[dim] // shards_of).reshape([-1 if axis == dim else 1 for axis in range(len(dims))])
    return level


def noise(rng, shape, scale, most, cuts=(), kind=jnp.bfloat16):
    values = jax.random.normal(rng, shape, jnp.float32) * scale
    if len(cuts) > 0:
        values = block_levels(rng, shape, cuts, -0.22, 0.18) * values
    return jnp.clip(values, min=-most, max=most).astype(kind)


def setup_inputs(seed: int = 0) -> dict:
    keys = jax.random.split(jax.random.key(seed), 15)
    return {
        "tokens": draw_tokens(jax.random.fold_in(keys[14], 71), 0),
        "lengths": draw_lengths(jax.random.fold_in(keys[14], 71), 0),
        "input_weights": noise(keys[2], (3, D, D), (D // 4) ** -0.5, 0.4375, ((2, 4),)),
        "output_weight": noise(keys[3], (D, D), D ** -0.5, 0.21875, ((0, 4),)),
        "conv_taps": noise(keys[4], (HEADS, KW), KW ** -0.5, 1.0, ((0, 4),), jnp.float32),
        "first_gain": jnp.clip(1.0 + 0.1 * jax.random.normal(keys[5], (D,), jnp.float32), 0.5, 1.5),
        "first_bias": noise(keys[6], (D,), 0.3, 1.8, (), jnp.float32),
        "up_weight": noise(keys[7], (D, FF), D ** -0.5, 0.21875),
        "up_bias": noise(keys[8], (FF,), 0.3, 1.8, (), jnp.float32),
        "down_weight": noise(keys[9], (FF, D), FF ** -0.5, 0.109375),
        "down_bias": noise(keys[10], (D,), 0.3, 1.8, (), jnp.float32),
        "second_gain": jnp.clip(1.0 + 0.1 * jax.random.normal(keys[11], (D,), jnp.float32), 0.5, 1.5),
        "second_bias": noise(keys[12], (D,), 0.3, 1.8, (), jnp.float32),
        "cotangent": noise(keys[13], (TOKENS, D), 1.0, 6.0, ((0, 32),)),
    }


@jax.custom_vjp
def low(v):
    return lax.optimization_barrier(v.astype(jnp.bfloat16)).astype(jnp.float32)

@jax.custom_vjp
def low_back(v):
    return v

def low_keep(v):
    return (low(v), None)

def low_pass(kept, grad):
    return (grad,)

def back_keep(v):
    return (v, None)

def back_low(kept, grad):
    return (low(grad),)
low.defvjp(low_keep, low_pass)
low_back.defvjp(back_keep, back_low)
norm_eps = 1e-05

def exact_dot(left_side, right_side):
    return jnp.dot(left_side, right_side, precision=lax.Precision.HIGHEST)

def layer_norm(resid, gain, bias):
    center = lax.optimization_barrier(jnp.mean(resid, axis=-1, keepdims=True))
    centered = resid - center
    spread = lax.optimization_barrier(jnp.mean(centered * centered, axis=-1, keepdims=True))
    return centered * lax.rsqrt(spread + norm_eps) * gain + bias

def newton_inverse(matrix):
    identity = jnp.eye(LANDMARKS, dtype=matrix.dtype)
    col_total = jnp.max(lax.optimization_barrier(jnp.sum(matrix, axis=0)))
    approx = matrix.T / col_total
    for sweep_index in range(NEWTON):
        product = exact_dot(matrix, approx)
        inner = 7.0 * identity - product
        inner = 15.0 * identity - exact_dot(product, inner)
        inner = 13.0 * identity - exact_dot(product, inner)
        approx = 0.25 * exact_dot(approx, inner)
    return approx

def head_core(queries, keys_in, values, tap_row, length):
    slot_len = queries.shape[0]
    places = jnp.arange(slot_len, dtype=jnp.int32)
    is_live = (places < length).astype(queries.dtype)
    score_scale = HEAD_DIM ** (-0.25)
    queries = queries * is_live[:, None] * score_scale
    keys_in = keys_in * is_live[:, None] * score_scale
    landmark_ids = jnp.arange(LANDMARKS, dtype=jnp.int32)
    seg_start = landmark_ids * length // LANDMARKS
    seg_end = (landmark_ids + 1) * length // LANDMARKS
    member = ((places[:, None] >= seg_start[None, :]) & (places[:, None] < seg_end[None, :])).astype(queries.dtype)
    counts = (seg_end - seg_start).astype(queries.dtype)
    query_marks = exact_dot(member.T, queries) / counts[:, None]
    key_marks = exact_dot(member.T, keys_in) / counts[:, None]
    first_kernel = jax.nn.softmax(exact_dot(queries, key_marks.T), axis=-1)
    middle_kernel = jax.nn.softmax(exact_dot(query_marks, key_marks.T), axis=-1)
    last_kernel = jax.nn.softmax(exact_dot(query_marks, keys_in.T) + (is_live[None, :] - 1.0) * 1000000000.0, axis=-1)
    inverse = newton_inverse(middle_kernel)
    summary = exact_dot(last_kernel, values)
    mixture = exact_dot(first_kernel, exact_dot(inverse, summary))
    padded = jnp.pad(values * is_live[:, None], ((KW // 2, KW // 2), (0, 0)))
    convolved = jnp.zeros_like(values)
    for offset in range(KW):
        convolved = convolved + tap_row[offset] * padded[offset:offset + slot_len]
    return (mixture + convolved) * is_live[:, None]

def core_block(heads_in, taps_in, seq_lengths):
    per_head = jax.vmap(head_core, in_axes=(1, 1, 1, 0, None), out_axes=1)
    per_seq = jax.vmap(per_head, in_axes=(0, 0, 0, None, 0), out_axes=0)
    return per_seq(heads_in[:, :, 0], heads_in[:, :, 1], heads_in[:, :, 2], taps_in, seq_lengths)

def group_layer(block_tokens, block_lengths, input_weights, output_weight, conv_taps, first_gain, first_bias, up_weight, up_bias, down_weight, down_bias, second_gain, second_bias):
    projected = low_back(low(jnp.einsum('td,cdk->tck', block_tokens, input_weights, precision=lax.Precision.HIGHEST)))
    shaped = projected.reshape(SEQ_DEV, SLOT, 3, HEADS, HEAD_DIM)
    attended = low(core_block(shaped, conv_taps, block_lengths).reshape(GROUP, D))
    attention = low_back(exact_dot(attended, output_weight))
    normed = layer_norm(block_tokens + attention, first_gain, first_bias)
    ffn_in = low(normed)
    hidden_pre = low_back(exact_dot(ffn_in, up_weight)) + up_bias
    hidden = low(jax.nn.gelu(hidden_pre, approximate=False))
    ffn_out = low_back(exact_dot(hidden, down_weight)) + down_bias
    return layer_norm(normed + ffn_out, second_gain, second_bias)

def reference(tokens, lengths, input_weights, output_weight, conv_taps, first_gain, first_bias, up_weight, up_bias, down_weight, down_bias, second_gain, second_bias, cotangent):
    inputs_all = tokens.astype(jnp.float32).reshape(N_WIDE, GROUP, D)
    lengths_all = lengths.reshape(N_WIDE, SEQ_DEV)
    params = (input_weights.astype(jnp.float32), output_weight.astype(jnp.float32), conv_taps.astype(jnp.float32), first_gain.astype(jnp.float32), first_bias.astype(jnp.float32), up_weight.astype(jnp.float32), up_bias.astype(jnp.float32), down_weight.astype(jnp.float32), down_bias.astype(jnp.float32), second_gain.astype(jnp.float32), second_bias.astype(jnp.float32))

    def forward(inputs_in, params_in):
        saved_layer = jax.checkpoint(group_layer)

        def one_group(item):
            return saved_layer(item[0], item[1], *params_in)
        return lax.map(one_group, (inputs_in, lengths_all))
    outputs, pullback = jax.vjp(forward, inputs_all, params)
    inputs_grad, params_grad = pullback(cotangent.astype(jnp.float32).reshape(N_WIDE, GROUP, D))
    return (outputs.reshape(TOKENS, D).astype(jnp.bfloat16), inputs_grad.reshape(TOKENS, D).astype(jnp.bfloat16), params_grad[0], params_grad[1], params_grad[2], params_grad[3], params_grad[4], params_grad[5], params_grad[6], params_grad[7], params_grad[8], params_grad[9], params_grad[10])
```

```python
import jax
import jax.numpy as jnp
from jax import lax
from jax.experimental import pallas as pl
from jax.experimental.pallas import tpu as pltpu
from jax.sharding import PartitionSpec as P

BF = jnp.bfloat16
F32 = jnp.float32
HD = 64
LM = 64
KW = 33
NEWTON = 6
AXES = ("wide", "narrow")


def dot(a, b, ca, cb):
    return lax.dot_general(a, b, (((ca,), (cb,)), ((), ())), preferred_element_type=F32)

def nn(a, b): return dot(a, b, 1, 0)
def nt(a, b): return dot(a, b, 1, 1)
def tn(a, b): return dot(a, b, 0, 0)

def split(a):
    hi = a.astype(BF)
    return hi, (a - hi.astype(F32)).astype(BF)

def split3(a):
    hi = a.astype(BF)
    rest = a - hi.astype(F32)
    mid = rest.astype(BF)
    return hi, mid, (rest - mid.astype(F32)).astype(BF)

def m3(op, a, b):
    return op(a[0], b[0]) + (op(a[1], b[0]) + op(a[0], b[1]))

def m6(op, a, b):
    return op(a[0], b[0]) + ((op(a[1], b[0]) + op(a[0], b[1])) + (op(a[1], b[1]) + (op(a[2], b[0]) + op(a[0], b[2]))))

def m2l(op, a, b):
    return op(a[0], b) + op(a[1], b)

def m2r(op, a, b):
    return op(a, b[0]) + op(a, b[1])


def frame(length, slots, heads):
    n = heads * LM
    row = lax.broadcasted_iota(jnp.int32, (n, n), 0)
    col = lax.broadcasted_iota(jnp.int32, (n, n), 1)
    block = (row >> 6) == (col >> 6)
    place = lax.broadcasted_iota(jnp.int32, (1, slots), 1)
    live = place < length
    mark = lax.broadcasted_iota(jnp.int32, (n, 1), 0) & (LM - 1)
    begin = (mark * length) >> 6
    end = ((mark + 1) * length) >> 6
    member = jnp.where((place >= begin) & (place < end), 1.0, 0.0).astype(BF)
    mark_l = lax.broadcasted_iota(jnp.int32, (1, n), 1) & (LM - 1)
    count_l = ((((mark_l + 1) * length) >> 6) - ((mark_l * length) >> 6)).astype(F32)
    count_s = (end - begin).astype(F32)
    return block, live, member, 1.0 / count_s, 1.0 / count_l


def head_lane_max(row, heads):
    lane = lax.broadcasted_iota(jnp.int32, row.shape, 1) >> 6
    out = jnp.zeros_like(row)
    for h in range(heads):
        top = jnp.max(jnp.where(lane == h, row, -1.0), axis=1, keepdims=True)
        out = jnp.where(lane == h, top, out)
    return out


def head_lane_sum(row, heads):
    lane = lax.broadcasted_iota(jnp.int32, row.shape, 1) >> 6
    out = jnp.zeros_like(row)
    for h in range(heads):
        total = jnp.sum(jnp.where(lane == h, row, 0.0), axis=1, keepdims=True)
        out = jnp.where(lane == h, total, out)
    return out


def windows(arr, h):
    slots = arr.shape[1]
    rows = arr[HD * h : HD * (h + 1)]
    zero = jnp.zeros((HD, 128), arr.dtype)
    wide = jnp.concatenate([zero, rows, zero], axis=1)
    return jnp.concatenate([wide[:, 128 * b : 128 * b + 384] for b in range(slots // 128)], axis=0)


def conv_apply(arr, taps_hi, taps_lo, heads):
    slots = arr.shape[1]
    parts = []
    for h in range(heads):
        win = windows(arr, h)
        out = nn(win, taps_hi[h]) + nn(win, taps_lo[h])
        parts.append(jnp.concatenate([out[HD * b : HD * (b + 1)] for b in range(slots // 128)], axis=1))
    return jnp.concatenate(parts, axis=0)


def core_forward(q, k, v, length, taps_hi, taps_lo):
    n, slots = q.shape
    heads = n // HD
    block, live, member, inv_s, inv_l = frame(length, slots, heads)
    k_land = jnp.where(block, nt(member, k), 0.0) * inv_s
    q_land = jnp.where(block, nt(member, q), 0.0) * inv_s
    k3, q3 = split3(k_land), split3(q_land)
    x2 = m6(nt, q3, k3) * 0.125
    x2 = jnp.where(block, x2, -1e30)
    e2 = jnp.exp(x2 - jnp.max(x2, axis=1, keepdims=True))
    mid = e2 * (1.0 / jnp.sum(e2, axis=1, keepdims=True))
    cols = jnp.sum(mid, axis=0, keepdims=True)
    inv_max = 1.0 / head_lane_max(cols, heads)
    x3 = m2l(nn, q3[:2], k) * 0.125 + jnp.where(live, 0.0, -1e9)
    e3 = jnp.exp(x3 - jnp.max(x3, axis=1, keepdims=True))
    last = e3 * (1.0 / jnp.sum(e3, axis=1, keepdims=True))
    last_s = split(last)
    x1 = (m2l(nn, k3[:2], q) * 0.125).reshape(heads, LM, slots)
    e1 = jnp.exp(x1 - jnp.max(x1, axis=1, keepdims=True))
    first = (e1 * (1.0 / jnp.sum(e1, axis=1, keepdims=True))).reshape(n, slots)
    first_s = split(first)
    eye = jnp.where(lax.broadcasted_iota(jnp.int32, (n, n), 0) == lax.broadcasted_iota(jnp.int32, (n, n), 1), 1.0, 0.0)
    mid_s = split(mid)
    p = m3(nt, mid_s, mid_s) * inv_max
    root = None
    kept = []
    for step in range(NEWTON):
        ps = split(p)
        p2 = m3(nn, ps, ps)
        p2s = split(p2)
        p3 = m3(nn, p2s, ps)
        poly = 0.25 * (13.0 * eye - 15.0 * p + 7.0 * p2 - p3)
        kept.append((p, p2, p3, root))
        if step < NEWTON - 1:
            p4 = m3(nn, p2s, p2s)
            p = 0.25 * (13.0 * p - 15.0 * p2 + 7.0 * p3 - p4)
        root = poly if root is None else m3(nn, split(root), split(poly))
    root_s = split(root)
    mid_t = split(mid.T)
    z = m3(nn, mid_t, root_s) * inv_max
    z_s = split(z)
    sum_t = jnp.where(block, m2r(nt, v, last_s), 0.0)
    y_t = m3(nt, split(sum_t), z_s)
    out = m3(nn, split(y_t), first_s)
    out = out + conv_apply(jnp.where(live, v, jnp.zeros_like(v)), taps_hi, taps_lo, heads)
    att = jnp.where(live, out, 0.0).astype(BF)
    return att, first, last, mid, z, sum_t, y_t, root, kept, k_land, q_land


def core_backward(g, q, k, v, length, first, last, mid, z, sum_t, y_t, root, kept, k_land, q_land, rev_hi, rev_lo):
    n, slots = q.shape
    heads = n // HD
    block, live, member, inv_s, inv_l = frame(length, slots, heads)
    g = jnp.where(live, g, jnp.zeros_like(g))
    first_s, last_s = split(first), split(last)
    mid_s = split(mid)
    cols = jnp.sum(mid, axis=0, keepdims=True)
    top = head_lane_max(cols, heads)
    inv_max = 1.0 / top
    z_s = split(z)
    y = y_t.T
    dfirst = m2l(nn, split(y), g)
    dy_t = jnp.where(block, m2r(nt, g, first_s), 0.0)
    dy = dy_t.T
    dy_s, dyt_s, st_s = split(dy), split(dy_t), split(sum_t)
    s_s = split(sum_t.T)
    dz = m3(nn, dy_s, st_s)
    dz_t = m3(nn, s_s, dyt_s)
    ds_t = m3(nn, dyt_s, z_s)
    ds = ds_t.T
    dlast = m2l(nn, split(ds), v)
    dv = m3(nn, split(ds_t), last_s)
    dv = dv + jnp.where(live, conv_apply(g, rev_hi, rev_lo, heads), 0.0)
    dx3 = last * (dlast - jnp.sum(dlast * last, axis=1, keepdims=True)) * 0.125
    f3 = first.reshape(heads, LM, slots)
    d3 = dfirst.reshape(heads, LM, slots)
    dx1 = (f3 * (d3 - jnp.sum(d3 * f3, axis=1, keepdims=True)) * 0.125).reshape(n, slots)
    root_s = split(root)
    dz_s, dzt_s = split(dz), split(dz_t)
    dmid = m3(nn, root_s, dzt_s) * inv_max
    droot = m3(nn, mid_s, dz_s) * inv_max
    dtop = -jnp.sum(dz * z, axis=0, keepdims=True)
    dp = None
    for step in range(NEWTON - 1, -1, -1):
        p, p2, p3, before = kept[step]
        ps, p2s = split(p), split(p2)
        if before is None:
            dpoly = 0.25 * droot
        else:
            eye = jnp.where(lax.broadcasted_iota(jnp.int32, (n, n), 0) == lax.broadcasted_iota(jnp.int32, (n, n), 1), 1.0, 0.0)
            poly = 0.25 * (13.0 * eye - 15.0 * p + 7.0 * p2 - p3)
            droot_s = split(droot)
            dpoly = 0.25 * m3(nn, split(before), droot_s)
            droot = m3(nn, droot_s, split(poly))
        d1 = -15.0 * dpoly
        d2 = 7.0 * dpoly
        d3_ = -dpoly
        if dp is not None:
            e = 0.25 * dp
            d1 = d1 + 13.0 * e
            d2 = d2 - 15.0 * e
            d3_ = d3_ + 7.0 * e
            es = split(e)
            d2 = d2 - (m3(nn, es, p2s) + m3(nn, p2s, es))
        d3s = split(d3_)
        d2 = d2 + m3(nn, d3s, ps)
        d1 = d1 + m3(nn, p2s, d3s)
        d2s = split(d2)
        dp = d1 + (m3(nn, d2s, ps) + m3(nn, ps, d2s))
    dmid = dmid + m3(nn, split(dp + dp.T), mid_s) * inv_max
    dtop = dtop - jnp.sum(dp * kept[0][0], axis=0, keepdims=True)
    dtop = head_lane_sum(dtop, heads) * inv_max
    hit = jnp.where(cols == top, 1.0, 0.0)
    dmid = dmid + jnp.where(block, dtop * hit / head_lane_sum(hit, heads), 0.0)
    dx2 = mid * (dmid - jnp.sum(dmid * mid, axis=1, keepdims=True)) * 0.125
    dx2_s = split(dx2)
    dx1_s, dx3_s = split(dx1), split(dx3)
    kt_s, qt_s = split(k_land.T), split(q_land.T)
    dql_t = (jnp.where(block, m2r(nt, k, dx3_s), 0.0) + m3(nt, kt_s, dx2_s)) * inv_l
    dkl_t = (jnp.where(block, m2r(nt, q, dx1_s), 0.0) + m3(nn, qt_s, dx2_s)) * inv_l
    dq = m3(nn, kt_s, dx1_s) + m2l(nn, split(dql_t), member)
    dk = m3(nn, qt_s, dx3_s) + m2l(nn, split(dkl_t), member)
    corr = []
    vm = jnp.where(live, v, jnp.zeros_like(v))
    ri = lax.broadcasted_iota(jnp.int32, (128, 128), 0)
    ci = lax.broadcasted_iota(jnp.int32, (128, 128), 1)
    flip = jnp.where(ri + ci == 127, 1.0, 0.0).astype(BF)
    for h in range(heads):
        rows = g[HD * h : HD * (h + 1)]
        stack = jnp.concatenate([rows[:, 128 * b : 128 * b + 128] for b in range(slots // 128)], axis=0)
        near = tn(nn(stack, flip).astype(BF), windows(vm, h))
        near = pltpu.roll(near, 0, axis=1, stride=1, stride_axis=0)
        corr.append(jnp.sum(near, axis=0, keepdims=True))
    return dq, dk, dv, corr


N_KEPT = 3 * NEWTON + NEWTON - 1


def forward_kernel(info, x0, x1, x2, x3, wt, tap, att_out, proj, first_o, last_o, mats, kept_o, att_s):
    nar, length = info[0], info[1]
    rows = x0.shape[0]
    count = 4
    offs = [pl.multiple_of((nar ^ r) * rows, rows) for r in range(count)]
    for r, x in enumerate((x0, x1, x2, x3)):
        proj[:, pl.ds(offs[r], rows)] = nt(wt[...], x[...]).astype(BF)
    n = wt.shape[0] // 3
    q, k, v = proj[0:n, :], proj[n:2 * n, :], proj[2 * n:3 * n, :]
    pairs = [split(tap[h]) for h in range(tap.shape[0])]
    att, first, last, mid, z, sum_t, y_t, root, kept, k_land, q_land = core_forward(
        q, k, v, length, [a for a, _ in pairs], [b for _, b in pairs])
    att_s[...] = att
    for r in range(count):
        att_out[r] = att_s[:, pl.ds(offs[r], rows)]
    first_o[...] = first
    last_o[...] = last
    for i, m in enumerate((mid, z, sum_t, y_t, root, k_land, q_land)):
        mats[i] = m
    i = 0
    for p, p2, p3, before in kept:
        for m in (p, p2, p3):
            kept_o[i] = m
            i += 1
    for _, _, _, before in kept[1:]:
        kept_o[i] = before
        i += 1


def forward_call(info, xs, wt, tap):
    rows, width = xs[0].shape
    n = wt.shape[0] // 3
    slots = 4 * rows
    vm = pl.BlockSpec(memory_space=pltpu.VMEM)
    return pl.pallas_call(
        forward_kernel,
        in_specs=[pl.BlockSpec(memory_space=pltpu.SMEM)] + [vm] * 6,
        out_specs=[vm] * 6,
        out_shape=[
            jax.ShapeDtypeStruct((4, n, rows), BF),
            jax.ShapeDtypeStruct((3 * n, slots), BF),
            jax.ShapeDtypeStruct((n, slots), F32),
            jax.ShapeDtypeStruct((n, slots), F32),
            jax.ShapeDtypeStruct((7, n, n), F32),
            jax.ShapeDtypeStruct((N_KEPT, n, n), F32),
        ],
        scratch_shapes=[pltpu.VMEM((n, slots), BF)],
        compiler_params=pltpu.CompilerParams(vmem_limit_bytes=48 << 20),
        name="core_forward",
    )(info, *xs, wt, tap)


def backward_kernel(info, g0, g1, g2, g3, proj, first_i, last_i, mats, kept_i, x0, x1, x2, x3, wt, rev,
                    dx, in_grad, taps_o, g_s, dp_s):
    nar, length = info[0], info[1]
    rows = x0.shape[0]
    offs = [pl.multiple_of((nar ^ r) * rows, rows) for r in range(4)]
    for r, g in enumerate((g0, g1, g2, g3)):
        g_s[:, pl.ds(offs[r], rows)] = g[...]
    n = wt.shape[0] // 3
    q, k, v = proj[0:n, :], proj[n:2 * n, :], proj[2 * n:3 * n, :]
    mid, z, sum_t, y_t, root, k_land, q_land = [mats[i] for i in range(7)]
    kept = []
    for step in range(NEWTON):
        kept.append(tuple(kept_i[3 * step + i] for i in range(3)) + ((kept_i[3 * NEWTON + step - 1] if step else None),))
    pairs = [split(rev[h]) for h in range(rev.shape[0])]
    dq, dk, dv, corr = core_backward(g_s[...], q, k, v, length, first_i[...], last_i[...], mid, z, sum_t, y_t, root,
                                     kept, k_land, q_land, [a for a, _ in pairs], [b for _, b in pairs])
    dp_s[0:n, :] = dq.astype(BF)
    dp_s[n:2 * n, :] = dk.astype(BF)
    dp_s[2 * n:3 * n, :] = dv.astype(BF)
    for h, c in enumerate(corr):
        taps_o[h : h + 1, :] = c
    total = None
    for r, x in enumerate((x0, x1, x2, x3)):
        block = dp_s[:, pl.ds(offs[r], rows)]
        dx[r] = tn(block, wt[...]).astype(BF)
        term = nn(block, x[...])
        total = term if total is None else total + term
    in_grad[...] = total.astype(BF)


def backward_call(info, gs, proj, first, last, mats, kept, xs, wt, rev):
    rows, width = xs[0].shape
    n = wt.shape[0] // 3
    slots = 4 * rows
    vm = pl.BlockSpec(memory_space=pltpu.VMEM)
    return pl.pallas_call(
        backward_kernel,
        in_specs=[pl.BlockSpec(memory_space=pltpu.SMEM)] + [vm] * 15,
        out_specs=[vm] * 3,
        out_shape=[
            jax.ShapeDtypeStruct((4, rows, width), BF),
            jax.ShapeDtypeStruct((3 * n, width), BF),
            jax.ShapeDtypeStruct((n // HD, 384), F32),
        ],
        scratch_shapes=[pltpu.VMEM((n, slots), BF), pltpu.VMEM((3 * n, slots), BF)],
        compiler_params=pltpu.CompilerParams(vmem_limit_bytes=56 << 20),
        name="core_backward",
    )(info, *gs, proj, first, last, mats, kept, *xs, wt, rev)


norm_eps = 1e-05


def layer_norm(resid, gain, bias):
    center = jnp.mean(resid, axis=-1, keepdims=True)
    centered = resid - center
    spread = jnp.mean(centered * centered, axis=-1, keepdims=True)
    inverse = lax.rsqrt(spread + norm_eps)
    normalized = centered * inverse
    return (normalized * gain + bias, (normalized, inverse))


def norm_back(grad_out, stats, gain):
    normalized, inverse = stats
    scaled = grad_out * gain
    resid_grad = inverse * (
        scaled
        - jnp.mean(scaled, axis=-1, keepdims=True)
        - normalized * jnp.mean(scaled * normalized, axis=-1, keepdims=True)
    )
    return (resid_grad, jnp.sum(grad_out * normalized, axis=0), jnp.sum(grad_out, axis=0))


def gelu_exact(values):
    return jax.nn.gelu(values, approximate=False)


def toeplitz(taps):
    i = lax.broadcasted_iota(jnp.int32, (384, 128), 0)
    t = lax.broadcasted_iota(jnp.int32, (384, 128), 1)

    def pick(index):
        out = jnp.zeros((taps.shape[0], 384, 128), F32)
        for w in range(KW):
            out = jnp.where(index == w, taps[:, w][:, None, None], out)
        return out

    return pick(i - t - 112), pick(t - i + 144)


def build(mesh):
    n_wide, n_narrow = mesh.shape["wide"], mesh.shape["narrow"]
    count = n_wide * n_narrow
    wide_bits = []
    bit = n_narrow
    while bit < count:
        wide_bits.append(bit)
        bit *= 2

    def swap(block, mask):
        return lax.ppermute(block, AXES, [(i, i ^ mask) for i in range(count)])

    def halve(me, parts, axis, mask):
        mine = (me & mask) // mask
        sent = lax.dynamic_index_in_dim(parts, 1 - mine, axis, keepdims=False)
        kept = lax.dynamic_index_in_dim(parts, mine, axis, keepdims=False)
        came = swap(sent, mask)
        return (kept.astype(F32) + came.astype(F32)).astype(BF)

    def double(me, block, mask):
        came = swap(block, mask)
        mine = (me & mask) // mask
        low = jnp.where(mine == 0, block, came)
        high = jnp.where(mine == 0, came, block)
        return jnp.concatenate([low, high], axis=0)

    def gather_relative(block):
        far = swap(block, 2)
        near = swap(block, 1)
        return [block, near, far, swap(far, 1)]

    def exchange_relative(blocks):
        return [blocks[r] if r == 0 else swap(blocks[r], r) for r in range(n_narrow)]

    def reduce_relative(blocks):
        came = swap(jnp.stack([blocks[1], blocks[3]]), 1).astype(F32)
        far = (blocks[2].astype(F32) + came[1]).astype(BF)
        return blocks[0].astype(F32) + came[0] + swap(far, 2).astype(F32)

    def reduce_part(me, part, order):
        masks = sorted(order, reverse=True)
        shaped = part.reshape([2] * len(masks) + list(part.shape[-2:]))
        for mask in order:
            axis = masks.index(mask)
            shaped = halve(me, shaped, axis, mask)
            masks.pop(axis)
        return shaped

    def on_device(
        tokens,
        lengths,
        input_weights,
        output_weight,
        conv_taps,
        first_gain,
        first_bias,
        up_weight,
        up_bias,
        down_weight,
        down_bias,
        second_gain,
        second_bias,
        cotangent,
    ):
        me = lax.axis_index(AXES)
        nar = lax.axis_index("narrow")
        rows, width = tokens.shape
        local_width = input_weights.shape[2]
        info = jnp.stack([nar.astype(jnp.int32), lengths[0]])
        weights_t = jnp.swapaxes(input_weights, 1, 2).reshape(3 * local_width, width)
        conv_mat, conv_rev = toeplitz(conv_taps)
        token_blocks = gather_relative(tokens)
        out_rel = jnp.concatenate(gather_relative(output_weight), axis=0)
        att, proj, first, last, mats, kept = forward_call(info, token_blocks, weights_t, conv_mat)
        own_att = jnp.concatenate(
            exchange_relative([att[r] for r in range(n_narrow)]), axis=0
        )
        outer_dims = (((0,), (0,)), ((), ()))
        inner_dims = (((1,), (1,)), ((), ()))

        def outer(a, b):
            return lax.dot_general(a, b, outer_dims, preferred_element_type=F32)

        def inner(a, b):
            return lax.dot_general(a, b, inner_dims, preferred_element_type=F32)

        attention = outer(own_att, out_rel)
        normed, first_stats = layer_norm(tokens.astype(F32) + attention, first_gain, first_bias)
        ffn_in = normed.astype(BF)
        hidden_pre = jnp.dot(ffn_in, up_weight, preferred_element_type=F32) + up_bias
        hidden_out, gelu_pull = jax.vjp(gelu_exact, hidden_pre)
        hidden_low = hidden_out.astype(BF)
        ffn_out = jnp.dot(hidden_low, down_weight, preferred_element_type=F32) + down_bias
        mixed, second_stats = layer_norm(normed + ffn_out, second_gain, second_bias)
        second_in_grad, second_gain_grad, second_bias_grad = norm_back(
            cotangent.astype(F32), second_stats, second_gain
        )
        down_bias_grad = jnp.sum(second_in_grad, axis=0)
        ffn_grad_low = second_in_grad.astype(BF)
        down_grad = outer(hidden_low, ffn_grad_low).astype(BF)
        hidden_grad = inner(ffn_grad_low, down_weight)
        pre_grad = gelu_pull(hidden_grad)[0]
        up_bias_part = jnp.sum(pre_grad, axis=0)
        pre_low = pre_grad.astype(BF)
        up_grad_t = outer(pre_low, ffn_in).astype(BF)
        normed_grad = second_in_grad + inner(pre_low, up_weight)
        first_in_grad, first_gain_grad, first_bias_grad = norm_back(
            normed_grad, first_stats, first_gain
        )
        attn_grad = first_in_grad.astype(BF)
        own_att_grad = inner(out_rel, attn_grad).astype(BF)
        att_grad_blocks = exchange_relative(
            [own_att_grad[r * local_width : (r + 1) * local_width] for r in range(n_narrow)]
        )
        input_term, input_grad_t, taps_grad = backward_call(
            info, att_grad_blocks, proj, first, last, mats, kept, token_blocks, weights_t, conv_rev
        )
        input_sum = reduce_relative([input_term[r] for r in range(n_narrow)])
        tokens_grad = (first_in_grad + input_sum).astype(BF)

        ff_rows = up_weight.shape[1] // count
        grads = jnp.concatenate(
            [
                up_grad_t.reshape(count, ff_rows, width),
                down_grad.reshape(count, ff_rows, width),
                jnp.pad(
                    up_bias_part.astype(BF).reshape(count, 1, ff_rows),
                    ((0, 0), (0, 7), (0, width - ff_rows)),
                ),
            ],
            axis=1,
        )
        chunk = grads.shape[1]
        half_width = width // 2
        grads_core = halve(me, grads.reshape(n_wide * 2, 2, chunk, width), 1, 1)
        left = reduce_part(me, grads_core[..., :half_width], [2] + wide_bits)
        right = reduce_part(
            me, grads_core[..., half_width:], [wide_bits[0], 2] + wide_bits[1:]
        )
        ffn_sums = jnp.concatenate([left, right], axis=1).astype(F32)
        up_out = ffn_sums[:ff_rows].T
        down_out = ffn_sums[ff_rows : 2 * ff_rows]
        up_bias_out = ffn_sums[2 * ff_rows, :ff_rows]

        output_part = jnp.dot(own_att, attn_grad, preferred_element_type=F32)
        output_part = output_part.astype(BF).reshape(n_narrow, local_width, width)
        output_sum = reduce_relative([output_part[r] for r in range(n_narrow)])
        vectors = jnp.stack(
            [first_gain_grad, first_bias_grad, down_bias_grad, second_gain_grad, second_bias_grad]
        )
        vectors = vectors + swap(vectors, 1)
        vectors = vectors + swap(vectors, 2)
        taps_row = jnp.pad(
            taps_grad[:, 239 : 239 + KW].reshape(1, -1), ((0, 0), (0, width - conv_taps.size))
        )
        used = 4 * local_width + 6
        total_rows = -(-used // (n_wide * 8)) * n_wide * 8
        pool = jnp.concatenate(
            [
                input_grad_t,
                output_sum.astype(BF),
                vectors.astype(BF),
                taps_row.astype(BF),
                jnp.zeros((total_rows - used, width), BF),
            ],
            axis=0,
        ).reshape(n_wide, total_rows // n_wide, width)
        pool = reduce_part(me, pool, wide_bits)
        for mask in wide_bits:
            pool = double(me, pool, mask)
        pool = pool.astype(F32)
        first_rows = 3 * local_width
        input_out = pool[:first_rows].reshape(3, local_width, width).transpose(0, 2, 1)
        output_out = pool[first_rows : first_rows + local_width]
        vec = pool[first_rows + local_width : first_rows + local_width + 5]
        taps_out = pool[first_rows + local_width + 5, : conv_taps.size].reshape(conv_taps.shape)
        return (
            mixed.astype(BF),
            tokens_grad,
            input_out,
            output_out,
            taps_out,
            vec[0],
            vec[1],
            up_out,
            up_bias_out,
            down_out,
            vec[2],
            vec[3],
            vec[4],
        )

    return on_device


def solution(mesh):
    spread = P(AXES, None)
    placed = (
        spread,
        P("wide"),
        P(None, None, "narrow"),
        P("narrow", None),
        P("narrow", None),
        P(),
        P(),
        P(),
        P(),
        P(),
        P(),
        P(),
        P(),
        spread,
    )
    results = (
        spread,
        spread,
        P(None, None, "narrow"),
        P("narrow", None),
        P("narrow", None),
        P(),
        P(),
        P(None, AXES),
        P(AXES),
        spread,
        P(),
        P(),
        P(),
    )
    return jax.shard_map(
        build(mesh), mesh=mesh, in_specs=placed, out_specs=results, check_vma=False
    )
```

```python
import functools
import jax
import jax.numpy as jnp
from jax import lax
from jax.experimental import pallas as pl
from jax.experimental.pallas import tpu as pltpu
from jax.sharding import PartitionSpec as P

BF = jnp.bfloat16
F32 = jnp.float32
HD = 64
LM = 64
KW = 33
NEWTON = 6
AXES = ("wide", "narrow")


def dot(a, b, ca, cb):
    return lax.dot_general(a, b, (((ca,), (cb,)), ((), ())), preferred_element_type=F32)

def nn(a, b): return dot(a, b, 1, 0)
def nt(a, b): return dot(a, b, 1, 1)
def tn(a, b): return dot(a, b, 0, 0)

def split(a):
    hi = a.astype(BF)
    return hi, (a - hi.astype(F32)).astype(BF)

def split3(a):
    hi = a.astype(BF)
    rest = a - hi.astype(F32)
    mid = rest.astype(BF)
    return hi, mid, (rest - mid.astype(F32)).astype(BF)

def m3(op, a, b):
    return op(a[0], b[0]) + (op(a[1], b[0]) + op(a[0], b[1]))

def m6(op, a, b):
    return op(a[0], b[0]) + ((op(a[1], b[0]) + op(a[0], b[1])) + (op(a[1], b[1]) + (op(a[2], b[0]) + op(a[0], b[2]))))

def m2l(op, a, b):
    return op(a[0], b) + op(a[1], b)

def m2r(op, a, b):
    return op(a, b[0]) + op(a, b[1])


def frame(length, slots, heads):
    n = heads * LM
    row = lax.broadcasted_iota(jnp.int32, (n, n), 0)
    col = lax.broadcasted_iota(jnp.int32, (n, n), 1)
    block = (row >> 6) == (col >> 6)
    place = lax.broadcasted_iota(jnp.int32, (1, slots), 1)
    live = place < length
    mark = lax.broadcasted_iota(jnp.int32, (n, 1), 0) & (LM - 1)
    begin = (mark * length) >> 6
    end = ((mark + 1) * length) >> 6
    member = jnp.where((place >= begin) & (place < end), 1.0, 0.0).astype(BF)
    mark_l = lax.broadcasted_iota(jnp.int32, (1, n), 1) & (LM - 1)
    count_l = ((((mark_l + 1) * length) >> 6) - ((mark_l * length) >> 6)).astype(F32)
    count_s = (end - begin).astype(F32)
    return block, live, member, 1.0 / count_s, 1.0 / count_l


def head_lane_max(row, heads):
    lane = lax.broadcasted_iota(jnp.int32, row.shape, 1) >> 6
    out = jnp.zeros_like(row)
    for h in range(heads):
        top = jnp.max(jnp.where(lane == h, row, -1.0), axis=1, keepdims=True)
        out = jnp.where(lane == h, top, out)
    return out


def head_lane_sum(row, heads):
    lane = lax.broadcasted_iota(jnp.int32, row.shape, 1) >> 6
    out = jnp.zeros_like(row)
    for h in range(heads):
        total = jnp.sum(jnp.where(lane == h, row, 0.0), axis=1, keepdims=True)
        out = jnp.where(lane == h, total, out)
    return out


def windows(arr, h):
    slots = arr.shape[1]
    rows = arr[HD * h : HD * (h + 1)]
    zero = jnp.zeros((HD, 128), arr.dtype)
    wide = jnp.concatenate([zero, rows, zero], axis=1)
    return jnp.concatenate([wide[:, 128 * b : 128 * b + 384] for b in range(slots // 128)], axis=0)


def bands(base):
    out = []
    for h in range(base.shape[0]):
        spread = jnp.broadcast_to(base[h : h + 1, :], (128, 384))
        out.append(split(pltpu.roll(spread, 0, axis=1, stride=1, stride_axis=0)))
    return out


def conv_apply(arr, band, heads):
    slots = arr.shape[1]
    parts = []
    for h in range(heads):
        out = m2r(nt, windows(arr, h), band[h])
        parts.append(jnp.concatenate([out[HD * b : HD * (b + 1)] for b in range(slots // 128)], axis=1))
    return jnp.concatenate(parts, axis=0)


def core_forward(q, k, v, length, band):
    n, slots = q.shape
    heads = n // HD
    block, live, member, inv_s, inv_l = frame(length, slots, heads)
    k_land = jnp.where(block, nt(member, k), 0.0) * inv_s
    q_land = jnp.where(block, nt(member, q), 0.0) * inv_s
    k3, q3 = split3(k_land), split3(q_land)
    x2 = m6(nt, q3, k3) * 0.125
    x2 = jnp.where(block, x2, -1e30)
    e2 = jnp.exp(x2 - jnp.max(x2, axis=1, keepdims=True))
    mid = e2 * (1.0 / jnp.sum(e2, axis=1, keepdims=True))
    cols = jnp.sum(mid, axis=0, keepdims=True)
    inv_max = 1.0 / head_lane_max(cols, heads)
    x3 = m2l(nn, q3[:2], k) * 0.125 + jnp.where(live, 0.0, -1e9)
    e3 = jnp.exp(x3 - jnp.max(x3, axis=1, keepdims=True))
    last = e3 * (1.0 / jnp.sum(e3, axis=1, keepdims=True))
    last_s = split(last)
    x1 = (m2l(nn, k3[:2], q) * 0.125).reshape(heads, LM, slots)
    e1 = jnp.exp(x1 - jnp.max(x1, axis=1, keepdims=True))
    first = (e1 * (1.0 / jnp.sum(e1, axis=1, keepdims=True))).reshape(n, slots)
    first_s = split(first)
    eye = jnp.where(lax.broadcasted_iota(jnp.int32, (n, n), 0) == lax.broadcasted_iota(jnp.int32, (n, n), 1), 1.0, 0.0)
    mid_s = split(mid)
    p = m3(nt, mid_s, mid_s) * inv_max
    root = None
    kept = []
    for step in range(NEWTON):
        ps = split(p)
        p2 = m3(nn, ps, ps)
        p2s = split(p2)
        p3 = m3(nn, p2s, ps)
        poly = 0.25 * (13.0 * eye - 15.0 * p + 7.0 * p2 - p3)
        kept.append((p, p2, p3, root))
        if step < NEWTON - 1:
            p4 = m3(nn, p2s, p2s)
            p = 0.25 * (13.0 * p - 15.0 * p2 + 7.0 * p3 - p4)
        root = poly if root is None else m3(nn, split(root), split(poly))
    root_s = split(root)
    mid_t = split(mid.T)
    z = m3(nn, mid_t, root_s) * inv_max
    z_s = split(z)
    sum_t = jnp.where(block, m2r(nt, v, last_s), 0.0)
    y_t = m3(nt, split(sum_t), z_s)
    out = m3(nn, split(y_t), first_s)
    out = out + conv_apply(jnp.where(live, v, jnp.zeros_like(v)), band, heads)
    att = jnp.where(live, out, 0.0).astype(BF)
    return att, first, last, mid, z, sum_t, y_t, root, kept, k_land, q_land


def core_backward(g, q, k, v, length, first, last, mid, z, sum_t, y_t, root, kept, k_land, q_land, band):
    n, slots = q.shape
    heads = n // HD
    block, live, member, inv_s, inv_l = frame(length, slots, heads)
    g = jnp.where(live, g, jnp.zeros_like(g))
    first_s, last_s = split(first), split(last)
    mid_s = split(mid)
    cols = jnp.sum(mid, axis=0, keepdims=True)
    top = head_lane_max(cols, heads)
    inv_max = 1.0 / top
    z_s = split(z)
    y = y_t.T
    dfirst = m2l(nn, split(y), g)
    dy_t = jnp.where(block, m2r(nt, g, first_s), 0.0)
    dy = dy_t.T
    dy_s, dyt_s, st_s = split(dy), split(dy_t), split(sum_t)
    s_s = split(sum_t.T)
    dz = m3(nn, dy_s, st_s)
    dz_t = m3(nn, s_s, dyt_s)
    ds_t = m3(nn, dyt_s, z_s)
    ds = ds_t.T
    dlast = m2l(nn, split(ds), v)
    dv = m3(nn, split(ds_t), last_s)
    dv = dv + jnp.where(live, conv_apply(g, band, heads), 0.0)
    dx3 = last * (dlast - jnp.sum(dlast * last, axis=1, keepdims=True)) * 0.125
    f3 = first.reshape(heads, LM, slots)
    d3 = dfirst.reshape(heads, LM, slots)
    dx1 = (f3 * (d3 - jnp.sum(d3 * f3, axis=1, keepdims=True)) * 0.125).reshape(n, slots)
    root_s = split(root)
    dz_s, dzt_s = split(dz), split(dz_t)
    dmid = m3(nn, root_s, dzt_s) * inv_max
    droot = m3(nn, mid_s, dz_s) * inv_max
    dtop = -jnp.sum(dz * z, axis=0, keepdims=True)
    dp = None
    for step in range(NEWTON - 1, -1, -1):
        p, p2, p3, before = kept[step]
        ps, p2s = split(p), split(p2)
        if before is None:
            dpoly = 0.25 * droot
        else:
            eye = jnp.where(lax.broadcasted_iota(jnp.int32, (n, n), 0) == lax.broadcasted_iota(jnp.int32, (n, n), 1), 1.0, 0.0)
            poly = 0.25 * (13.0 * eye - 15.0 * p + 7.0 * p2 - p3)
            droot_s = split(droot)
            dpoly = 0.25 * m3(nn, split(before), droot_s)
            droot = m3(nn, droot_s, split(poly))
        d1 = -15.0 * dpoly
        d2 = 7.0 * dpoly
        d3_ = -dpoly
        if dp is not None:
            e = 0.25 * dp
            d1 = d1 + 13.0 * e
            d2 = d2 - 15.0 * e
            d3_ = d3_ + 7.0 * e
            es = split(e)
            d2 = d2 - (m3(nn, es, p2s) + m3(nn, p2s, es))
        d3s = split(d3_)
        d2 = d2 + m3(nn, d3s, ps)
        d1 = d1 + m3(nn, p2s, d3s)
        d2s = split(d2)
        dp = d1 + (m3(nn, d2s, ps) + m3(nn, ps, d2s))
    dmid = dmid + m3(nn, split(dp + dp.T), mid_s) * inv_max
    dtop = dtop - jnp.sum(dp * kept[0][0], axis=0, keepdims=True)
    dtop = head_lane_sum(dtop, heads) * inv_max
    hit = jnp.where(cols == top, 1.0, 0.0)
    dmid = dmid + jnp.where(block, dtop * hit / head_lane_sum(hit, heads), 0.0)
    dx2 = mid * (dmid - jnp.sum(dmid * mid, axis=1, keepdims=True)) * 0.125
    dx2_s = split(dx2)
    dx1_s, dx3_s = split(dx1), split(dx3)
    kt_s, qt_s = split(k_land.T), split(q_land.T)
    dql_t = (jnp.where(block, m2r(nt, k, dx3_s), 0.0) + m3(nt, kt_s, dx2_s)) * inv_l
    dkl_t = (jnp.where(block, m2r(nt, q, dx1_s), 0.0) + m3(nn, qt_s, dx2_s)) * inv_l
    dq = m3(nn, kt_s, dx1_s) + m2l(nn, split(dql_t), member)
    dk = m3(nn, qt_s, dx3_s) + m2l(nn, split(dkl_t), member)
    corr = []
    vm = jnp.where(live, v, jnp.zeros_like(v))
    ri = lax.broadcasted_iota(jnp.int32, (128, 128), 0)
    ci = lax.broadcasted_iota(jnp.int32, (128, 128), 1)
    flip = jnp.where(ri + ci == 127, 1.0, 0.0).astype(BF)
    for h in range(heads):
        rows = g[HD * h : HD * (h + 1)]
        stack = jnp.concatenate([rows[:, 128 * b : 128 * b + 128] for b in range(slots // 128)], axis=0)
        near = tn(nn(stack, flip).astype(BF), windows(vm, h))
        near = pltpu.roll(near, 0, axis=1, stride=1, stride_axis=0)
        corr.append(jnp.sum(near, axis=0, keepdims=True))
    return dq, dk, dv, corr


N_MATS = 7
VEC_TAPS = 9
N_KEPT = 4 * NEWTON - 1
VM = pl.BlockSpec(memory_space=pltpu.VMEM)
SM = pl.BlockSpec(memory_space=pltpu.SMEM)
HB = pl.BlockSpec(memory_space=pltpu.HBM)


def struct(shape, kind):
    return jax.ShapeDtypeStruct(shape, kind)


def cost(micros):
    return pl.CostEstimate(flops=int(micros * 1.0e9), bytes_accessed=1 << 20, transcendentals=0)


def start(pairs, sems, first=0):
    copies = [pltpu.make_async_copy(src, dst, sems.at[first + i]) for i, (src, dst) in enumerate(pairs)]
    for copy in copies:
        copy.start()
    return copies


def finish(copies):
    for copy in copies:
        copy.wait()


def forward_kernel(info, x0, x1, x2, x3, wt, tap, att0, att1, att2, att3, proj_h, first_h, last_h, mats_h, kept_h,
                   att_s, proj, first_s, last_s, mats, kept_s, sems):
    nar, length = info[0], info[1]
    rows = x0.shape[0]
    offs = [pl.multiple_of((nar ^ r) * rows, rows) for r in range(4)]
    for r, x in enumerate((x0, x1, x2, x3)):
        proj[:, pl.ds(offs[r], rows)] = nt(wt[...], x[...]).astype(BF)
    copies = start([(proj, proj_h)], sems)
    n = wt.shape[0] // 3
    q, k, v = proj[0:n, :], proj[n:2 * n, :], proj[2 * n:3 * n, :]
    att, first, last, mid, z, sum_t, y_t, root, kept, k_land, q_land = core_forward(q, k, v, length, bands(tap))
    first_s[...] = first
    last_s[...] = last
    copies += start([(first_s, first_h), (last_s, last_h)], sems, 1)
    i = 0
    for entry in kept:
        for m in entry:
            if m is not None:
                kept_s[i] = m
                i += 1
    copies += start([(kept_s, kept_h)], sems, 3)
    for i, m in enumerate((mid, z, sum_t, y_t, root, k_land, q_land)):
        mats[i] = m
    copies += start([(mats, mats_h)], sems, 4)
    att_s[...] = att
    for r, out in enumerate((att0, att1, att2, att3)):
        out[...] = att_s[:, pl.ds(offs[r], rows)]
    finish(copies)


def forward_call(info, xs, wt, tap):
    rows, width = xs[0].shape
    n = wt.shape[0] // 3
    slots = 4 * rows
    saved = [((3 * n, slots), BF), ((n, slots), F32), ((n, slots), F32), ((N_MATS, n, n), F32), ((N_KEPT, n, n), F32)]
    return pl.pallas_call(
        forward_kernel,
        in_specs=[SM] + [VM] * 6,
        out_specs=[VM] * 4 + [HB] * 5,
        out_shape=[struct((n, rows), BF)] * 4 + [struct(*s) for s in saved],
        scratch_shapes=[pltpu.VMEM((n, slots), BF)]
        + [pltpu.VMEM(*s) for s in saved]
        + [pltpu.SemaphoreType.DMA((5,))],
        compiler_params=pltpu.CompilerParams(vmem_limit_bytes=60 << 20),
        cost_estimate=cost(10),
        name="core_forward",
    )(info, *xs, wt, tap)


def backward_kernel(slotted, info, g0, g1, g2, g3, proj_h, first_h, last_h, mats_h, kept_h, x0, x1, x2, x3, wt, rev,
                    dx0, dx13, dx2, in_grad, vec_o, g_s, dp_s, tot_s, vec_s, proj, first_s, last_s, mats, kept_s, sems):
    nar, length = info[0], info[1]
    copies = start([(mats_h, mats), (first_h, first_s), (proj_h, proj), (last_h, last_s), (kept_h, kept_s)], sems)
    rows = x0.shape[0]
    offs = [pl.multiple_of((nar ^ r) * rows, rows) for r in range(4)]
    for r, g in enumerate((g0, g1, g2, g3)):
        g_s[:, pl.ds(offs[r], rows)] = g[0 : g_s.shape[0], :]
    tail = sum(g[g_s.shape[0] :, :].astype(F32) for g in (g0, g1, g2, g3))
    band = bands(rev[...])
    n = wt.shape[0] // 3
    finish(copies)
    q, k, v = proj[0:n, :], proj[n:2 * n, :], proj[2 * n:3 * n, :]
    mid, z, sum_t, y_t, root, k_land, q_land = [mats[i] for i in range(N_MATS)]
    kept, i = [], 0
    for step in range(NEWTON):
        size = 4 if step else 3
        kept.append(tuple(kept_s[i + j] for j in range(size)) + (() if step else (None,)))
        i += size
    dq, dk, dv, corr = core_backward(g_s[...], q, k, v, length, first_s[...], last_s[...], mid, z, sum_t, y_t, root,
                                     kept, k_land, q_land, band)
    dp_s[0:n, :] = dq.astype(BF)
    dp_s[n:2 * n, :] = dk.astype(BF)
    dp_s[2 * n:3 * n, :] = dv.astype(BF)
    total = None
    for r, x in enumerate((x0, x1, x2, x3)):
        block = dp_s[:, pl.ds(offs[r], rows)]
        back = tn(block, wt[...]).astype(BF)
        if r & 1:
            dx13[r >> 1] = back
        else:
            (dx2 if r else dx0)[...] = back
        term = nn(block, x[...])
        total = term if total is None else total + term
    per = x0.shape[1] // rows
    vec_s[...] = jnp.zeros_like(vec_s)
    lines = [jnp.concatenate([tail[per * i + j : per * i + j + 1, :] for j in range(per)], axis=1) for i in range(VEC_TAPS)]
    lines += corr
    if not slotted:
        in_grad[...] = total.astype(BF)
        for i, line in enumerate(lines):
            vec_o[i : i + 1, 0 : line.shape[1]] = line
        return
    tot_s[...] = total
    for i, line in enumerate(lines):
        vec_s[i >> 1, (i & 1) : (i & 1) + 1, 0 : line.shape[1]] = line
    wides = in_grad.shape[0]
    part = total.shape[0] // wides
    for s in range(wides):
        w = s ^ info[2]
        in_grad[s, 0:part, :] = tot_s[pl.ds(pl.multiple_of(w * part, 8), part), :].astype(BF)
        in_grad[s, part : part + 8, :] = vec_s[w].astype(BF)


def backward_call(info, gs, saved, xs, wt, rev, n_wide, slotted):
    rows, width = xs[0].shape
    n = wt.shape[0] // 3
    slots = 4 * rows
    return pl.pallas_call(
        functools.partial(backward_kernel, slotted),
        in_specs=[SM] + [VM] * 4 + [HB] * 5 + [VM] * 6,
        out_specs=[VM] * 5,
        out_shape=[
            struct((rows, width), BF),
            struct((2, rows, width), BF),
            struct((rows, width), BF),
            struct((n_wide, 3 * n // n_wide + 8, width) if slotted else (3 * n, width), BF),
            struct((16, width), F32),
        ],
        scratch_shapes=[pltpu.VMEM((n, slots), BF), pltpu.VMEM((3 * n, slots), BF)]
        + [pltpu.VMEM((3 * n, width), F32), pltpu.VMEM((8, 8, width), F32)]
        + [pltpu.VMEM(s.shape, s.dtype) for s in saved]
        + [pltpu.SemaphoreType.DMA((5,))],
        compiler_params=pltpu.CompilerParams(vmem_limit_bytes=60 << 20),
        cost_estimate=cost(19),
        name="core_backward",
    )(info, *gs, *saved, *xs, wt, rev)


EPS = 1e-05


def norm_stats(resid):
    center = jnp.mean(resid, axis=1, keepdims=True)
    centered = resid - center
    inverse = lax.rsqrt(jnp.mean(centered * centered, axis=1, keepdims=True) + EPS)
    return centered * inverse, inverse


def norm_pull(grad, normalized, inverse, gain):
    scaled = grad * gain
    return inverse * (
        scaled
        - jnp.mean(scaled, axis=1, keepdims=True)
        - normalized * jnp.mean(scaled * normalized, axis=1, keepdims=True)
    )


def total(rows):
    return jnp.sum(rows, axis=0, keepdims=True)


def ffn_kernel(slotted, info, x, a0, a1, a2, a3, w0, w1, w2, w3, g1, b1, ub, db, g2, b2, cot, up_h, down_h,
               mixed, res1, d0, d1, d2, d3, *rest):
    outs, (up, down, hid_s, slope, pre_s, hold_d, hold_u, hold_p, sems) = rest[:-9], rest[-9:]
    chunks = 4
    ff = up.shape[1]
    size = ff // chunks
    cuts = [pl.ds(c * size, size) for c in range(chunks)]
    copies = start(
        [pair for cut in cuts for pair in ((up_h.at[:, cut], up.at[:, cut]), (down_h.at[cut, :], down.at[cut, :]))], sems
    )
    leaving = []
    used = 2 * chunks
    nar, wide = info[0], info[2]
    if slotted:
        down_same, down_other, up_same, up_other = outs
        n_wide, rows = down_same.shape[1], down_same.shape[2]
    else:
        down_all, up_all, part_all = outs

    def outer(left, right, hold, c, same, other):
        nonlocal leaving, used
        group = 4 * rows if slotted else size
        for i in range(size // group):
            w = c * (size // group) + i
            hold[w * group : (w + 1) * group, :] = tn(left[:, w * group : (w + 1) * group], right).astype(BF)
            for n in range(4 if slotted else 0):
                block = hold.at[pl.ds(w * group + n * rows, rows), :]
                slot_n, slot_w = n ^ nar, w ^ wide
                for core, target in ((0, same), (1, other)):

                    @pl.when((slot_n & 1) == core)
                    def _():
                        pltpu.make_async_copy(
                            block, target.at[slot_n >> 1, slot_w, pl.ds(0, rows)], sems.at[used]
                        ).start()

                leaving.append(pltpu.make_async_copy(block, same.at[0, 0, pl.ds(0, rows)], sems.at[used]))
                used += 1
            if not slotted:
                leaving += start([(hold.at[pl.ds(w * group, group), :], same.at[pl.ds(w * group, group), :])], sems, used)
                used += 1

    attention = tn(a0[...], w0[...]) + tn(a1[...], w1[...]) + tn(a2[...], w2[...]) + tn(a3[...], w3[...])
    n1, inv1 = norm_stats(x[...].astype(F32) + attention)
    normed = n1 * g1[...] + b1[...]
    ffn_in = normed.astype(BF)
    out = None
    for c, cut in enumerate(cuts):
        copies[2 * c].wait()
        pre = nn(ffn_in, up[:, cut]) + ub[:, cut]
        below = 0.5 * (1.0 + lax.erf(pre * 0.7071067811865476))
        hid = (pre * below).astype(BF)
        slope[:, cut] = below + pre * (0.3989422804014327 * jnp.exp(-0.5 * (pre * pre)))
        hid_s[:, cut] = hid
        copies[2 * c + 1].wait()
        term = nn(hid, down[cut, :])
        out = term if out is None else out + term
    n2, inv2 = norm_stats(normed + (out + db[...]))
    mixed[...] = (n2 * g2[...] + b2[...]).astype(BF)
    cotangent = cot[...].astype(F32)
    res2 = norm_pull(cotangent, n2, inv2, g2[...])
    low = res2.astype(BF)
    for c in range(chunks):
        outer(hid_s, low, hold_d, c, *((down_same, down_other) if slotted else (down_all, None)))
    grad = res2
    bias = []
    for c, cut in enumerate(cuts):
        pre = nt(low, down[cut, :]) * slope[:, cut]
        bias.append(total(pre))
        pre = pre.astype(BF)
        pre_s[:, cut] = pre
        grad = grad + nt(pre, up[:, cut])
        outer(pre_s, ffn_in, hold_u, c, *((up_same, up_other) if slotted else (up_all, None)))
    back = norm_pull(grad, n1, inv1, g1[...])
    res1[...] = back
    attn = back.astype(BF)
    vectors = [total(grad * n1), total(grad), total(res2), total(cotangent * n2), total(cotangent)]
    vectors += bias
    per = vectors[0].shape[1] // x.shape[0]
    lanes = x.shape[0]
    tail = [v[:, lanes * j : lanes * (j + 1)] for v in vectors for j in range(per)]
    tail = jnp.concatenate(tail + [jnp.zeros((32 - len(tail), lanes), F32)], axis=0).astype(BF)
    local = w0.shape[0]
    for w, d in ((w0, d0), (w1, d1), (w2, d2), (w3, d3)):
        d[0:local, :] = nt(w[...], attn).astype(BF)
        d[local : local + 32, :] = tail
    for r, a in enumerate((a0, a1, a2, a3)):
        hold_p[r] = nn(a[...], attn).astype(BF)
        if slotted:
            more = local // n_wide
            target = (up_other if r & 1 else up_same).at[r >> 1]
            for i in range(n_wide):
                block = hold_p.at[r, pl.ds(pl.multiple_of((i ^ wide) * more, 8), more), :]
                leaving += start([(block, target.at[i, pl.ds(rows, more)])], sems, used)
                used += 1
        else:
            leaving += start([(hold_p.at[r], part_all.at[r])], sems, used)
            used += 1
    finish(leaving)


def ffn_call(info, x, att, wo, g1, b1, ub, db, g2, b2, cot, up, down, n_wide, slotted):
    rows, width = x.shape
    ff = up.shape[1]
    local = wo[0].shape[0]
    part = ff // (4 * n_wide)
    if slotted:
        sums = [struct((2, n_wide, part, width), BF)] * 2 + [struct((2, n_wide, part + local // n_wide, width), BF)] * 2
    else:
        sums = [struct((ff, width), BF)] * 2 + [struct((4, local, width), BF)]
    return pl.pallas_call(
        functools.partial(ffn_kernel, slotted),
        in_specs=[SM] + [VM] * 16 + [HB] * 2,
        out_specs=[VM] * 6 + [HB] * len(sums),
        out_shape=[struct((rows, width), BF), struct((rows, width), F32)] + [struct((local + 32, rows), BF)] * 4 + sums,
        scratch_shapes=[
            pltpu.VMEM((width, ff), BF),
            pltpu.VMEM((ff, width), BF),
            pltpu.VMEM((rows, ff), BF),
            pltpu.VMEM((rows, ff), F32),
            pltpu.VMEM((rows, ff), BF),
            pltpu.VMEM((ff, width), BF),
            pltpu.VMEM((ff, width), BF),
            pltpu.VMEM((4, local, width), BF),
            pltpu.SemaphoreType.DMA((8 + 12 * max(n_wide, 8),)),
        ],
        compiler_params=pltpu.CompilerParams(vmem_limit_bytes=60 << 20),
        cost_estimate=cost(20),
        name="ffn",
    )(info, x, *att, *wo, g1, b1, ub, db, g2, b2, cot, up, down)


def to_slots(me, whole, n_wide):
    count = 4 * n_wide
    slot = jnp.arange(count).reshape(n_wide, 2, 2).transpose(2, 1, 0)
    picked = whole.reshape(count, -1, whole.shape[-1])[slot ^ me]
    return picked[0], picked[1]


def part_slots(me, parts, n_wide):
    near = jnp.arange(4).reshape(2, 2).T
    parts = parts.reshape(4, n_wide, -1, parts.shape[-1])
    picked = parts[near[:, :, None], (jnp.arange(n_wide) ^ (me // 4))[None, None, :]]
    return picked[0], picked[1]


def finish_kernel(info, pool, input_o, vec_o, rows_s, vec_s):
    wides, rows = pool.shape[0], pool.shape[1]
    part = rows_s.shape[0] // wides
    for s in range(wides):
        w = s ^ info[2]
        rows_s[pl.ds(pl.multiple_of(w * part, 8), part), :] = pool[s, 0:part, :].astype(F32)
        vec_s[w] = pool[s, part : part + 8, :].astype(F32)
    local = rows_s.shape[0] // 3
    for c in range(3):
        input_o[c] = rows_s[local * c : local * (c + 1), :].T
    vec_o[...] = vec_s[...]


def finish_call(info, pool, local):
    wides, rows, width = pool.shape
    return pl.pallas_call(
        finish_kernel,
        in_specs=[SM, VM],
        out_specs=[VM, VM],
        out_shape=[struct((3, width, local), F32), struct((wides, 8, width), F32)],
        scratch_shapes=[pltpu.VMEM((3 * local, width), F32), pltpu.VMEM((wides, 8, width), F32)],
        compiler_params=pltpu.CompilerParams(vmem_limit_bytes=24 << 20),
        cost_estimate=cost(3),
        name="finish",
    )(info, pool)


def build(mesh):
    n_wide, n_narrow = mesh.shape["wide"], mesh.shape["narrow"]
    count = n_wide * n_narrow
    wide_bits = []
    bit = n_narrow
    while bit < count:
        wide_bits.append(bit)
        bit *= 2

    def swap(block, mask):
        return lax.ppermute(block, AXES, [(i, i ^ mask) for i in range(count)])

    def after(value, *earlier):
        return lax.optimization_barrier((value, earlier))[0]

    def gather_relative(block):
        far = swap(block, 2)
        near = swap(block, 1)
        return [block, near, far, swap(far, 1)]

    def exchange_relative(blocks):
        return [blocks[r] if r == 0 else swap(blocks[r], r) for r in range(n_narrow)]

    def reduce_relative(own, pair, far):
        came = swap(pair, 1)
        far = (far.astype(F32) + came[1].astype(F32)).astype(BF)
        return own.astype(F32) + came[0].astype(F32) + swap(far, 2).astype(F32)

    class Halving:
        def __init__(self, left, right, masks):
            shape = [2] * len(masks) + list(left.shape[-2:])
            self.masks, self.left, self.right = list(masks), left.reshape(shape), right.reshape(shape)

        def side(self, axis, i):
            return sum(
                lax.index_in_dim(part, i, axis, keepdims=False).astype(F32) for part in (self.left, self.right)
            )

        def split(self, mask):
            self.axis, self.mask = self.masks.index(mask), mask
            self.masks.pop(self.axis)
            self.sent = self.side(self.axis, 1).astype(BF)
            self.kept = self.side(self.axis, 0).astype(BF)

        def send(self):
            self.left, self.right = self.kept, swap(self.sent, self.mask)

        def step(self, mask):
            self.split(mask)
            self.send()

        def total(self):
            return self.left.astype(F32) + self.right.astype(F32)

    def on_device(
        tokens,
        lengths,
        input_weights,
        output_weight,
        conv_taps,
        first_gain,
        first_bias,
        up_weight,
        up_bias,
        down_weight,
        down_bias,
        second_gain,
        second_bias,
        cotangent,
    ):
        me = lax.axis_index(AXES)
        nar = lax.axis_index("narrow")
        rows, width = tokens.shape
        local_width = input_weights.shape[2]
        heads = local_width // HD
        wide = lax.axis_index("wide")
        info = jnp.stack([nar.astype(jnp.int32), lengths[0], wide.astype(jnp.int32)])
        weights_t = jnp.swapaxes(input_weights, 1, 2).reshape(3 * local_width, width)
        conv_base = jnp.pad(conv_taps, ((0, 0), (112, 384 - 112 - KW)))
        conv_rev = jnp.pad(conv_taps[:, ::-1], ((0, 0), (112, 384 - 112 - KW)))
        token_blocks = gather_relative(tokens)
        weight = after(output_weight, token_blocks[2])
        far, near = swap(weight, 2), swap(weight, 1)
        *att, s0, s1, s2, s3, s4 = forward_call(info, token_blocks, weights_t, conv_base)
        own_att = exchange_relative(att)
        out_rel = [output_weight, near, far, swap(after(far, att[0]), 1)]
        ff_rows = up_weight.shape[1] // count
        slotted = ff_rows % 32 == 0 and n_wide == 8

        def row(vector):
            return vector[None, :]

        mixed, res1, *rest = ffn_call(
            info, tokens, own_att, out_rel, row(first_gain), row(first_bias), row(up_bias), row(down_bias),
            row(second_gain), row(second_bias), cotangent, up_weight, down_weight, n_wide, slotted,
        )
        att_grad = exchange_relative(rest[:4])
        if slotted:
            down_same, down_other, up_same, up_other = rest[4:]
        else:
            down_same, down_other = to_slots(me, rest[4], n_wide)
            up_same, up_other = [
                jnp.concatenate(pair, axis=2)
                for pair in zip(to_slots(me, rest[5], n_wide), part_slots(me, rest[6], n_wide))
            ]
        masks = [2] + wide_bits[::-1]
        down = Halving(down_same, swap(down_other, 1), masks)
        up = Halving(up_same, swap(up_other, 1), masks)
        down.split(wide_bits[0])
        up.split(2)
        att_grad = list(after(tuple(att_grad), down.sent, up.sent))
        down.send()
        up.send()
        back0, back13, back2, pool, vec = backward_call(
            info, att_grad, [s0, s1, s2, s3, s4], token_blocks, weights_t, conv_rev, n_wide, slotted
        )
        per_wide = -(-(VEC_TAPS + heads) // n_wide)
        if not slotted:
            vec = vec[: VEC_TAPS + heads]
            vec = jnp.pad(vec, ((0, per_wide * n_wide - vec.shape[0]), (0, 0)))
            pool = jnp.concatenate(
                [pool.reshape(n_wide, -1, width), vec.reshape(n_wide, per_wide, width).astype(BF)], axis=1
            )[jnp.arange(n_wide) ^ wide]
        pool = after(pool, down.right)
        pool = Halving(pool, jnp.zeros_like(pool), wide_bits[::-1])
        for mask in wide_bits:
            pool.step(mask)
        tokens_grad = (res1 + reduce_relative(back0, back13, back2)).astype(BF)
        down.step(2)
        up.step(wide_bits[0])
        for mask in wide_bits[1:]:
            down.step(mask)
            up.step(mask)
        down_out = down.total()
        up_sum = up.total()
        up_out = up_sum[:ff_rows].T
        pool = jnp.concatenate([pool.total(), up_sum[ff_rows:]], axis=0).astype(BF)[None]
        for mask in wide_bits:
            pool = jnp.concatenate([pool, swap(pool, mask)], axis=0)
        part = 3 * local_width // n_wide
        order = jnp.arange(n_wide) ^ wide
        if slotted:
            input_out, vec = finish_call(info, pool, local_width)
            vec = vec[:, :per_wide].reshape(-1, width)
        else:
            whole = pool[order].astype(F32)
            input_out = whole[:, :part].reshape(3, local_width, width).transpose(0, 2, 1)
            vec = whole[:, part : part + per_wide].reshape(-1, width)
        output_out = pool[:, pool.shape[1] - local_width // n_wide :][order].astype(F32).reshape(local_width, width)
        taps_out = vec[VEC_TAPS : VEC_TAPS + heads, 239 : 239 + KW]
        up_bias_out = lax.dynamic_slice_in_dim(vec[5:VEC_TAPS].reshape(-1), me * ff_rows, ff_rows)
        return (
            mixed,
            tokens_grad,
            input_out,
            output_out,
            taps_out,
            vec[0],
            vec[1],
            up_out,
            up_bias_out,
            down_out,
            vec[2],
            vec[3],
            vec[4],
        )

    return on_device


def solution(mesh):
    spread = P(AXES, None)
    placed = (
        spread,
        P("wide"),
        P(None, None, "narrow"),
        P("narrow", None),
        P("narrow", None),
        P(),
        P(),
        P(),
        P(),
        P(),
        P(),
        P(),
        P(),
        spread,
    )
    results = (
        spread,
        spread,
        P(None, None, "narrow"),
        P("narrow", None),
        P("narrow", None),
        P(),
        P(),
        P(None, AXES),
        P(AXES),
        spread,
        P(),
        P(),
        P(),
    )
    return jax.shard_map(
        build(mesh), mesh=mesh, in_specs=placed, out_specs=results, check_vma=False
    )
```

```python
import functools
import jax
import jax.numpy as jnp
from jax import lax
from jax.experimental import pallas as pl
from jax.experimental.pallas import tpu as pltpu
from jax.sharding import PartitionSpec as P

BF = jnp.bfloat16
F32 = jnp.float32
HD = 64
LM = 64
KW = 33
NEWTON = 6
AXES = ("wide", "narrow")


def dot(a, b, ca, cb):
    return lax.dot_general(a, b, (((ca,), (cb,)), ((), ())), preferred_element_type=F32)

def nn(a, b): return dot(a, b, 1, 0)
def nt(a, b): return dot(a, b, 1, 1)
def tn(a, b): return dot(a, b, 0, 0)

def split(a):
    hi = a.astype(BF)
    return hi, (a - hi.astype(F32)).astype(BF)

def split3(a):
    hi = a.astype(BF)
    rest = a - hi.astype(F32)
    mid = rest.astype(BF)
    return hi, mid, (rest - mid.astype(F32)).astype(BF)

def m3(op, a, b):
    return op(a[0], b[0]) + (op(a[1], b[0]) + op(a[0], b[1]))

def m6(op, a, b):
    return op(a[0], b[0]) + ((op(a[1], b[0]) + op(a[0], b[1])) + (op(a[1], b[1]) + (op(a[2], b[0]) + op(a[0], b[2]))))

def m2l(op, a, b):
    return op(a[0], b) + op(a[1], b)

def m2r(op, a, b):
    return op(a, b[0]) + op(a, b[1])


def frame(length, slots, heads):
    n = heads * LM
    row = lax.broadcasted_iota(jnp.int32, (n, n), 0)
    col = lax.broadcasted_iota(jnp.int32, (n, n), 1)
    block = (row >> 6) == (col >> 6)
    place = lax.broadcasted_iota(jnp.int32, (1, slots), 1)
    live = place < length
    mark = lax.broadcasted_iota(jnp.int32, (n, 1), 0) & (LM - 1)
    begin = (mark * length) >> 6
    end = ((mark + 1) * length) >> 6
    member = jnp.where((place >= begin) & (place < end), 1.0, 0.0).astype(BF)
    mark_l = lax.broadcasted_iota(jnp.int32, (1, n), 1) & (LM - 1)
    count_l = ((((mark_l + 1) * length) >> 6) - ((mark_l * length) >> 6)).astype(F32)
    count_s = (end - begin).astype(F32)
    return block, live, member, 1.0 / count_s, 1.0 / count_l


def head_lane_max(row, heads):
    lane = lax.broadcasted_iota(jnp.int32, row.shape, 1) >> 6
    out = jnp.zeros_like(row)
    for h in range(heads):
        top = jnp.max(jnp.where(lane == h, row, -1.0), axis=1, keepdims=True)
        out = jnp.where(lane == h, top, out)
    return out


def head_lane_sum(row, heads):
    lane = lax.broadcasted_iota(jnp.int32, row.shape, 1) >> 6
    out = jnp.zeros_like(row)
    for h in range(heads):
        total = jnp.sum(jnp.where(lane == h, row, 0.0), axis=1, keepdims=True)
        out = jnp.where(lane == h, total, out)
    return out


def windows(arr, h):
    slots = arr.shape[1]
    rows = arr[HD * h : HD * (h + 1)]
    zero = jnp.zeros((HD, 128), arr.dtype)
    wide = jnp.concatenate([zero, rows, zero], axis=1)
    return jnp.concatenate([wide[:, 128 * b : 128 * b + 384] for b in range(slots // 128)], axis=0)


def bands(taps, heads, turned):
    lane = lax.broadcasted_iota(jnp.int32, (1, 384), 1) - 112
    out = []
    for h in range(heads):
        base = jnp.zeros((1, 384), F32)
        for w in range(KW):
            base = jnp.where(lane == (KW - 1 - w if turned else w), taps[h, w], base)
        out.append(split(pltpu.roll(jnp.broadcast_to(base, (128, 384)), 0, axis=1, stride=1, stride_axis=0)))
    return out


def squeeze(matrix):
    return sum(matrix[HD * h : HD * (h + 1)] for h in range(matrix.shape[0] // HD))


def spread(packed, block):
    return jnp.where(block, jnp.concatenate([packed] * (block.shape[0] // HD), axis=0), 0.0)


def conv_apply(arr, band, heads):
    slots = arr.shape[1]
    parts = []
    for h in range(heads):
        out = m2r(nt, windows(arr, h), band[h])
        parts.append(jnp.concatenate([out[HD * b : HD * (b + 1)] for b in range(slots // 128)], axis=1))
    return jnp.concatenate(parts, axis=0)


def core_forward(q, k, v, length, band, keep):
    n, slots = q.shape
    heads = n // HD
    block, live, member, inv_s, inv_l = frame(length, slots, heads)
    k_land = jnp.where(block, nt(member, k), 0.0) * inv_s
    q_land = jnp.where(block, nt(member, q), 0.0) * inv_s
    k3, q3 = split3(k_land), split3(q_land)
    x2 = m6(nt, q3, k3) * 0.125
    x2 = jnp.where(block, x2, -1e30)
    e2 = jnp.exp(x2 - jnp.max(x2, axis=1, keepdims=True))
    mid = e2 * (1.0 / jnp.sum(e2, axis=1, keepdims=True))
    cols = jnp.sum(mid, axis=0, keepdims=True)
    inv_max = 1.0 / head_lane_max(cols, heads)
    x3 = m2l(nn, q3[:2], k) * 0.125 + jnp.where(live, 0.0, -1e9)
    e3 = jnp.exp(x3 - jnp.max(x3, axis=1, keepdims=True))
    last = e3 * (1.0 / jnp.sum(e3, axis=1, keepdims=True))
    last_s = split(last)
    keep("last", last)
    x1 = (m2l(nn, k3[:2], q) * 0.125).reshape(heads, LM, slots)
    e1 = jnp.exp(x1 - jnp.max(x1, axis=1, keepdims=True))
    first = (e1 * (1.0 / jnp.sum(e1, axis=1, keepdims=True))).reshape(n, slots)
    first_s = split(first)
    keep("first", first)
    eye = jnp.where(lax.broadcasted_iota(jnp.int32, (n, n), 0) == lax.broadcasted_iota(jnp.int32, (n, n), 1), 1.0, 0.0)
    mid_s = split(mid)
    p = m3(nt, mid_s, mid_s) * inv_max

    def powers(p):
        ps = split(p)
        p2 = m3(nn, ps, ps)
        p2s = split(p2)
        p3 = m3(nn, p2s, ps)
        return p2, p2s, p3, 0.25 * (13.0 * eye - 15.0 * p + 7.0 * p2 - p3)

    def onward(p, p2, p2s, p3):
        return 0.25 * (13.0 * p - 15.0 * p2 + 7.0 * p3 - m3(nn, p2s, p2s))

    p2, p2s, p3, root = powers(p)
    keep(0, (p, p2, p3))
    p = onward(p, p2, p2s, p3)

    def sweep(step, carry):
        p, root = carry
        p2, p2s, p3, poly = powers(p)
        keep(step, (p, p2, p3, root))
        return onward(p, p2, p2s, p3), m3(nn, split(root), split(poly))

    p, root = lax.fori_loop(1, NEWTON - 1, sweep, (p, root))
    p2, p2s, p3, poly = powers(p)
    keep(NEWTON - 1, (p, p2, p3, root))
    root = m3(nn, split(root), split(poly))
    root_s = split(root)
    mid_t = split(mid.T)
    z = m3(nn, mid_t, root_s) * inv_max
    z_s = split(z)
    sum_t = jnp.where(block, m2r(nt, v, last_s), 0.0)
    y_t = m3(nt, split(sum_t), z_s)
    out = m3(nn, split(y_t), first_s)
    out = out + conv_apply(jnp.where(live, v, jnp.zeros_like(v)), band, heads)
    att = jnp.where(live, out, 0.0).astype(BF)
    return att, first, last, mid, z, sum_t, y_t, root, k_land, q_land


def core_backward(g, q, k, v, parts, first, last, mid, z, sum_t, y_t, root, kept, k_land, q_land, band, before_newton):
    n, slots = q.shape
    heads = n // HD
    block, live, member, inv_s, inv_l = parts
    g = jnp.where(live, g, jnp.zeros_like(g))
    first_s, last_s = split(first), split(last)
    mid_s = split(mid)
    cols = jnp.sum(mid, axis=0, keepdims=True)
    top = head_lane_max(cols, heads)
    inv_max = 1.0 / top
    z_s = split(z)
    y = y_t.T
    dfirst = m2l(nn, split(y), g)
    dy_t = jnp.where(block, m2r(nt, g, first_s), 0.0)
    dy = dy_t.T
    dy_s, dyt_s, st_s = split(dy), split(dy_t), split(sum_t)
    s_s = split(sum_t.T)
    dz = m3(nn, dy_s, st_s)
    dz_t = m3(nn, s_s, dyt_s)
    ds_t = m3(nn, dyt_s, z_s)
    ds = ds_t.T
    dlast = m2l(nn, split(ds), v)
    dv = m3(nn, split(ds_t), last_s)
    dv = dv + jnp.where(live, conv_apply(g, band, heads), 0.0)
    dx3 = last * (dlast - jnp.sum(dlast * last, axis=1, keepdims=True)) * 0.125
    f3 = first.reshape(heads, LM, slots)
    d3 = dfirst.reshape(heads, LM, slots)
    dx1 = (f3 * (d3 - jnp.sum(d3 * f3, axis=1, keepdims=True)) * 0.125).reshape(n, slots)
    before_newton()
    root_s = split(root)
    dz_s, dzt_s = split(dz), split(dz_t)
    dmid = m3(nn, root_s, dzt_s) * inv_max
    droot = m3(nn, mid_s, dz_s) * inv_max
    dtop = -jnp.sum(dz * z, axis=0, keepdims=True)
    eye = jnp.where(lax.broadcasted_iota(jnp.int32, (n, n), 0) == lax.broadcasted_iota(jnp.int32, (n, n), 1), 1.0, 0.0)

    def unsweep(step, dp, droot):
        p, p2, p3, before = kept(step)
        ps, p2s = split(p), split(p2)
        if before is None:
            dpoly = 0.25 * droot
        else:
            poly = 0.25 * (13.0 * eye - 15.0 * p + 7.0 * p2 - p3)
            droot_s = split(droot)
            dpoly = 0.25 * m3(nn, split(before), droot_s)
            droot = m3(nn, droot_s, split(poly))
        d1, d2, d3 = -15.0 * dpoly, 7.0 * dpoly, -dpoly
        if dp is not None:
            e = 0.25 * dp
            es = split(e)
            d1 = d1 + 13.0 * e
            d2 = d2 - 15.0 * e - (m3(nn, es, p2s) + m3(nn, p2s, es))
            d3 = d3 + 7.0 * e
        d3s = split(d3)
        d2 = d2 + m3(nn, d3s, ps)
        d1 = d1 + m3(nn, p2s, d3s)
        d2s = split(d2)
        return d1 + (m3(nn, d2s, ps) + m3(nn, ps, d2s)), droot

    dp, droot = unsweep(NEWTON - 1, None, droot)
    dp, droot = lax.fori_loop(1, NEWTON - 1, lambda i, c: unsweep(NEWTON - 1 - i, *c), (dp, droot))
    dp, droot = unsweep(0, dp, droot)
    dmid = dmid + m3(nn, split(dp + dp.T), mid_s) * inv_max
    dtop = dtop - jnp.sum(dp * kept(0)[0], axis=0, keepdims=True)
    dtop = head_lane_sum(dtop, heads) * inv_max
    hit = jnp.where(cols == top, 1.0, 0.0)
    dmid = dmid + jnp.where(block, dtop * hit / head_lane_sum(hit, heads), 0.0)
    dx2 = mid * (dmid - jnp.sum(dmid * mid, axis=1, keepdims=True)) * 0.125
    dx2_s = split(dx2)
    dx1_s, dx3_s = split(dx1), split(dx3)
    kt_s, qt_s = split(k_land.T), split(q_land.T)
    dql_t = (jnp.where(block, m2r(nt, k, dx3_s), 0.0) + m3(nt, kt_s, dx2_s)) * inv_l
    dkl_t = (jnp.where(block, m2r(nt, q, dx1_s), 0.0) + m3(nn, qt_s, dx2_s)) * inv_l
    dq = m3(nn, kt_s, dx1_s) + m2l(nn, split(dql_t), member)
    dk = m3(nn, qt_s, dx3_s) + m2l(nn, split(dkl_t), member)
    corr = []
    vm = jnp.where(live, v, jnp.zeros_like(v))
    ri = lax.broadcasted_iota(jnp.int32, (128, 128), 0)
    ci = lax.broadcasted_iota(jnp.int32, (128, 128), 1)
    flip = jnp.where(ri + ci == 127, 1.0, 0.0).astype(BF)
    for h in range(heads):
        rows = g[HD * h : HD * (h + 1)]
        stack = jnp.concatenate([rows[:, 128 * b : 128 * b + 128] for b in range(slots // 128)], axis=0)
        near = tn(nn(stack, flip).astype(BF), windows(vm, h))
        near = pltpu.roll(near, 0, axis=1, stride=1, stride_axis=0)
        corr.append(jnp.sum(near, axis=0, keepdims=True))
    return dq, dk, dv, corr


N_MATS = 7
VEC_TAPS = 9
N_KEPT = 4 * NEWTON
VM = pl.BlockSpec(memory_space=pltpu.VMEM)
SM = pl.BlockSpec(memory_space=pltpu.SMEM)
HB = pl.BlockSpec(memory_space=pltpu.HBM)


def struct(shape, kind):
    return jax.ShapeDtypeStruct(shape, kind)


def cost(micros):
    return pl.CostEstimate(flops=int(micros * 1.0e9), bytes_accessed=1 << 20, transcendentals=0)


def start(pairs, sems, first=0):
    copies = [pltpu.make_async_copy(src, dst, sems.at[first + i]) for i, (src, dst) in enumerate(pairs)]
    for copy in copies:
        copy.start()
    return copies


def finish(copies):
    for copy in copies:
        copy.wait()


def forward_kernel(lengths, taps, x0, x1, x2, x3, wt, att0, att1, att2, att3, proj_h, first_h, last_h, mats_h, kept_h, att_h,
                   att_s, proj, first_s, last_s, mats, kept_s, sems):
    nar, length = lax.axis_index("narrow"), lengths[0]
    rows = x0.shape[0]
    offs = [pl.multiple_of((nar ^ r) * rows, rows) for r in range(4)]
    for r, x in enumerate((x0, x1, x2, x3)):
        proj[:, pl.ds(offs[r], rows)] = nt(wt[...], x[...]).astype(BF)
    copies = start([(proj, proj_h)], sems)
    n = wt.shape[0] // 3
    q, k, v = proj[0:n, :], proj[n:2 * n, :], proj[2 * n:3 * n, :]

    def saved(step):
        return pltpu.make_async_copy(kept_s.at[pl.ds(4 * step, 4)], kept_h.at[pl.ds(4 * step, 4)], sems.at[4 + step])

    def keep(step, arrays):
        if step == "first":
            first_s[...] = arrays
            copies.extend(start([(first_s, first_h)], sems, 1))
        elif step == "last":
            last_s[...] = arrays
            copies.extend(start([(last_s, last_h)], sems, 2))
        else:
            for i, array in enumerate(arrays):
                kept_s[4 * step + i] = squeeze(array)
            saved(step).start()

    kept_s[3] = jnp.zeros(kept_s.shape[1:], F32)
    att, first, last, mid, z, sum_t, y_t, root, k_land, q_land = core_forward(
        q, k, v, length, bands(taps, n // HD, False), keep)
    for i, m in enumerate((mid, z, sum_t, y_t, root, k_land, q_land)):
        mats[i] = squeeze(m)
    copies += start([(mats, mats_h)], sems, 3)
    att_s[...] = att
    copies += start([(att_s, att_h)], sems, 4 + NEWTON)
    for r, out in enumerate((att0, att1, att2, att3)):
        out[...] = att_s[:, pl.ds(offs[r], rows)]
    for step in range(NEWTON):
        saved(step).wait()
    finish(copies)


def forward_call(lengths, taps, xs, wt):
    rows, width = xs[0].shape
    n = wt.shape[0] // 3
    slots = 4 * rows
    saved = [((3 * n, slots), BF), ((n, slots), F32), ((n, slots), F32), ((N_MATS, HD, n), F32), ((N_KEPT, HD, n), F32)]
    attended = struct((n, slots), BF)
    return pl.pallas_call(
        forward_kernel,
        in_specs=[SM] * 2 + [VM] * 5,
        out_specs=[VM] * 4 + [HB] * 6,
        out_shape=[struct((n, rows), BF)] * 4 + [struct(*s) for s in saved] + [attended],
        scratch_shapes=[pltpu.VMEM((n, slots), BF)]
        + [pltpu.VMEM(*s) for s in saved]
        + [pltpu.SemaphoreType.DMA((5 + NEWTON,))],
        compiler_params=pltpu.CompilerParams(vmem_limit_bytes=60 << 20),
        cost_estimate=cost(10),
        name="core_forward",
    )(lengths, taps, *xs, wt)


def backward_kernel(slotted, lengths, taps, a0, a1, a2, a3, b0, b1, b2, b3, wo, proj_h, first_h, last_h, mats_h, kept_h, att_h, x0, x1, x2, x3, wt,
                    dx0, dx13, dx2, *rest):
    outs, (g_s, dp_s, tot_s, vec_s, out_s, proj, first_s, last_s, mats, kept_s, att_s, sems) = rest[:-12], rest[-12:]
    nar, wide, length = lax.axis_index("narrow"), lax.axis_index("wide"), lengths[0]
    copies = start([(mats_h, mats), (first_h, first_s), (proj_h, proj), (last_h, last_s), (kept_h, kept_s), (att_h, att_s)], sems)
    rows = x0.shape[0]
    offs = [pl.multiple_of((nar ^ r) * rows, rows) for r in range(4)]
    half = rows // 2
    for r, (a, b) in enumerate(((a0, b0), (a1, b1), (a2, b2), (a3, b3))):
        g_s[:, pl.ds(offs[r], half)] = nt(wo[...], a[...]).astype(BF)
        g_s[:, pl.ds(pl.multiple_of(offs[r] + half, half), half)] = nt(wo[...], b[0:half, :]).astype(BF)
    vectors = sum(b[half:, :].astype(F32) for b in (b0, b1, b2, b3))
    n = wt.shape[0] // 3
    heads = n // HD
    band = bands(taps, heads, True)
    parts = frame(length, 4 * rows, heads)
    block = parts[0]
    finish(copies[:4])
    q, k, v = proj[0:n, :], proj[n:2 * n, :], proj[2 * n:3 * n, :]
    mid, z, sum_t, y_t, root, k_land, q_land = [spread(mats[i], block) for i in range(N_MATS)]

    def kept(step):
        first = isinstance(step, int) and step == 0
        got = [spread(kept_s[4 * step + i], block) for i in range(3 if first else 4)]
        return got + [None] if first else got

    dq, dk, dv, corr = core_backward(g_s[...], q, k, v, parts, first_s[...], last_s[...], mid, z, sum_t, y_t, root,
                                     kept, k_land, q_land, band, copies[4].wait)
    dp_s[0:n, :] = dq.astype(BF)
    dp_s[n:2 * n, :] = dk.astype(BF)
    dp_s[2 * n:3 * n, :] = dv.astype(BF)
    total = None
    for r, x in enumerate((x0, x1, x2, x3)):
        block = dp_s[:, pl.ds(offs[r], rows)]
        back = tn(block, wt[...]).astype(BF)
        if r & 1:
            dx13[r >> 1] = back
        else:
            (dx2 if r else dx0)[...] = back
        term = nn(block, x[...])
        total = term if total is None else total + term
    copies[5].wait()
    output = None
    for r, (a, b) in enumerate(((a0, b0), (a1, b1), (a2, b2), (a3, b3))):
        term = nn(att_s[:, pl.ds(offs[r], half)], a[...])
        term = term + nn(att_s[:, pl.ds(pl.multiple_of(offs[r] + half, half), half)], b[0:half, :])
        output = term if output is None else output + term
    vec_s[...] = jnp.zeros_like(vec_s)
    lines = [vectors[i : i + 1, :] for i in range(VEC_TAPS)]
    lines += corr
    if not slotted:
        in_grad, out_grad, vec_o = outs
        in_grad[...] = total.astype(BF)
        out_grad[...] = output.astype(BF)
        for i, line in enumerate(lines):
            vec_o[i : i + 1, 0 : line.shape[1]] = line
        return
    tot_s[...] = total
    out_s[...] = output
    for i, line in enumerate(lines):
        vec_s[i >> 1, (i & 1) : (i & 1) + 1, 0 : line.shape[1]] = line
    wides = 8
    part, more, half = total.shape[0] // wides, output.shape[0] // wides, total.shape[1] // 2
    for s in range(wides):
        w = s ^ wide
        x, z0, z1 = s & 1, (s >> 1) & 1, s >> 2
        rows_in = tot_s[pl.ds(pl.multiple_of(w * part, 8), part), :].astype(BF)
        rows_vec = vec_s[w].astype(BF)
        rows_out = out_s[pl.ds(pl.multiple_of(w * more, 8), more), :].astype(BF)
        for slot, lanes in ((outs[x].at[z0, z1], slice(0, half)), (outs[2 + z0].at[x, z1], slice(half, 2 * half))):
            slot[0:part, :] = rows_in[:, lanes]
            slot[part : part + 8, :] = rows_vec[:, lanes]
            slot[part + 8 : part + 8 + more, :] = rows_out[:, lanes]


def backward_call(lengths, taps, attn, wo, saved, xs, wt, n_wide, slotted):
    rows, width = xs[0].shape
    n = wt.shape[0] // 3
    slots = 4 * rows
    sums = (
        [struct((2, 2, 4 * n // n_wide + 8, width // 2), BF)] * 4
        if slotted
        else [struct((3 * n, width), BF), struct((n, width), BF), struct((16, width), F32)]
    )
    return pl.pallas_call(
        functools.partial(backward_kernel, slotted),
        in_specs=[SM] * 2 + [VM] * 9 + [HB] * 6 + [VM] * 5,
        out_specs=[VM] * (3 + len(sums)),
        out_shape=[struct((rows, width), BF), struct((2, rows, width), BF), struct((rows, width), BF)] + sums,
        scratch_shapes=[
            pltpu.VMEM((n, slots), BF),
            pltpu.VMEM((3 * n, slots), BF),
            pltpu.VMEM((3 * n, width), F32),
            pltpu.VMEM((8, 8, width), F32),
            pltpu.VMEM((n, width), F32),
        ]
        + [pltpu.VMEM(s.shape, s.dtype) for s in saved]
        + [pltpu.SemaphoreType.DMA((6,))],
        compiler_params=pltpu.CompilerParams(vmem_limit_bytes=60 << 20),
        cost_estimate=cost(19),
        name="core_backward",
    )(lengths, taps, *attn, wo, *saved, *xs, wt)


EPS = 1e-05
U = [1, 8, 1]


def norm_stats(resid):
    center = jnp.mean(resid, axis=1, keepdims=True)
    centered = resid - center
    inverse = lax.rsqrt(jnp.mean(centered * centered, axis=1, keepdims=True) + EPS)
    return centered * inverse, inverse


def norm_pull(grad, normalized, inverse, gain):
    scaled = grad * gain
    return inverse * (
        scaled
        - jnp.mean(scaled, axis=1, keepdims=True)
        - normalized * jnp.mean(scaled * normalized, axis=1, keepdims=True)
    )


def total(rows):
    return jnp.sum(rows, axis=0, keepdims=True)


def ffn_kernel(slotted, x, a0, a1, a2, a3, w0, w1, w2, w3, g1, b1, ub, db, g2, b2, cot, up_h, down_h,
               mixed, res1, attn_a, attn_b, *rest):
    outs, (up, down, hid_s, slope, pre_s, hold_d, hold_u, bias_s, sems) = rest[:-9], rest[-9:]
    chunks = 4
    ff = up.shape[1]
    size = ff // chunks
    nar, wide = lax.axis_index("narrow"), lax.axis_index("wide")

    def part(c):
        return pl.ds(pl.multiple_of(c * size, size), size)

    def up_copy(c):
        return pltpu.make_async_copy(up_h.at[:, part(c)], up.at[:, part(c)], sems.at[2 * c])

    def down_copy(c):
        return pltpu.make_async_copy(down_h.at[part(c), :], down.at[part(c), :], sems.at[2 * c + 1])

    for c in range(chunks):
        up_copy(c).start()
        down_copy(c).start()
    first_sem = 2 * chunks
    if slotted:
        down_to, up_to = outs[:4], outs[4:]
        n_wide, rows = 8, down_to[0].shape[3]
        group, many = 4 * rows, 4
    else:
        down_to, up_to = outs[:1], outs[1:]
        group, many = size, 1
    groups = ff // group

    def outer(left, right, hold, w, sem, targets):
        at = pl.multiple_of(w * group, group)
        hold[pl.ds(at, group), :] = tn(left[:, pl.ds(at, group)], right).astype(BF)
        if not slotted:
            pltpu.make_async_copy(hold.at[pl.ds(at, group), :], targets[0].at[pl.ds(at, group), :], sems.at[sem + w]).start()
        for n in range(4 if slotted else 0):
            block = hold.at[pl.ds(pl.multiple_of(at + n * rows, rows), rows), :]
            slot_n, slot_w = n ^ nar, w ^ wide
            core, y, x, z0, z1 = slot_n & 1, slot_n >> 1, slot_w & 1, (slot_w >> 1) & 1, slot_w >> 2
            lead, second = (x, y) if targets is down_to else (y, x)
            for i in range(4):

                @pl.when(2 * core + lead == i)
                def _():
                    pltpu.make_async_copy(
                        block, targets[i].at[second, z0, z1, pl.ds(0, rows)], sems.at[sem + 4 * w + n]
                    ).start()

    def outer_wait(hold, sem, targets):
        def one(i, carry):
            height = group // many
            block = hold.at[pl.ds(pl.multiple_of(i * height, height), height), :]
            target = targets[0].at[0, 0, 0, pl.ds(0, rows)] if slotted else targets[0].at[pl.ds(0, group), :]
            pltpu.make_async_copy(block, target, sems.at[sem + i]).wait()
            return carry

        lax.fori_loop(0, groups * many, one, 0)

    attention = tn(a0[...], w0[...]) + tn(a1[...], w1[...]) + tn(a2[...], w2[...]) + tn(a3[...], w3[...])
    n1, inv1 = norm_stats(x[...].astype(F32) + attention)
    normed = n1 * g1[...] + b1[...]
    ffn_in = normed.astype(BF)

    def ahead(c, out):
        cut = part(c)
        up_copy(c).wait()
        pre = nn(ffn_in, up[:, cut]) + ub[:, cut]
        below = 0.5 * (1.0 + lax.erf(pre * 0.7071067811865476))
        hid = (pre * below).astype(BF)
        slope[:, cut] = below + pre * (0.3989422804014327 * jnp.exp(-0.5 * (pre * pre)))
        hid_s[:, cut] = hid
        down_copy(c).wait()
        return out + nn(hid, down[cut, :])

    out = lax.fori_loop(0, chunks, ahead, jnp.zeros(x.shape, F32), unroll=U[0])
    n2, inv2 = norm_stats(normed + (out + db[...]))
    mixed[...] = (n2 * g2[...] + b2[...]).astype(BF)
    cotangent = cot[...].astype(F32)
    res2 = norm_pull(cotangent, n2, inv2, g2[...])
    low = res2.astype(BF)

    def down_outer(w, carry):
        outer(hid_s, low, hold_d, w, first_sem, down_to)
        return carry

    lax.fori_loop(0, groups, down_outer, 0, unroll=U[1])
    second_sem = first_sem + groups * many

    def behind(c, grad):
        cut = part(c)
        pre = nt(low, down[cut, :]) * slope[:, cut]
        bias_s[:, cut] = total(pre)
        pre = pre.astype(BF)
        pre_s[:, cut] = pre
        for i in range(groups // chunks):
            outer(pre_s, ffn_in, hold_u, c * (groups // chunks) + i, second_sem, up_to)
        return grad + nt(pre, up[:, cut])

    grad = lax.fori_loop(0, chunks, behind, res2, unroll=U[2])
    back = norm_pull(grad, n1, inv1, g1[...])
    res1[...] = back
    attn = back.astype(BF)
    half = x.shape[0] // 2
    attn_a[...] = attn[:half]
    attn_b[0:half, :] = attn[half:]
    vectors = [total(grad * n1), total(grad), total(res2), total(cotangent * n2), total(cotangent)]
    width = x.shape[1]
    vectors += [bias_s[:, width * j : width * (j + 1)] for j in range(ff // width)]
    vectors.append(jnp.zeros((attn_b.shape[0] - half - len(vectors), width), F32))
    attn_b[half:, :] = jnp.concatenate(vectors, axis=0).astype(BF)
    outer_wait(hold_d, first_sem, down_to)
    outer_wait(hold_u, second_sem, up_to)


def ffn_call(x, att, wo, g1, b1, ub, db, g2, b2, cot, up, down, n_wide, slotted):
    rows, width = x.shape
    ff = up.shape[1]
    part = ff // (4 * n_wide)
    if slotted:
        sums = [struct((2, 2, 2, part, width), BF)] * 8
    else:
        sums = [struct((ff, width), BF)] * 2
    return pl.pallas_call(
        functools.partial(ffn_kernel, slotted),
        in_specs=[VM] * 16 + [HB] * 2,
        out_specs=[VM] * 4 + [HB] * len(sums),
        out_shape=[struct((rows, width), BF), struct((rows, width), F32)]
        + [struct((rows // 2 + more, width), BF) for more in (0, 16)]
        + sums,
        scratch_shapes=[
            pltpu.VMEM((width, ff), BF),
            pltpu.VMEM((ff, width), BF),
            pltpu.VMEM((rows, ff), BF),
            pltpu.VMEM((rows, ff), F32),
            pltpu.VMEM((rows, ff), BF),
            pltpu.VMEM((ff, width), BF),
            pltpu.VMEM((ff, width), BF),
            pltpu.VMEM((1, ff), F32),
            pltpu.SemaphoreType.DMA((8 + 64,)),
        ],
        compiler_params=pltpu.CompilerParams(vmem_limit_bytes=60 << 20),
        cost_estimate=cost(20),
        name="ffn",
    )(x, *att, *wo, g1, b1, ub, db, g2, b2, cot, up, down)


def to_slots(me, whole, n_wide):
    count = 4 * n_wide
    slot = jnp.arange(count).reshape(n_wide, 2, 2).transpose(2, 1, 0)
    picked = whole.reshape(count, -1, whole.shape[-1])[slot ^ me]
    return picked[0], picked[1]


def finish_kernel(orders, left, right, input_o, output_o, vec_o):
    wide = lax.axis_index("wide")
    wides, half = left.shape[0], left.shape[2]
    local = output_o.shape[0]
    part, more = 3 * local // wides, local // wides
    for side, (pool, order) in enumerate(zip((left, right), orders)):
        lanes = pl.ds(side * half, half)
        for s in range(wides):
            w = order[s] ^ wide
            input_o[pl.ds(pl.multiple_of(w * part, 8), part), lanes] = pool[s, 0:part, :].astype(F32)
            vec_o[w, :, lanes] = pool[s, part : part + 8, :].astype(F32)
            output_o[pl.ds(pl.multiple_of(w * more, 8), more), lanes] = pool[s, part + 8 : part + 8 + more, :].astype(F32)


def finish_call(orders, left, right, local):
    wides, rows, half = left.shape
    return pl.pallas_call(
        functools.partial(finish_kernel, orders),
        in_specs=[VM, VM],
        out_specs=[VM] * 3,
        out_shape=[struct((3 * local, 2 * half), F32), struct((local, 2 * half), F32), struct((wides, 8, 2 * half), F32)],
        compiler_params=pltpu.CompilerParams(vmem_limit_bytes=60 << 20),
        cost_estimate=cost(3),
        name="finish",
    )(left, right)


def build(mesh):
    n_wide, n_narrow = mesh.shape["wide"], mesh.shape["narrow"]
    count = n_wide * n_narrow
    wide_bits = []
    bit = n_narrow
    while bit < count:
        wide_bits.append(bit)
        bit *= 2

    def swap(block, mask):
        return lax.ppermute(block, AXES, [(i, i ^ mask) for i in range(count)])

    def after(value, *earlier):
        return lax.optimization_barrier((value, earlier))[0]

    def gather_relative(block):
        far = swap(block, 2)
        near = swap(block, 1)
        return [block, near, far, swap(far, 1)]

    def exchange_relative(blocks):
        return [blocks[r] if r == 0 else swap(blocks[r], r) for r in range(n_narrow)]

    class Halving:
        def __init__(self, parts, masks):
            shape = [2] * len(masks) + list(parts[0].shape[-2:])
            self.masks, self.parts = list(masks), [part.reshape(shape) for part in parts]

        def split(self, mask):
            axis = self.masks.index(mask)
            self.masks.pop(axis)
            sides = [[lax.index_in_dim(part, i, axis, keepdims=False) for part in self.parts] for i in range(2)]
            self.parts = sides[0]
            self.sent = sum(part.astype(F32) for part in sides[1]).astype(BF)
            self.mask = mask

        def send(self):
            self.parts = self.parts + [swap(self.sent, self.mask)]

        def step(self, mask):
            self.split(mask)
            self.send()

        def total(self):
            return sum(part.astype(F32) for part in self.parts)

    def gather_order(masks):
        order = [0]
        for mask in masks:
            order = order + [w ^ (mask // n_narrow) for w in order]
        return order

    def double(block, mask):
        return jnp.concatenate([block, swap(block, mask)], axis=0)

    def on_device(
        tokens,
        lengths,
        input_weights,
        output_weight,
        conv_taps,
        first_gain,
        first_bias,
        up_weight,
        up_bias,
        down_weight,
        down_bias,
        second_gain,
        second_bias,
        cotangent,
    ):
        me = lax.axis_index(AXES)
        rows, width = tokens.shape
        local_width = input_weights.shape[2]
        heads = local_width // HD
        wide = lax.axis_index("wide")
        weights_t = jnp.swapaxes(input_weights, 1, 2).reshape(3 * local_width, width)
        token_blocks = gather_relative(tokens)
        weight = after(output_weight, token_blocks[2])
        far, near = swap(weight, 2), swap(weight, 1)
        *att, s0, s1, s2, s3, s4, s5 = forward_call(lengths, conv_taps, token_blocks, weights_t)
        own_att = exchange_relative(att)
        out_rel = [output_weight, near, far, swap(after(far, att[0]), 1)]
        ff_rows = up_weight.shape[1] // count
        slotted = ff_rows % 32 == 0 and n_wide == 8

        def row(vector):
            return vector[None, :]

        mixed, res1, *rest = ffn_call(
            tokens, own_att, out_rel, row(first_gain), row(first_bias), row(up_bias), row(down_bias),
            row(second_gain), row(second_bias), cotangent, up_weight, down_weight, n_wide, slotted,
        )
        attn_a, attn_b, *rest = rest
        attn = gather_relative(attn_a) + gather_relative(attn_b)
        first, *more = wide_bits
        if slotted:

            def begin(parts, lead):
                return (parts[1].astype(F32) + swap(parts[3], 1).astype(F32)).astype(BF), parts, lead

            def go_on(begun, masks):
                sent, parts, lead = begun
                return Halving([parts[0], swap(parts[2], 1), swap(sent, lead)], masks)

            down, up = begin(rest[:4], first), begin(rest[4:], 2)
            attn = list(after(tuple(attn), down[0], up[0]))
            down, up = go_on(down, [2] + more), go_on(up, wide_bits)
        else:
            masks = [2] + wide_bits[::-1]
            same, other = to_slots(me, rest[0], n_wide)
            down = Halving([same, swap(other, 1)], masks)
            down.step(first)
            same, other = to_slots(me, rest[1], n_wide)
            up = Halving([same, swap(other, 1)], masks)
            up.step(2)
        back0, back13, back2, *sums = backward_call(
            lengths, conv_taps, attn, output_weight, [s0, s1, s2, s3, s4, s5], token_blocks, weights_t, n_wide, slotted
        )
        per_wide = -(-(VEC_TAPS + heads) // n_wide)
        near = swap(back13, 1)
        far = (back2.astype(F32) + near[1].astype(F32)).astype(BF)
        if slotted:
            second, third = more
            sent = after((sums[1], sums[3]), down.parts[-1], up.parts[-1])
            left = Halving([sums[0], swap(sent[0], first)], [second, third])
            right = Halving([sums[2], swap(sent[1], second)], [first, third])
            down.split(2)
            down.sent = after(down.sent, sent)
            down.send()

            def both(left_mask, right_mask, *earlier):
                left.split(left_mask)
                right.split(right_mask)
                left.sent, right.sent = after((left.sent, right.sent), *earlier)
                left.send()
                right.send()
                return left.sent, right.sent

            now = both(second, third, near)
            up.split(first)
            up.sent = after(up.sent, now)
            up.send()
            far = swap(after(far, now), 2)
            now = both(third, first)
            left, right = after((left.total().astype(BF), right.total().astype(BF)), down.parts[-1])
            left, right = double(left[None], third), double(right[None], first)
            down.split(second)
            down.sent = after(down.sent, now)
            down.send()
            left, right = after((left, right), far)
            left, right = double(left, second), double(right, third)
            left, right = after((left, right), up.parts[-1], down.parts[-1])
            up.split(second)
            up.sent = after(up.sent, left)
            up.send()
            down.split(third)
            down.sent = after(down.sent, left)
            down.send()
            left, right = double(left, first), double(right, second)
            up.step(third)
            input_out, output_out, vec = finish_call(
                (gather_order([third, second, first]), gather_order([first, third, second])), left, right, local_width
            )
            input_out = jnp.swapaxes(input_out.reshape(3, local_width, width), 1, 2)
            vec = vec[:, :per_wide].reshape(-1, width)
        else:
            far = swap(far, 2)
            vec = sums[2][: VEC_TAPS + heads]
            vec = jnp.pad(vec, ((0, per_wide * n_wide - vec.shape[0]), (0, 0)))
            pool = [block.astype(BF).reshape(n_wide, -1, width) for block in (sums[0], sums[1], vec)]
            pool = Halving([jnp.concatenate(pool, axis=1)[jnp.arange(n_wide) ^ wide]], wide_bits[::-1])
            for mask in wide_bits:
                pool.step(mask)
            pool = pool.total().astype(BF)[None]
            for mask in wide_bits[::-1]:
                pool = double(pool, mask)
            down.step(2)
            up.step(first)
            for mask in more:
                down.step(mask)
                up.step(mask)
            order = jnp.argsort(jnp.array(gather_order(wide_bits[::-1])))[jnp.arange(n_wide) ^ wide]
            pool = pool[order].astype(F32)
            part = local_width // n_wide
            input_out = pool[:, : 3 * part].reshape(3, local_width, width).transpose(0, 2, 1)
            output_out = pool[:, 3 * part : 4 * part].reshape(local_width, width)
            vec = pool[:, 4 * part :].reshape(-1, width)
        tokens_grad = (res1 + back0.astype(F32) + near[0].astype(F32) + far.astype(F32)).astype(BF)
        down_out = down.total()
        up_out = up.total().T
        taps_out = vec[VEC_TAPS : VEC_TAPS + heads, 239 : 239 + KW]
        up_bias_out = lax.dynamic_slice_in_dim(vec[5:VEC_TAPS].reshape(-1), me * ff_rows, ff_rows)
        return (
            mixed,
            tokens_grad,
            input_out,
            output_out,
            taps_out,
            vec[0],
            vec[1],
            up_out,
            up_bias_out,
            down_out,
            vec[2],
            vec[3],
            vec[4],
        )

    return on_device


def solution(mesh):
    spread = P(AXES, None)
    placed = (
        spread,
        P("wide"),
        P(None, None, "narrow"),
        P("narrow", None),
        P("narrow", None),
        P(),
        P(),
        P(),
        P(),
        P(),
        P(),
        P(),
        P(),
        spread,
    )
    results = (
        spread,
        spread,
        P(None, None, "narrow"),
        P("narrow", None),
        P("narrow", None),
        P(),
        P(),
        P(None, AXES),
        P(AXES),
        spread,
        P(),
        P(),
        P(),
    )
    return jax.shard_map(
        build(mesh), mesh=mesh, in_specs=placed, out_specs=results, check_vma=False
    )
```

```python
import functools
import jax
import jax.numpy as jnp
from jax import lax
from jax.experimental import pallas as pl
from jax.experimental.pallas import tpu as pltpu
from jax.sharding import PartitionSpec as P

BF = jnp.bfloat16
F32 = jnp.float32
HD = 64
LM = 64
KW = 33
NEWTON = 6
AXES = ("wide", "narrow")


def dot(a, b, ca, cb):
    return lax.dot_general(a, b, (((ca,), (cb,)), ((), ())), preferred_element_type=F32)

def nn(a, b): return dot(a, b, 1, 0)
def nt(a, b): return dot(a, b, 1, 1)
def tn(a, b): return dot(a, b, 0, 0)

def split(a):
    hi = a.astype(BF)
    return hi, (a - hi.astype(F32)).astype(BF)

def split3(a):
    hi = a.astype(BF)
    rest = a - hi.astype(F32)
    mid = rest.astype(BF)
    return hi, mid, (rest - mid.astype(F32)).astype(BF)

def m3(op, a, b):
    return op(a[0], b[0]) + (op(a[1], b[0]) + op(a[0], b[1]))

def m6(op, a, b):
    return op(a[0], b[0]) + ((op(a[1], b[0]) + op(a[0], b[1])) + (op(a[1], b[1]) + (op(a[2], b[0]) + op(a[0], b[2]))))

def m2l(op, a, b):
    return op(a[0], b) + op(a[1], b)

def m2r(op, a, b):
    return op(a, b[0]) + op(a, b[1])


def frame(length, slots, heads):
    n = heads * LM
    row = lax.broadcasted_iota(jnp.int32, (n, n), 0)
    col = lax.broadcasted_iota(jnp.int32, (n, n), 1)
    block = (row >> 6) == (col >> 6)
    place = lax.broadcasted_iota(jnp.int32, (1, slots), 1)
    live = place < length
    mark = lax.broadcasted_iota(jnp.int32, (n, 1), 0) & (LM - 1)
    begin = (mark * length) >> 6
    end = ((mark + 1) * length) >> 6
    member = jnp.where((place >= begin) & (place < end), 1.0, 0.0).astype(BF)
    mark_l = lax.broadcasted_iota(jnp.int32, (1, n), 1) & (LM - 1)
    count_l = ((((mark_l + 1) * length) >> 6) - ((mark_l * length) >> 6)).astype(F32)
    count_s = (end - begin).astype(F32)
    return block, live, member, 1.0 / count_s, 1.0 / count_l


def head_lane_max(row, heads):
    lane = lax.broadcasted_iota(jnp.int32, row.shape, 1) >> 6
    out = jnp.zeros_like(row)
    for h in range(heads):
        top = jnp.max(jnp.where(lane == h, row, -1.0), axis=1, keepdims=True)
        out = jnp.where(lane == h, top, out)
    return out


def head_lane_sum(row, heads):
    lane = lax.broadcasted_iota(jnp.int32, row.shape, 1) >> 6
    out = jnp.zeros_like(row)
    for h in range(heads):
        total = jnp.sum(jnp.where(lane == h, row, 0.0), axis=1, keepdims=True)
        out = jnp.where(lane == h, total, out)
    return out


def windows(arr, h):
    slots = arr.shape[1]
    rows = arr[HD * h : HD * (h + 1)]
    zero = jnp.zeros((HD, 128), arr.dtype)
    wide = jnp.concatenate([zero, rows, zero], axis=1)
    return jnp.concatenate([wide[:, 128 * b : 128 * b + 384] for b in range(slots // 128)], axis=0)


def bands(taps, heads, turned):
    lane = lax.broadcasted_iota(jnp.int32, (1, 384), 1) - 112
    out = []
    for h in range(heads):
        base = jnp.zeros((1, 384), F32)
        for w in range(KW):
            base = jnp.where(lane == (KW - 1 - w if turned else w), taps[h, w], base)
        out.append(split(pltpu.roll(jnp.broadcast_to(base, (128, 384)), 0, axis=1, stride=1, stride_axis=0)))
    return out


def squeeze(matrix):
    return sum(matrix[HD * h : HD * (h + 1)] for h in range(matrix.shape[0] // HD))


def times(left, right):
    both = nn(jnp.concatenate([left[0], left[1]], axis=0), right[0])
    return both[:HD] + (both[HD:] + nn(left[0], right[1]))


def blocks(pair, block_low):
    return tuple(jnp.concatenate([part] * (block_low.shape[0] // HD), axis=0) * block_low for part in pair)


def packed_eye(n):
    row = lax.broadcasted_iota(jnp.int32, (HD, n), 0)
    lane = lax.broadcasted_iota(jnp.int32, (HD, n), 1)
    return jnp.where(row == (lane & (HD - 1)), 1.0, 0.0)


def spread(packed, block):
    return jnp.where(block, jnp.concatenate([packed] * (block.shape[0] // HD), axis=0), 0.0)


def conv_apply(arr, band, heads):
    slots = arr.shape[1]
    parts = []
    for h in range(heads):
        out = m2r(nt, windows(arr, h), band[h])
        parts.append(jnp.concatenate([out[HD * b : HD * (b + 1)] for b in range(slots // 128)], axis=1))
    return jnp.concatenate(parts, axis=0)


def core_forward(q, k, v, length, band, keep):
    n, slots = q.shape
    heads = n // HD
    block, live, member, inv_s, inv_l = frame(length, slots, heads)
    k_land = jnp.where(block, nt(member, k), 0.0) * inv_s
    q_land = jnp.where(block, nt(member, q), 0.0) * inv_s
    k3, q3 = split3(k_land), split3(q_land)
    x2 = m6(nt, q3, k3) * 0.125
    x2 = jnp.where(block, x2, -1e30)
    e2 = jnp.exp(x2 - jnp.max(x2, axis=1, keepdims=True))
    mid = e2 * (1.0 / jnp.sum(e2, axis=1, keepdims=True))
    cols = jnp.sum(mid, axis=0, keepdims=True)
    inv_max = 1.0 / head_lane_max(cols, heads)
    x3 = m2l(nn, q3[:2], k) * 0.125 + jnp.where(live, 0.0, -1e9)
    e3 = jnp.exp(x3 - jnp.max(x3, axis=1, keepdims=True))
    last = e3 * (1.0 / jnp.sum(e3, axis=1, keepdims=True))
    last_s = split(last)
    keep("last", last)
    x1 = (m2l(nn, k3[:2], q) * 0.125).reshape(heads, LM, slots)
    e1 = jnp.exp(x1 - jnp.max(x1, axis=1, keepdims=True))
    first = (e1 * (1.0 / jnp.sum(e1, axis=1, keepdims=True))).reshape(n, slots)
    first_s = split(first)
    keep("first", first)
    eye = packed_eye(n)
    low = jnp.where(block, 1.0, 0.0).astype(BF)
    mid_s = split(mid)
    mid_p = tuple(squeeze(part) for part in mid_s)
    p = m3(nt, mid_p, mid_s) * inv_max

    def powers(p):
        ps = split(p)
        pb = blocks(ps, low)
        p2 = times(ps, pb)
        p2s = split(p2)
        p3 = times(p2s, pb)
        return p2, p2s, p3, 0.25 * (13.0 * eye - 15.0 * p + 7.0 * p2 - p3)

    def onward(p, p2, p2s, p3):
        return 0.25 * (13.0 * p - 15.0 * p2 + 7.0 * p3 - times(p2s, blocks(p2s, low)))

    p2, p2s, p3, root = powers(p)
    keep(0, (p, p2, p3))
    p = onward(p, p2, p2s, p3)

    def sweep(step, carry):
        p, root = carry
        p2, p2s, p3, poly = powers(p)
        keep(step, (p, p2, p3, root))
        return onward(p, p2, p2s, p3), times(split(root), blocks(split(poly), low))

    p, root = lax.fori_loop(1, NEWTON - 1, sweep, (p, root))
    p2, p2s, p3, poly = powers(p)
    keep(NEWTON - 1, (p, p2, p3, root))
    root = times(split(root), blocks(split(poly), low))
    z_t = times(split(root), mid_s) * inv_max
    sum_t = jnp.where(block, m2r(nt, v, last_s), 0.0)
    y_t = m3(nn, split(sum_t), blocks(split(z_t), low))
    out = m3(nn, split(y_t), first_s)
    out = out + conv_apply(jnp.where(live, v, jnp.zeros_like(v)), band, heads)
    att = jnp.where(live, out, 0.0).astype(BF)
    return att, first, last, mid, z_t, sum_t, y_t, root, k_land, q_land


def core_backward(g, q, k, v, parts, first, last, mid, z_t, sum_t, y_t, root, kept, k_land, q_land, band, before_newton):
    n, slots = q.shape
    heads = n // HD
    block, live, member, inv_s, inv_l = parts
    g = jnp.where(live, g, jnp.zeros_like(g))
    first_s, last_s = split(first), split(last)
    mid_s = split(mid)
    cols = jnp.sum(mid, axis=0, keepdims=True)
    top = head_lane_max(cols, heads)
    inv_max = 1.0 / top
    low = jnp.where(block, 1.0, 0.0).astype(BF)
    zt_s = blocks(split(z_t), low)
    y = y_t.T
    dfirst = m2l(nn, split(y), g)
    dy_t = jnp.where(block, m2r(nt, g, first_s), 0.0)
    dy = dy_t.T
    dy_s, dyt_s, st_s = split(dy), split(dy_t), split(sum_t)
    s_s = split(sum_t.T)
    dz = m3(nn, dy_s, st_s)
    dz_t = m3(nn, s_s, dyt_s)
    ds_t = m3(nt, dyt_s, zt_s)
    ds = ds_t.T
    dlast = m2l(nn, split(ds), v)
    dv = m3(nn, split(ds_t), last_s)
    dv = dv + jnp.where(live, conv_apply(g, band, heads), 0.0)
    dx3 = last * (dlast - jnp.sum(dlast * last, axis=1, keepdims=True)) * 0.125
    f3 = first.reshape(heads, LM, slots)
    d3 = dfirst.reshape(heads, LM, slots)
    dx1 = (f3 * (d3 - jnp.sum(d3 * f3, axis=1, keepdims=True)) * 0.125).reshape(n, slots)
    before_newton()
    eye = packed_eye(n)
    mid_p = tuple(squeeze(part) for part in mid_s)
    dmid = times(split(root), split(dz_t)) * inv_max
    droot = times(mid_p, split(dz)) * inv_max
    dtop = -jnp.sum(squeeze(dz_t) * z_t, axis=0, keepdims=True)

    def unsweep(step, dp, droot):
        p, p2, p3, before = kept(step)
        ps, p2s = split(p), split(p2)
        pb = blocks(ps, low)
        if before is None:
            dpoly = 0.25 * droot
        else:
            poly = 0.25 * (13.0 * eye - 15.0 * p + 7.0 * p2 - p3)
            droot_s = split(droot)
            dpoly = 0.25 * times(split(before), blocks(droot_s, low))
            droot = times(droot_s, blocks(split(poly), low))
        d1, d2, d3 = -15.0 * dpoly, 7.0 * dpoly, -dpoly
        if dp is not None:
            e = 0.25 * dp
            es = split(e)
            d1 = d1 + 13.0 * e
            d2 = d2 - 15.0 * e - (times(es, blocks(p2s, low)) + times(p2s, blocks(es, low)))
            d3 = d3 + 7.0 * e
        d3s = split(d3)
        d2 = d2 + times(d3s, pb)
        d1 = d1 + times(p2s, blocks(d3s, low))
        d2s = split(d2)
        return d1 + (times(d2s, pb) + times(ps, blocks(d2s, low))), droot

    dp, droot = unsweep(NEWTON - 1, None, droot)
    dp, droot = lax.fori_loop(1, NEWTON - 1, lambda i, c: unsweep(NEWTON - 1 - i, *c), (dp, droot))
    dp, droot = unsweep(0, dp, droot)
    both = spread(dp, block)
    dmid = dmid + times(split(squeeze(both + both.T)), mid_s) * inv_max
    dtop = dtop - jnp.sum(dp * kept(0)[0], axis=0, keepdims=True)
    dtop = head_lane_sum(dtop, heads) * inv_max
    hit = jnp.where(cols == top, 1.0, 0.0)
    dmid = spread(dmid + dtop * hit / head_lane_sum(hit, heads), block)
    dx2 = mid * (dmid - jnp.sum(dmid * mid, axis=1, keepdims=True)) * 0.125
    dx2_s = split(dx2)
    dx1_s, dx3_s = split(dx1), split(dx3)
    kt_s, qt_s = split(k_land.T), split(q_land.T)
    dql_t = (jnp.where(block, m2r(nt, k, dx3_s), 0.0) + m3(nt, kt_s, dx2_s)) * inv_l
    dkl_t = (jnp.where(block, m2r(nt, q, dx1_s), 0.0) + m3(nn, qt_s, dx2_s)) * inv_l
    dq = m3(nn, kt_s, dx1_s) + m2l(nn, split(dql_t), member)
    dk = m3(nn, qt_s, dx3_s) + m2l(nn, split(dkl_t), member)
    corr = []
    vm = jnp.where(live, v, jnp.zeros_like(v))
    ri = lax.broadcasted_iota(jnp.int32, (128, 128), 0)
    ci = lax.broadcasted_iota(jnp.int32, (128, 128), 1)
    flip = jnp.where(ri + ci == 127, 1.0, 0.0).astype(BF)
    for h in range(heads):
        rows = g[HD * h : HD * (h + 1)]
        stack = jnp.concatenate([rows[:, 128 * b : 128 * b + 128] for b in range(slots // 128)], axis=0)
        near = tn(nn(stack, flip).astype(BF), windows(vm, h))
        near = pltpu.roll(near, 0, axis=1, stride=1, stride_axis=0)
        corr.append(jnp.sum(near, axis=0, keepdims=True))
    return dq, dk, dv, corr


N_MATS = 7
VEC_TAPS = 9
N_KEPT = 4 * NEWTON
VM = pl.BlockSpec(memory_space=pltpu.VMEM)
SM = pl.BlockSpec(memory_space=pltpu.SMEM)
HB = pl.BlockSpec(memory_space=pltpu.HBM)


def struct(shape, kind):
    return jax.ShapeDtypeStruct(shape, kind)


def cost(micros):
    return pl.CostEstimate(flops=int(micros * 1.0e9), bytes_accessed=1 << 20, transcendentals=0)


def start(pairs, sems, first=0):
    copies = [pltpu.make_async_copy(src, dst, sems.at[first + i]) for i, (src, dst) in enumerate(pairs)]
    for copy in copies:
        copy.start()
    return copies


def finish(copies):
    for copy in copies:
        copy.wait()


def forward_kernel(lengths, taps, x0, x1, x2, x3, wt, att0, att1, att2, att3, proj_h, first_h, last_h, mats_h, kept_h, att_h,
                   att_s, proj, first_s, last_s, mats, kept_s, sems):
    nar, length = lax.axis_index("narrow"), lengths[0]
    rows = x0.shape[0]
    offs = [pl.multiple_of((nar ^ r) * rows, rows) for r in range(4)]
    for r, x in enumerate((x0, x1, x2, x3)):
        proj[:, pl.ds(offs[r], rows)] = nt(wt[...], x[...]).astype(BF)
    copies = start([(proj, proj_h)], sems)
    n = wt.shape[0] // 3
    q, k, v = proj[0:n, :], proj[n:2 * n, :], proj[2 * n:3 * n, :]

    def saved(step):
        return pltpu.make_async_copy(kept_s.at[pl.ds(4 * step, 4)], kept_h.at[pl.ds(4 * step, 4)], sems.at[4 + step])

    def keep(step, arrays):
        if step == "first":
            first_s[...] = arrays
            copies.extend(start([(first_s, first_h)], sems, 1))
        elif step == "last":
            last_s[...] = arrays
            copies.extend(start([(last_s, last_h)], sems, 2))
        else:
            for i, array in enumerate(arrays):
                kept_s[4 * step + i] = array
            saved(step).start()

    kept_s[3] = jnp.zeros(kept_s.shape[1:], F32)
    att, first, last, mid, z_t, sum_t, y_t, root, k_land, q_land = core_forward(
        q, k, v, length, bands(taps, n // HD, False), keep)
    for i, m in enumerate((mid, z_t, sum_t, y_t, root, k_land, q_land)):
        mats[i] = m if i in (1, 4) else squeeze(m)
    copies += start([(mats, mats_h)], sems, 3)
    att_s[...] = att
    copies += start([(att_s, att_h)], sems, 4 + NEWTON)
    for r, out in enumerate((att0, att1, att2, att3)):
        out[...] = att_s[:, pl.ds(offs[r], rows)]
    for step in range(NEWTON):
        saved(step).wait()
    finish(copies)


def forward_call(lengths, taps, xs, wt):
    rows, width = xs[0].shape
    n = wt.shape[0] // 3
    slots = 4 * rows
    saved = [((3 * n, slots), BF), ((n, slots), F32), ((n, slots), F32), ((N_MATS, HD, n), F32), ((N_KEPT, HD, n), F32)]
    attended = struct((n, slots), BF)
    return pl.pallas_call(
        forward_kernel,
        in_specs=[SM] * 2 + [VM] * 5,
        out_specs=[VM] * 4 + [HB] * 6,
        out_shape=[struct((n, rows), BF)] * 4 + [struct(*s) for s in saved] + [attended],
        scratch_shapes=[pltpu.VMEM((n, slots), BF)]
        + [pltpu.VMEM(*s) for s in saved]
        + [pltpu.SemaphoreType.DMA((5 + NEWTON,))],
        compiler_params=pltpu.CompilerParams(vmem_limit_bytes=60 << 20),
        cost_estimate=cost(10),
        name="core_forward",
    )(lengths, taps, *xs, wt)


def backward_kernel(slotted, lengths, taps, a0, a1, a2, a3, b0, b1, b2, b3, wo, proj_h, first_h, last_h, mats_h, kept_h, att_h, x0, x1, x2, x3, wt,
                    dx0, dx13, dx2, *rest):
    outs, (g_s, dp_s, tot_s, vec_s, out_s, proj, first_s, last_s, mats, kept_s, att_s, sems) = rest[:-12], rest[-12:]
    nar, wide, length = lax.axis_index("narrow"), lax.axis_index("wide"), lengths[0]
    copies = start([(mats_h, mats), (first_h, first_s), (proj_h, proj), (last_h, last_s), (kept_h, kept_s), (att_h, att_s)], sems)
    rows = x0.shape[0]
    offs = [pl.multiple_of((nar ^ r) * rows, rows) for r in range(4)]
    half = rows // 2
    for r, (a, b) in enumerate(((a0, b0), (a1, b1), (a2, b2), (a3, b3))):
        g_s[:, pl.ds(offs[r], half)] = nt(wo[...], a[...]).astype(BF)
        g_s[:, pl.ds(pl.multiple_of(offs[r] + half, half), half)] = nt(wo[...], b[0:half, :]).astype(BF)
    vectors = sum(b[half:, :].astype(F32) for b in (b0, b1, b2, b3))
    n = wt.shape[0] // 3
    heads = n // HD
    band = bands(taps, heads, True)
    parts = frame(length, 4 * rows, heads)
    block = parts[0]
    finish(copies[:4])
    q, k, v = proj[0:n, :], proj[n:2 * n, :], proj[2 * n:3 * n, :]
    mid, z_t, sum_t, y_t, root, k_land, q_land = [mats[i] if i in (1, 4) else spread(mats[i], block) for i in range(N_MATS)]

    def kept(step):
        first = isinstance(step, int) and step == 0
        got = [kept_s[4 * step + i] for i in range(3 if first else 4)]
        return got + [None] if first else got

    dq, dk, dv, corr = core_backward(g_s[...], q, k, v, parts, first_s[...], last_s[...], mid, z_t, sum_t, y_t, root,
                                     kept, k_land, q_land, band, copies[4].wait)
    dp_s[0:n, :] = dq.astype(BF)
    dp_s[n:2 * n, :] = dk.astype(BF)
    dp_s[2 * n:3 * n, :] = dv.astype(BF)
    total = None
    for r, x in enumerate((x0, x1, x2, x3)):
        block = dp_s[:, pl.ds(offs[r], rows)]
        back = tn(block, wt[...]).astype(BF)
        if r & 1:
            dx13[r >> 1] = back
        else:
            (dx2 if r else dx0)[...] = back
        term = nn(block, x[...])
        total = term if total is None else total + term
    copies[5].wait()
    output = None
    for r, (a, b) in enumerate(((a0, b0), (a1, b1), (a2, b2), (a3, b3))):
        term = nn(att_s[:, pl.ds(offs[r], half)], a[...])
        term = term + nn(att_s[:, pl.ds(pl.multiple_of(offs[r] + half, half), half)], b[0:half, :])
        output = term if output is None else output + term
    vec_s[...] = jnp.zeros_like(vec_s)
    lines = [vectors[i : i + 1, :] for i in range(VEC_TAPS)]
    lines += corr
    if not slotted:
        in_grad, out_grad, vec_o = outs
        in_grad[...] = total.astype(BF)
        out_grad[...] = output.astype(BF)
        for i, line in enumerate(lines):
            vec_o[i : i + 1, 0 : line.shape[1]] = line
        return
    tot_s[...] = total
    out_s[...] = output
    for i, line in enumerate(lines):
        vec_s[i >> 1, (i & 1) : (i & 1) + 1, 0 : line.shape[1]] = line
    wides = 8
    part, more = total.shape[0] // wides, output.shape[0] // wides
    for s in range(wides):
        w = s ^ wide
        slot = outs[s & 3].at[s >> 2]
        slot[0:part, :] = tot_s[pl.ds(pl.multiple_of(w * part, 8), part), :].astype(BF)
        slot[part : part + 8, :] = vec_s[w].astype(BF)
        slot[part + 8 : part + 8 + more, :] = out_s[pl.ds(pl.multiple_of(w * more, 8), more), :].astype(BF)


def backward_call(lengths, taps, attn, wo, saved, xs, wt, n_wide, slotted):
    rows, width = xs[0].shape
    n = wt.shape[0] // 3
    slots = 4 * rows
    sums = (
        [struct((2, 4 * n // n_wide + 8, width), BF)] * 4
        if slotted
        else [struct((3 * n, width), BF), struct((n, width), BF), struct((16, width), F32)]
    )
    return pl.pallas_call(
        functools.partial(backward_kernel, slotted),
        in_specs=[SM] * 2 + [VM] * 9 + [HB] * 6 + [VM] * 5,
        out_specs=[VM] * (3 + len(sums)),
        out_shape=[struct((rows, width), BF), struct((2, rows, width), BF), struct((rows, width), BF)] + sums,
        scratch_shapes=[
            pltpu.VMEM((n, slots), BF),
            pltpu.VMEM((3 * n, slots), BF),
            pltpu.VMEM((3 * n, width), F32),
            pltpu.VMEM((8, 8, width), F32),
            pltpu.VMEM((n, width), F32),
        ]
        + [pltpu.VMEM(s.shape, s.dtype) for s in saved]
        + [pltpu.SemaphoreType.DMA((6,))],
        compiler_params=pltpu.CompilerParams(vmem_limit_bytes=60 << 20),
        cost_estimate=cost(28),
        name="core_backward",
    )(lengths, taps, *attn, wo, *saved, *xs, wt)


EPS = 1e-05
U = [4, 8, 4]


def norm_stats(resid):
    center = jnp.mean(resid, axis=1, keepdims=True)
    centered = resid - center
    inverse = lax.rsqrt(jnp.mean(centered * centered, axis=1, keepdims=True) + EPS)
    return centered * inverse, inverse


def norm_pull(grad, normalized, inverse, gain):
    scaled = grad * gain
    return inverse * (
        scaled
        - jnp.mean(scaled, axis=1, keepdims=True)
        - normalized * jnp.mean(scaled * normalized, axis=1, keepdims=True)
    )


def total(rows):
    return jnp.sum(rows, axis=0, keepdims=True)


def ffn_kernel(slotted, x, a0, a1, a2, a3, w0, w1, w2, w3, g1, b1, ub, db, g2, b2, cot, up_h, down_h,
               mixed, res1, attn_a, attn_b, *rest):
    outs, (up, down, hid_s, slope, pre_s, hold_d, hold_u, bias_s, sems) = rest[:-9], rest[-9:]
    chunks = 4
    ff = up.shape[1]
    size = ff // chunks
    nar, wide = lax.axis_index("narrow"), lax.axis_index("wide")

    def part(c):
        return pl.ds(pl.multiple_of(c * size, size), size)

    def up_copy(c):
        return pltpu.make_async_copy(up_h.at[:, part(c)], up.at[:, part(c)], sems.at[2 * c])

    def down_copy(c):
        return pltpu.make_async_copy(down_h.at[part(c), :], down.at[part(c), :], sems.at[2 * c + 1])

    for c in range(chunks):
        up_copy(c).start()
        down_copy(c).start()
    first_sem = 2 * chunks
    if slotted:
        down_to, up_to = outs[:4], outs[4:]
        n_wide, rows = 8, down_to[0].shape[3]
        group, many = 4 * rows, 4
    else:
        down_to, up_to = outs[:1], outs[1:]
        group, many = size, 1
    groups = ff // group

    def outer(left, right, hold, w, sem, targets):
        at = pl.multiple_of(w * group, group)
        hold[pl.ds(at, group), :] = tn(left[:, pl.ds(at, group)], right).astype(BF)
        if not slotted:
            pltpu.make_async_copy(hold.at[pl.ds(at, group), :], targets[0].at[pl.ds(at, group), :], sems.at[sem + w]).start()
        for n in range(4 if slotted else 0):
            block = hold.at[pl.ds(pl.multiple_of(at + n * rows, rows), rows), :]
            slot_n, slot_w = n ^ nar, w ^ wide
            core, y, x, z0, z1 = slot_n & 1, slot_n >> 1, slot_w & 1, (slot_w >> 1) & 1, slot_w >> 2
            lead, second = (x, y) if targets is down_to else (y, x)
            for i in range(4):

                @pl.when(2 * core + lead == i)
                def _():
                    pltpu.make_async_copy(
                        block, targets[i].at[second, z0, z1, pl.ds(0, rows)], sems.at[sem + 4 * w + n]
                    ).start()

    def outer_wait(hold, sem, targets):
        def one(i, carry):
            height = group // many
            block = hold.at[pl.ds(pl.multiple_of(i * height, height), height), :]
            target = targets[0].at[0, 0, 0, pl.ds(0, rows)] if slotted else targets[0].at[pl.ds(0, group), :]
            pltpu.make_async_copy(block, target, sems.at[sem + i]).wait()
            return carry

        lax.fori_loop(0, groups * many, one, 0)

    attention = tn(a0[...], w0[...]) + tn(a1[...], w1[...]) + tn(a2[...], w2[...]) + tn(a3[...], w3[...])
    n1, inv1 = norm_stats(x[...].astype(F32) + attention)
    normed = n1 * g1[...] + b1[...]
    ffn_in = normed.astype(BF)

    def ahead(c, out):
        cut = part(c)
        up_copy(c).wait()
        pre = nn(ffn_in, up[:, cut]) + ub[:, cut]
        below = 0.5 * (1.0 + lax.erf(pre * 0.7071067811865476))
        hid = (pre * below).astype(BF)
        slope[:, cut] = below + pre * (0.3989422804014327 * jnp.exp(-0.5 * (pre * pre)))
        hid_s[:, cut] = hid
        down_copy(c).wait()
        return out + nn(hid, down[cut, :])

    out = lax.fori_loop(0, chunks, ahead, jnp.zeros(x.shape, F32), unroll=U[0])
    n2, inv2 = norm_stats(normed + (out + db[...]))
    mixed[...] = (n2 * g2[...] + b2[...]).astype(BF)
    cotangent = cot[...].astype(F32)
    res2 = norm_pull(cotangent, n2, inv2, g2[...])
    low = res2.astype(BF)

    def down_outer(w, carry):
        outer(hid_s, low, hold_d, w, first_sem, down_to)
        return carry

    lax.fori_loop(0, groups, down_outer, 0, unroll=U[1])
    second_sem = first_sem + groups * many

    def behind(c, grad):
        cut = part(c)
        pre = nt(low, down[cut, :]) * slope[:, cut]
        bias_s[:, cut] = total(pre)
        pre = pre.astype(BF)
        pre_s[:, cut] = pre
        for i in range(groups // chunks):
            outer(pre_s, ffn_in, hold_u, c * (groups // chunks) + i, second_sem, up_to)
        return grad + nt(pre, up[:, cut])

    grad = lax.fori_loop(0, chunks, behind, res2, unroll=U[2])
    back = norm_pull(grad, n1, inv1, g1[...])
    res1[...] = back
    attn = back.astype(BF)
    half = x.shape[0] // 2
    attn_a[...] = attn[:half]
    attn_b[0:half, :] = attn[half:]
    vectors = [total(grad * n1), total(grad), total(res2), total(cotangent * n2), total(cotangent)]
    width = x.shape[1]
    vectors += [bias_s[:, width * j : width * (j + 1)] for j in range(ff // width)]
    vectors.append(jnp.zeros((attn_b.shape[0] - half - len(vectors), width), F32))
    attn_b[half:, :] = jnp.concatenate(vectors, axis=0).astype(BF)
    outer_wait(hold_d, first_sem, down_to)
    outer_wait(hold_u, second_sem, up_to)


def ffn_call(x, att, wo, g1, b1, ub, db, g2, b2, cot, up, down, n_wide, slotted):
    rows, width = x.shape
    ff = up.shape[1]
    part = ff // (4 * n_wide)
    if slotted:
        sums = [struct((2, 2, 2, part, width), BF)] * 8
    else:
        sums = [struct((ff, width), BF)] * 2
    return pl.pallas_call(
        functools.partial(ffn_kernel, slotted),
        in_specs=[VM] * 16 + [HB] * 2,
        out_specs=[VM] * 4 + [HB] * len(sums),
        out_shape=[struct((rows, width), BF), struct((rows, width), F32)]
        + [struct((rows // 2 + more, width), BF) for more in (0, 16)]
        + sums,
        scratch_shapes=[
            pltpu.VMEM((width, ff), BF),
            pltpu.VMEM((ff, width), BF),
            pltpu.VMEM((rows, ff), BF),
            pltpu.VMEM((rows, ff), F32),
            pltpu.VMEM((rows, ff), BF),
            pltpu.VMEM((ff, width), BF),
            pltpu.VMEM((ff, width), BF),
            pltpu.VMEM((1, ff), F32),
            pltpu.SemaphoreType.DMA((8 + 64,)),
        ],
        compiler_params=pltpu.CompilerParams(vmem_limit_bytes=60 << 20),
        cost_estimate=cost(20),
        name="ffn",
    )(x, *att, *wo, g1, b1, ub, db, g2, b2, cot, up, down)


def to_slots(me, whole, n_wide):
    count = 4 * n_wide
    slot = jnp.arange(count).reshape(n_wide, 2, 2).transpose(2, 1, 0)
    picked = whole.reshape(count, -1, whole.shape[-1])[slot ^ me]
    return picked[0], picked[1]


def finish_kernel(*refs):
    pools, (input_o, output_o, vec_o, vec_s) = refs[:-4], refs[-4:]
    wide = lax.axis_index("wide")
    local = output_o.shape[0]
    part, more = 3 * local // 8, local // 8
    for s in range(8):
        pool, w = pools[s & 3].at[s >> 2], s ^ wide
        input_o[pl.ds(pl.multiple_of(w * part, 8), part), :] = pool[0:part, :].astype(F32)
        vec_s[w] = pool[part : part + 8, :].astype(F32)
        output_o[pl.ds(pl.multiple_of(w * more, 8), more), :] = pool[part + 8 : part + 8 + more, :].astype(F32)
    for w in range(8):
        vec_o[2 * w : 2 * w + 2, :] = vec_s[w, 0:2, :]


def finish_call(pools, local):
    width = pools[0].shape[2]
    return pl.pallas_call(
        finish_kernel,
        in_specs=[VM] * 4,
        out_specs=[VM] * 3,
        out_shape=[struct((3 * local, width), F32), struct((local, width), F32), struct((16, width), F32)],
        scratch_shapes=[pltpu.VMEM((8, 8, width), F32)],
        compiler_params=pltpu.CompilerParams(vmem_limit_bytes=60 << 20),
        cost_estimate=cost(3),
        name="finish",
    )(*pools)


def build(mesh):
    n_wide, n_narrow = mesh.shape["wide"], mesh.shape["narrow"]
    count = n_wide * n_narrow
    wide_bits = []
    bit = n_narrow
    while bit < count:
        wide_bits.append(bit)
        bit *= 2

    def swap(block, mask):
        return lax.ppermute(block, AXES, [(i, i ^ mask) for i in range(count)])

    def after(value, *earlier):
        return lax.optimization_barrier((value, earlier))[0]

    def gather_relative(block):
        far = swap(block, 2)
        near = swap(block, 1)
        return [block, near, far, swap(far, 1)]

    def exchange_relative(blocks):
        return [blocks[r] if r == 0 else swap(blocks[r], r) for r in range(n_narrow)]

    class Halving:
        def __init__(self, parts, masks):
            shape = [2] * len(masks) + list(parts[0].shape[-2:])
            self.masks, self.parts = list(masks), [part.reshape(shape) for part in parts]

        def split(self, mask):
            axis = self.masks.index(mask)
            self.masks.pop(axis)
            sides = [[lax.index_in_dim(part, i, axis, keepdims=False) for part in self.parts] for i in range(2)]
            self.parts = sides[0]
            self.sent = sum(part.astype(F32) for part in sides[1]).astype(BF)
            self.mask = mask

        def send(self):
            self.parts = self.parts + [swap(self.sent, self.mask)]

        def step(self, mask):
            self.split(mask)
            self.send()

        def total(self):
            return sum(part.astype(F32) for part in self.parts)

    def gather_order(masks):
        order = [0]
        for mask in masks:
            order = order + [w ^ (mask // n_narrow) for w in order]
        return order

    def double(block, mask):
        return jnp.concatenate([block, swap(block, mask)], axis=0)

    def on_device(
        tokens,
        lengths,
        input_weights,
        output_weight,
        conv_taps,
        first_gain,
        first_bias,
        up_weight,
        up_bias,
        down_weight,
        down_bias,
        second_gain,
        second_bias,
        cotangent,
    ):
        me = lax.axis_index(AXES)
        rows, width = tokens.shape
        local_width = input_weights.shape[2]
        heads = local_width // HD
        wide = lax.axis_index("wide")
        weights_t = jnp.swapaxes(input_weights, 1, 2).reshape(3 * local_width, width)
        token_blocks = gather_relative(tokens)
        weight = after(output_weight, token_blocks[2])
        far, near = swap(weight, 2), swap(weight, 1)
        *att, s0, s1, s2, s3, s4, s5 = forward_call(lengths, conv_taps, token_blocks, weights_t)
        own_att = exchange_relative(att)
        out_rel = [output_weight, near, far, swap(after(far, att[0]), 1)]
        ff_rows = up_weight.shape[1] // count
        slotted = ff_rows % 32 == 0 and n_wide == 8

        def row(vector):
            return vector[None, :]

        mixed, res1, *rest = ffn_call(
            tokens, own_att, out_rel, row(first_gain), row(first_bias), row(up_bias), row(down_bias),
            row(second_gain), row(second_bias), cotangent, up_weight, down_weight, n_wide, slotted,
        )
        attn_a, attn_b, *rest = rest
        attn = gather_relative(attn_a) + gather_relative(attn_b)
        first, *more = wide_bits
        if slotted:

            def begin(parts, lead):
                return (parts[1].astype(F32) + swap(parts[3], 1).astype(F32)).astype(BF), parts, lead

            def go_on(begun, masks):
                sent, parts, lead = begun
                return Halving([parts[0], swap(parts[2], 1), swap(sent, lead)], masks)

            down, up = begin(rest[:4], first), begin(rest[4:], 2)
            up = (after(up[0], attn[6]),) + up[1:]
            attn = list(after(tuple(attn), down[0], up[0]))
            down, up = go_on(down, [2] + more), go_on(up, wide_bits)
        else:
            masks = [2] + wide_bits[::-1]
            same, other = to_slots(me, rest[0], n_wide)
            down = Halving([same, swap(other, 1)], masks)
            down.step(first)
            same, other = to_slots(me, rest[1], n_wide)
            up = Halving([same, swap(other, 1)], masks)
            up.step(2)
        back0, back13, back2, *sums = backward_call(
            lengths, conv_taps, attn, output_weight, [s0, s1, s2, s3, s4, s5], token_blocks, weights_t, n_wide, slotted
        )
        per_wide = -(-(VEC_TAPS + heads) // n_wide)
        near = swap(back13, 1)
        far = (back2.astype(F32) + near[1].astype(F32)).astype(BF)

        def finish_tokens(far):
            return (res1 + back0.astype(F32) + near[0].astype(F32) + far.astype(F32)).astype(BF)

        if slotted:
            second, third = more

            def total(*blocks):
                return sum(block.astype(F32) for block in blocks)

            near_kept, near_sent, far_kept, far_sent = after(tuple(sums), down.parts[-1], up.parts[-1])
            far_came, near_came = swap(far_sent, first), swap(near_sent, first)
            down.parts, up.parts = after((down.parts, up.parts), far_came)
            far_sum = total(far_kept, far_came).astype(BF)
            z0_came = swap(far_sum, second)
            down.split(2)
            down.sent = after(down.sent, far_sum)
            down.send()
            far = swap(after(far, far_sum), 2)
            up.split(first)
            up.sent = after(up.sent, near_came)
            up.send()
            z1_sum = total(near_kept[1], near_came[1], z0_came[1]).astype(BF)
            own = total(near_kept[0], near_came[0], z0_came[0], swap(z1_sum, third)).astype(BF)
            pair = jnp.stack([own, swap(own, third)])
            z0_pair = swap(pair, second)
            own_x, z0_x = swap(pair, first), swap(z0_pair, first)
            tokens_grad = finish_tokens(far)

            def both(index):
                return jnp.concatenate([total(*[index(part) for part in side]) for side in (down.parts, up.parts)], axis=-2)

            sent = after(both(lambda part: part[1]).astype(BF), own)
            came = swap(sent, second)
            down.parts = [part[0] for part in down.parts] + [came[:, :ff_rows]]
            up.parts = [part[0] for part in up.parts] + [came[:, ff_rows:]]
            sent = after(both(lambda part: part[1]).astype(BF), z0_pair, tokens_grad)
            came = swap(sent, third)
            down = Halving([part[0] for part in down.parts] + [came[:ff_rows]], [])
            up = Halving([part[0] for part in up.parts] + [came[ff_rows:]], [])
            input_out, output_out, vec = finish_call([pair, own_x, z0_pair, z0_x], local_width)
            input_out = jnp.swapaxes(input_out.reshape(3, local_width, width), 1, 2)
        else:
            tokens_grad = finish_tokens(swap(far, 2))
            vec = sums[2][: VEC_TAPS + heads]
            vec = jnp.pad(vec, ((0, per_wide * n_wide - vec.shape[0]), (0, 0)))
            pool = [block.astype(BF).reshape(n_wide, -1, width) for block in (sums[0], sums[1], vec)]
            pool = Halving([jnp.concatenate(pool, axis=1)[jnp.arange(n_wide) ^ wide]], wide_bits[::-1])
            for mask in wide_bits:
                pool.step(mask)
            pool = pool.total().astype(BF)[None]
            for mask in wide_bits[::-1]:
                pool = double(pool, mask)
            down.step(2)
            up.step(first)
            for mask in more:
                down.step(mask)
                up.step(mask)
            order = jnp.argsort(jnp.array(gather_order(wide_bits[::-1])))[jnp.arange(n_wide) ^ wide]
            pool = pool[order].astype(F32)
            part = local_width // n_wide
            input_out = pool[:, : 3 * part].reshape(3, local_width, width).transpose(0, 2, 1)
            output_out = pool[:, 3 * part : 4 * part].reshape(local_width, width)
            vec = pool[:, 4 * part :].reshape(-1, width)
        down_out = down.total()
        up_out = up.total().T
        taps_out = vec[VEC_TAPS : VEC_TAPS + heads, 239 : 239 + KW]
        up_bias_out = lax.dynamic_slice_in_dim(vec[5:VEC_TAPS].reshape(-1), me * ff_rows, ff_rows)
        return (
            mixed,
            tokens_grad,
            input_out,
            output_out,
            taps_out,
            vec[0],
            vec[1],
            up_out,
            up_bias_out,
            down_out,
            vec[2],
            vec[3],
            vec[4],
        )

    return on_device


def solution(mesh):
    spread = P(AXES, None)
    placed = (
        spread,
        P("wide"),
        P(None, None, "narrow"),
        P("narrow", None),
        P("narrow", None),
        P(),
        P(),
        P(),
        P(),
        P(),
        P(),
        P(),
        P(),
        spread,
    )
    results = (
        spread,
        spread,
        P(None, None, "narrow"),
        P("narrow", None),
        P("narrow", None),
        P(),
        P(),
        P(None, AXES),
        P(AXES),
        spread,
        P(),
        P(),
        P(),
    )
    return jax.shard_map(
        build(mesh), mesh=mesh, in_specs=placed, out_specs=results, check_vma=False
    )
```

```python
import functools
import jax
import jax.numpy as jnp
from jax import lax
from jax.experimental import pallas as pl
from jax.experimental.pallas import tpu as pltpu
from jax.sharding import PartitionSpec as P

BF = jnp.bfloat16
F32 = jnp.float32
HD = 64
LM = 64
KW = 33
NEWTON = 6
AXES = ("wide", "narrow")


def dot(a, b, ca, cb):
    return lax.dot_general(a, b, (((ca,), (cb,)), ((), ())), preferred_element_type=F32)

def nn(a, b): return dot(a, b, 1, 0)
def nt(a, b): return dot(a, b, 1, 1)
def tn(a, b): return dot(a, b, 0, 0)

def split(a):
    hi = a.astype(BF)
    return hi, (a - hi.astype(F32)).astype(BF)

def split3(a):
    hi = a.astype(BF)
    rest = a - hi.astype(F32)
    mid = rest.astype(BF)
    return hi, mid, (rest - mid.astype(F32)).astype(BF)

def m3(op, a, b):
    return op(a[0], b[0]) + (op(a[1], b[0]) + op(a[0], b[1]))

def m6(op, a, b):
    return op(a[0], b[0]) + ((op(a[1], b[0]) + op(a[0], b[1])) + (op(a[1], b[1]) + (op(a[2], b[0]) + op(a[0], b[2]))))

def m2l(op, a, b):
    return op(a[0], b) + op(a[1], b)

def m2r(op, a, b):
    return op(a, b[0]) + op(a, b[1])


def frame(length, slots, heads):
    n = heads * LM
    row = lax.broadcasted_iota(jnp.int32, (n, n), 0)
    col = lax.broadcasted_iota(jnp.int32, (n, n), 1)
    block = (row >> 6) == (col >> 6)
    place = lax.broadcasted_iota(jnp.int32, (1, slots), 1)
    live = place < length
    mark = lax.broadcasted_iota(jnp.int32, (n, 1), 0) & (LM - 1)
    begin = (mark * length) >> 6
    end = ((mark + 1) * length) >> 6
    member = jnp.where((place >= begin) & (place < end), 1.0, 0.0).astype(BF)
    mark_l = lax.broadcasted_iota(jnp.int32, (1, n), 1) & (LM - 1)
    count_l = ((((mark_l + 1) * length) >> 6) - ((mark_l * length) >> 6)).astype(F32)
    count_s = (end - begin).astype(F32)
    return block, live, member, 1.0 / count_s, 1.0 / count_l


def head_lane_max(row, heads):
    lane = lax.broadcasted_iota(jnp.int32, row.shape, 1) >> 6
    out = jnp.zeros_like(row)
    for h in range(heads):
        top = jnp.max(jnp.where(lane == h, row, -1.0), axis=1, keepdims=True)
        out = jnp.where(lane == h, top, out)
    return out


def head_lane_sum(row, heads):
    lane = lax.broadcasted_iota(jnp.int32, row.shape, 1) >> 6
    out = jnp.zeros_like(row)
    for h in range(heads):
        total = jnp.sum(jnp.where(lane == h, row, 0.0), axis=1, keepdims=True)
        out = jnp.where(lane == h, total, out)
    return out


def windows(arr, h):
    slots = arr.shape[1]
    rows = arr[HD * h : HD * (h + 1)]
    zero = jnp.zeros((HD, 128), arr.dtype)
    wide = jnp.concatenate([zero, rows, zero], axis=1)
    return jnp.concatenate([wide[:, 128 * b : 128 * b + 384] for b in range(slots // 128)], axis=0)


def bands(taps, heads, turned):
    lane = lax.broadcasted_iota(jnp.int32, (1, 384), 1) - 112
    out = []
    for h in range(heads):
        base = jnp.zeros((1, 384), F32)
        for w in range(KW):
            base = jnp.where(lane == (KW - 1 - w if turned else w), taps[h, w], base)
        out.append(split(pltpu.roll(jnp.broadcast_to(base, (128, 384)), 0, axis=1, stride=1, stride_axis=0)))
    return out


def squeeze(matrix):
    return sum(matrix[HD * h : HD * (h + 1)] for h in range(matrix.shape[0] // HD))


def times(left, right):
    both = nn(jnp.concatenate([left[0], left[1]], axis=0), right[0])
    return both[:HD] + (both[HD:] + nn(left[0], right[1]))


def blocks(pair, block_low):
    return tuple(jnp.concatenate([part] * (block_low.shape[0] // HD), axis=0) * block_low for part in pair)


def packed_eye(n):
    row = lax.broadcasted_iota(jnp.int32, (HD, n), 0)
    lane = lax.broadcasted_iota(jnp.int32, (HD, n), 1)
    return jnp.where(row == (lane & (HD - 1)), 1.0, 0.0)


def spread(packed, block):
    return jnp.where(block, jnp.concatenate([packed] * (block.shape[0] // HD), axis=0), 0.0)


def conv_apply(arr, band, heads):
    slots = arr.shape[1]
    parts = []
    for h in range(heads):
        out = m2r(nt, windows(arr, h), band[h])
        parts.append(jnp.concatenate([out[HD * b : HD * (b + 1)] for b in range(slots // 128)], axis=1))
    return jnp.concatenate(parts, axis=0)


def core_forward(q, k, v, length, band, keep):
    n, slots = q.shape
    heads = n // HD
    block, live, member, inv_s, inv_l = frame(length, slots, heads)
    k_land = jnp.where(block, nt(member, k), 0.0) * inv_s
    q_land = jnp.where(block, nt(member, q), 0.0) * inv_s
    k3, q3 = split3(k_land), split3(q_land)
    x2 = m6(nt, q3, k3) * 0.125
    x2 = jnp.where(block, x2, -1e30)
    e2 = jnp.exp(x2 - jnp.max(x2, axis=1, keepdims=True))
    mid = e2 * (1.0 / jnp.sum(e2, axis=1, keepdims=True))
    cols = jnp.sum(mid, axis=0, keepdims=True)
    inv_max = 1.0 / head_lane_max(cols, heads)
    x3 = m2l(nn, q3[:2], k) * 0.125 + jnp.where(live, 0.0, -1e9)
    e3 = jnp.exp(x3 - jnp.max(x3, axis=1, keepdims=True))
    last = e3 * (1.0 / jnp.sum(e3, axis=1, keepdims=True))
    last_s = split(last)
    keep("last", last)
    x1 = (m2l(nn, k3[:2], q) * 0.125).reshape(heads, LM, slots)
    e1 = jnp.exp(x1 - jnp.max(x1, axis=1, keepdims=True))
    first = (e1 * (1.0 / jnp.sum(e1, axis=1, keepdims=True))).reshape(n, slots)
    first_s = split(first)
    keep("first", first)
    eye = packed_eye(n)
    low = jnp.where(block, 1.0, 0.0).astype(BF)
    mid_s = split(mid)
    mid_p = tuple(squeeze(part) for part in mid_s)
    p = m3(nt, mid_p, mid_s) * inv_max

    def powers(p):
        ps = split(p)
        pb = blocks(ps, low)
        p2 = times(ps, pb)
        p2s = split(p2)
        p3 = times(p2s, pb)
        return p2, p2s, p3, 0.25 * (13.0 * eye - 15.0 * p + 7.0 * p2 - p3)

    def onward(p, p2, p2s, p3):
        return 0.25 * (13.0 * p - 15.0 * p2 + 7.0 * p3 - times(p2s, blocks(p2s, low)))

    p2, p2s, p3, root = powers(p)
    keep(0, (p, p2, p3))
    p = onward(p, p2, p2s, p3)

    def sweep(step, carry):
        p, root = carry
        p2, p2s, p3, poly = powers(p)
        keep(step, (p, p2, p3, root))
        return onward(p, p2, p2s, p3), times(split(root), blocks(split(poly), low))

    p, root = lax.fori_loop(1, NEWTON - 1, sweep, (p, root))
    p2, p2s, p3, poly = powers(p)
    keep(NEWTON - 1, (p, p2, p3, root))
    root = times(split(root), blocks(split(poly), low))
    z_t = times(split(root), mid_s) * inv_max
    sum_t = jnp.where(block, m2r(nt, v, last_s), 0.0)
    y_t = m3(nn, split(sum_t), blocks(split(z_t), low))
    out = m3(nn, split(y_t), first_s)
    out = out + conv_apply(jnp.where(live, v, jnp.zeros_like(v)), band, heads)
    att = jnp.where(live, out, 0.0).astype(BF)
    return att, first, last, mid, z_t, sum_t, y_t, root, k_land, q_land


def core_backward(g, q, k, v, parts, first, last, mid, z_t, sum_t, y_t, root, kept, k_land, q_land, band, before_newton):
    n, slots = q.shape
    heads = n // HD
    block, live, member, inv_s, inv_l = parts
    g = jnp.where(live, g, jnp.zeros_like(g))
    first_s, last_s = split(first), split(last)
    mid_s = split(mid)
    cols = jnp.sum(mid, axis=0, keepdims=True)
    top = head_lane_max(cols, heads)
    inv_max = 1.0 / top
    low = jnp.where(block, 1.0, 0.0).astype(BF)
    zt_s = blocks(split(z_t), low)
    y = y_t.T
    dfirst = m2l(nn, split(y), g)
    dy_t = jnp.where(block, m2r(nt, g, first_s), 0.0)
    dy = dy_t.T
    dy_s, dyt_s, st_s = split(dy), split(dy_t), split(sum_t)
    s_s = split(sum_t.T)
    dz = m3(nn, dy_s, st_s)
    dz_t = m3(nn, s_s, dyt_s)
    ds_t = m3(nt, dyt_s, zt_s)
    ds = ds_t.T
    dlast = m2l(nn, split(ds), v)
    dv = m3(nn, split(ds_t), last_s)
    dv = dv + jnp.where(live, conv_apply(g, band, heads), 0.0)
    dx3 = last * (dlast - jnp.sum(dlast * last, axis=1, keepdims=True)) * 0.125
    f3 = first.reshape(heads, LM, slots)
    d3 = dfirst.reshape(heads, LM, slots)
    dx1 = (f3 * (d3 - jnp.sum(d3 * f3, axis=1, keepdims=True)) * 0.125).reshape(n, slots)
    before_newton()
    eye = packed_eye(n)
    mid_p = tuple(squeeze(part) for part in mid_s)
    dmid = times(split(root), split(dz_t)) * inv_max
    droot = times(mid_p, split(dz)) * inv_max
    dtop = -jnp.sum(squeeze(dz_t) * z_t, axis=0, keepdims=True)

    def unsweep(step, dp, droot):
        p, p2, p3, before = kept(step)
        ps, p2s = split(p), split(p2)
        pb = blocks(ps, low)
        if before is None:
            dpoly = 0.25 * droot
        else:
            poly = 0.25 * (13.0 * eye - 15.0 * p + 7.0 * p2 - p3)
            droot_s = split(droot)
            dpoly = 0.25 * times(split(before), blocks(droot_s, low))
            droot = times(droot_s, blocks(split(poly), low))
        d1, d2, d3 = -15.0 * dpoly, 7.0 * dpoly, -dpoly
        if dp is not None:
            e = 0.25 * dp
            es = split(e)
            d1 = d1 + 13.0 * e
            d2 = d2 - 15.0 * e - (times(es, blocks(p2s, low)) + times(p2s, blocks(es, low)))
            d3 = d3 + 7.0 * e
        d3s = split(d3)
        d2 = d2 + times(d3s, pb)
        d1 = d1 + times(p2s, blocks(d3s, low))
        d2s = split(d2)
        return d1 + (times(d2s, pb) + times(ps, blocks(d2s, low))), droot

    dp, droot = unsweep(NEWTON - 1, None, droot)
    dp, droot = lax.fori_loop(1, NEWTON - 1, lambda i, c: unsweep(NEWTON - 1 - i, *c), (dp, droot))
    dp, droot = unsweep(0, dp, droot)
    both = spread(dp, block)
    dmid = dmid + times(split(squeeze(both + both.T)), mid_s) * inv_max
    dtop = dtop - jnp.sum(dp * kept(0)[0], axis=0, keepdims=True)
    dtop = head_lane_sum(dtop, heads) * inv_max
    hit = jnp.where(cols == top, 1.0, 0.0)
    dmid = spread(dmid + dtop * hit / head_lane_sum(hit, heads), block)
    dx2 = mid * (dmid - jnp.sum(dmid * mid, axis=1, keepdims=True)) * 0.125
    dx2_s = split(dx2)
    dx1_s, dx3_s = split(dx1), split(dx3)
    kt_s, qt_s = split(k_land.T), split(q_land.T)
    dql_t = (jnp.where(block, m2r(nt, k, dx3_s), 0.0) + m3(nt, kt_s, dx2_s)) * inv_l
    dkl_t = (jnp.where(block, m2r(nt, q, dx1_s), 0.0) + m3(nn, qt_s, dx2_s)) * inv_l
    dq = m3(nn, kt_s, dx1_s) + m2l(nn, split(dql_t), member)
    dk = m3(nn, qt_s, dx3_s) + m2l(nn, split(dkl_t), member)
    corr = []
    vm = jnp.where(live, v, jnp.zeros_like(v))
    ri = lax.broadcasted_iota(jnp.int32, (128, 128), 0)
    ci = lax.broadcasted_iota(jnp.int32, (128, 128), 1)
    flip = jnp.where(ri + ci == 127, 1.0, 0.0).astype(BF)
    for h in range(heads):
        rows = g[HD * h : HD * (h + 1)]
        stack = jnp.concatenate([rows[:, 128 * b : 128 * b + 128] for b in range(slots // 128)], axis=0)
        near = tn(nn(stack, flip).astype(BF), windows(vm, h))
        near = pltpu.roll(near, 0, axis=1, stride=1, stride_axis=0)
        corr.append(jnp.sum(near, axis=0, keepdims=True))
    return dq, dk, dv, corr


N_MATS = 7
VEC_TAPS = 9
N_KEPT = 4 * NEWTON
VM = pl.BlockSpec(memory_space=pltpu.VMEM)
SM = pl.BlockSpec(memory_space=pltpu.SMEM)
HB = pl.BlockSpec(memory_space=pltpu.HBM)


def struct(shape, kind):
    return jax.ShapeDtypeStruct(shape, kind)


def cost(micros):
    return pl.CostEstimate(flops=int(micros * 1.0e9), bytes_accessed=1 << 20, transcendentals=0)


def start(pairs, sems, first=0):
    copies = [pltpu.make_async_copy(src, dst, sems.at[first + i]) for i, (src, dst) in enumerate(pairs)]
    for copy in copies:
        copy.start()
    return copies


def finish(copies):
    for copy in copies:
        copy.wait()


def forward_kernel(lengths, taps, x0, x1, x2, x3, wt, att0, att1, att2, att3, proj_h, first_h, last_h, mats_h, kept_h, att_h,
                   att_s, proj, first_s, last_s, mats, kept_s, sems):
    nar, length = lax.axis_index("narrow"), lengths[0]
    rows = x0.shape[0]
    offs = [pl.multiple_of((nar ^ r) * rows, rows) for r in range(4)]
    for r, x in enumerate((x0, x1, x2, x3)):
        proj[:, pl.ds(offs[r], rows)] = nt(wt[...], x[...]).astype(BF)
    copies = start([(proj, proj_h)], sems)
    n = wt.shape[0] // 3
    q, k, v = proj[0:n, :], proj[n:2 * n, :], proj[2 * n:3 * n, :]

    def saved(step):
        return pltpu.make_async_copy(kept_s.at[pl.ds(4 * step, 4)], kept_h.at[pl.ds(4 * step, 4)], sems.at[4 + step])

    def keep(step, arrays):
        if step == "first":
            first_s[...] = arrays
            copies.extend(start([(first_s, first_h)], sems, 1))
        elif step == "last":
            last_s[...] = arrays
            copies.extend(start([(last_s, last_h)], sems, 2))
        else:
            for i, array in enumerate(arrays):
                kept_s[4 * step + i] = array
            saved(step).start()

    kept_s[3] = jnp.zeros(kept_s.shape[1:], F32)
    att, first, last, mid, z_t, sum_t, y_t, root, k_land, q_land = core_forward(
        q, k, v, length, bands(taps, n // HD, False), keep)
    for i, m in enumerate((mid, z_t, sum_t, y_t, root, k_land, q_land)):
        mats[i] = m if i in (1, 4) else squeeze(m)
    copies += start([(mats, mats_h)], sems, 3)
    att_s[...] = att
    copies += start([(att_s, att_h)], sems, 4 + NEWTON)
    for r, out in enumerate((att0, att1, att2, att3)):
        out[...] = att_s[:, pl.ds(offs[r], rows)]
    for step in range(NEWTON):
        saved(step).wait()
    finish(copies)


def forward_call(lengths, taps, xs, wt):
    rows, width = xs[0].shape
    n = wt.shape[0] // 3
    slots = 4 * rows
    saved = [((3 * n, slots), BF), ((n, slots), F32), ((n, slots), F32), ((N_MATS, HD, n), F32), ((N_KEPT, HD, n), F32)]
    attended = struct((n, slots), BF)
    return pl.pallas_call(
        forward_kernel,
        in_specs=[SM] * 2 + [VM] * 5,
        out_specs=[VM] * 4 + [HB] * 6,
        out_shape=[struct((n, rows), BF)] * 4 + [struct(*s) for s in saved] + [attended],
        scratch_shapes=[pltpu.VMEM((n, slots), BF)]
        + [pltpu.VMEM(*s) for s in saved]
        + [pltpu.SemaphoreType.DMA((5 + NEWTON,))],
        compiler_params=pltpu.CompilerParams(vmem_limit_bytes=60 << 20),
        cost_estimate=cost(10),
        name="core_forward",
    )(lengths, taps, *xs, wt)


def backward_kernel(slotted, lengths, taps, a0, a1, a2, a3, b0, b1, b2, b3, wo, proj_h, first_h, last_h, mats_h, kept_h, att_h, x0, x1, x2, x3, wt,
                    dx0, dx13, dx2, *rest):
    outs, (g_s, dp_s, tot_s, vec_s, out_s, proj, first_s, last_s, mats, kept_s, att_s, sems) = rest[:-12], rest[-12:]
    nar, wide, length = lax.axis_index("narrow"), lax.axis_index("wide"), lengths[0]
    copies = start([(mats_h, mats), (first_h, first_s), (proj_h, proj), (last_h, last_s), (kept_h, kept_s), (att_h, att_s)], sems)
    rows = x0.shape[0]
    offs = [pl.multiple_of((nar ^ r) * rows, rows) for r in range(4)]
    half = rows // 2
    for r, (a, b) in enumerate(((a0, b0), (a1, b1), (a2, b2), (a3, b3))):
        g_s[:, pl.ds(offs[r], half)] = nt(wo[...], a[...]).astype(BF)
        g_s[:, pl.ds(pl.multiple_of(offs[r] + half, half), half)] = nt(wo[...], b[0:half, :]).astype(BF)
    vectors = sum(b[half:, :].astype(F32) for b in (b0, b1, b2, b3))
    n = wt.shape[0] // 3
    heads = n // HD
    band = bands(taps, heads, True)
    parts = frame(length, 4 * rows, heads)
    block = parts[0]
    finish(copies[:4])
    q, k, v = proj[0:n, :], proj[n:2 * n, :], proj[2 * n:3 * n, :]
    mid, z_t, sum_t, y_t, root, k_land, q_land = [mats[i] if i in (1, 4) else spread(mats[i], block) for i in range(N_MATS)]

    def kept(step):
        first = isinstance(step, int) and step == 0
        got = [kept_s[4 * step + i] for i in range(3 if first else 4)]
        return got + [None] if first else got

    dq, dk, dv, corr = core_backward(g_s[...], q, k, v, parts, first_s[...], last_s[...], mid, z_t, sum_t, y_t, root,
                                     kept, k_land, q_land, band, copies[4].wait)
    dp_s[0:n, :] = dq.astype(BF)
    dp_s[n:2 * n, :] = dk.astype(BF)
    dp_s[2 * n:3 * n, :] = dv.astype(BF)
    total = None
    for r, x in enumerate((x0, x1, x2, x3)):
        block = dp_s[:, pl.ds(offs[r], rows)]
        back = tn(block, wt[...]).astype(BF)
        if r & 1:
            dx13[r >> 1] = back
        else:
            (dx2 if r else dx0)[...] = back
        term = nn(block, x[...])
        total = term if total is None else total + term
    copies[5].wait()
    output = None
    for r, (a, b) in enumerate(((a0, b0), (a1, b1), (a2, b2), (a3, b3))):
        term = nn(att_s[:, pl.ds(offs[r], half)], a[...])
        term = term + nn(att_s[:, pl.ds(pl.multiple_of(offs[r] + half, half), half)], b[0:half, :])
        output = term if output is None else output + term
    vec_s[...] = jnp.zeros_like(vec_s)
    lines = [vectors[i : i + 1, :] for i in range(VEC_TAPS)]
    lines += corr
    if not slotted:
        in_grad, out_grad, vec_o = outs
        in_grad[...] = total.astype(BF)
        out_grad[...] = output.astype(BF)
        for i, line in enumerate(lines):
            vec_o[i : i + 1, 0 : line.shape[1]] = line
        return
    tot_s[...] = total
    out_s[...] = output
    for i, line in enumerate(lines):
        vec_s[i >> 1, (i & 1) : (i & 1) + 1, 0 : line.shape[1]] = line
    wides = 8
    part, more = total.shape[0] // wides, output.shape[0] // wides
    for s in range(wides):
        w = s ^ wide
        slot = outs[s & 3].at[s >> 2]
        slot[0:part, :] = tot_s[pl.ds(pl.multiple_of(w * part, 8), part), :].astype(BF)
        slot[part : part + 8, :] = vec_s[w].astype(BF)
        slot[part + 8 : part + 8 + more, :] = out_s[pl.ds(pl.multiple_of(w * more, 8), more), :].astype(BF)


def backward_call(lengths, taps, attn, wo, saved, xs, wt, n_wide, slotted):
    rows, width = xs[0].shape
    n = wt.shape[0] // 3
    slots = 4 * rows
    sums = (
        [struct((2, 4 * n // n_wide + 8, width), BF)] * 4
        if slotted
        else [struct((3 * n, width), BF), struct((n, width), BF), struct((16, width), F32)]
    )
    return pl.pallas_call(
        functools.partial(backward_kernel, slotted),
        in_specs=[SM] * 2 + [VM] * 9 + [HB] * 6 + [VM] * 5,
        out_specs=[VM] * (3 + len(sums)),
        out_shape=[struct((rows, width), BF), struct((2, rows, width), BF), struct((rows, width), BF)] + sums,
        scratch_shapes=[
            pltpu.VMEM((n, slots), BF),
            pltpu.VMEM((3 * n, slots), BF),
            pltpu.VMEM((3 * n, width), F32),
            pltpu.VMEM((8, 8, width), F32),
            pltpu.VMEM((n, width), F32),
        ]
        + [pltpu.VMEM(s.shape, s.dtype) for s in saved]
        + [pltpu.SemaphoreType.DMA((6,))],
        compiler_params=pltpu.CompilerParams(vmem_limit_bytes=60 << 20),
        cost_estimate=cost(19),
        name="core_backward",
    )(lengths, taps, *attn, wo, *saved, *xs, wt)


EPS = 1e-05
U = [4, 8, 4]


def norm_stats(resid):
    center = jnp.mean(resid, axis=1, keepdims=True)
    centered = resid - center
    inverse = lax.rsqrt(jnp.mean(centered * centered, axis=1, keepdims=True) + EPS)
    return centered * inverse, inverse


def norm_pull(grad, normalized, inverse, gain):
    scaled = grad * gain
    return inverse * (
        scaled
        - jnp.mean(scaled, axis=1, keepdims=True)
        - normalized * jnp.mean(scaled * normalized, axis=1, keepdims=True)
    )


def total(rows):
    return jnp.sum(rows, axis=0, keepdims=True)


def ffn_kernel(slotted, x_h, a0, a1, a2, a3, w0, w1, w2, w3, g1, b1, ub, db, g2, b2, cot_h, up_h, down_h,
               mixed, res1, attn_a, attn_b, *rest):
    outs, (up, down, hid_s, slope, pre_s, hold_d, hold_u, bias_s, x, cot, sems) = rest[:-11], rest[-11:]
    chunks = 4
    ff = up.shape[1]
    size = ff // chunks
    nar, wide = lax.axis_index("narrow"), lax.axis_index("wide")

    def part(c):
        return pl.ds(pl.multiple_of(c * size, size), size)

    def up_copy(c):
        return pltpu.make_async_copy(up_h.at[:, part(c)], up.at[:, part(c)], sems.at[2 * c])

    def down_copy(c):
        return pltpu.make_async_copy(down_h.at[part(c), :], down.at[part(c), :], sems.at[2 * c + 1])

    own = start([(x_h, x)], sems, 2 * chunks)
    for c in range(chunks):
        up_copy(c).start()
        down_copy(c).start()
    own += start([(cot_h, cot)], sems, 2 * chunks + 1)
    first_sem = 2 * chunks + 2
    if slotted:
        down_to, up_to = outs[:4], outs[4:]
        n_wide, rows = 8, down_to[0].shape[3]
        group, many = 4 * rows, 4
    else:
        down_to, up_to = outs[:1], outs[1:]
        group, many = size, 1
    groups = ff // group

    def outer(left, right, hold, w, sem, targets):
        at = pl.multiple_of(w * group, group)
        hold[pl.ds(at, group), :] = tn(left[:, pl.ds(at, group)], right).astype(BF)
        if not slotted:
            pltpu.make_async_copy(hold.at[pl.ds(at, group), :], targets[0].at[pl.ds(at, group), :], sems.at[sem + w]).start()
        for n in range(4 if slotted else 0):
            block = hold.at[pl.ds(pl.multiple_of(at + n * rows, rows), rows), :]
            slot_n, slot_w = n ^ nar, w ^ wide
            core, y, x, z0, z1 = slot_n & 1, slot_n >> 1, slot_w & 1, (slot_w >> 1) & 1, slot_w >> 2
            lead, second = (x, y) if targets is down_to else (y, x)
            for i in range(4):

                @pl.when(2 * core + lead == i)
                def _():
                    pltpu.make_async_copy(
                        block, targets[i].at[second, z0, z1, pl.ds(0, rows)], sems.at[sem + 4 * w + n]
                    ).start()

    def outer_wait(hold, sem, targets):
        def one(i, carry):
            height = group // many
            block = hold.at[pl.ds(pl.multiple_of(i * height, height), height), :]
            target = targets[0].at[0, 0, 0, pl.ds(0, rows)] if slotted else targets[0].at[pl.ds(0, group), :]
            pltpu.make_async_copy(block, target, sems.at[sem + i]).wait()
            return carry

        lax.fori_loop(0, groups * many, one, 0)

    attention = tn(a0[...], w0[...]) + tn(a1[...], w1[...]) + tn(a2[...], w2[...]) + tn(a3[...], w3[...])
    own[0].wait()
    n1, inv1 = norm_stats(x[...].astype(F32) + attention)
    normed = n1 * g1[...] + b1[...]
    ffn_in = normed.astype(BF)

    def ahead(c, out):
        cut = part(c)
        up_copy(c).wait()
        pre = nn(ffn_in, up[:, cut]) + ub[:, cut]
        below = 0.5 * (1.0 + lax.erf(pre * 0.7071067811865476))
        hid = (pre * below).astype(BF)
        slope[:, cut] = below + pre * (0.3989422804014327 * jnp.exp(-0.5 * (pre * pre)))
        hid_s[:, cut] = hid
        down_copy(c).wait()
        return out + nn(hid, down[cut, :])

    out = lax.fori_loop(0, chunks, ahead, jnp.zeros(x.shape, F32), unroll=U[0])
    n2, inv2 = norm_stats(normed + (out + db[...]))
    mixed[...] = (n2 * g2[...] + b2[...]).astype(BF)
    own[1].wait()
    cotangent = cot[...].astype(F32)
    res2 = norm_pull(cotangent, n2, inv2, g2[...])
    low = res2.astype(BF)

    def down_outer(w, carry):
        outer(hid_s, low, hold_d, w, first_sem, down_to)
        return carry

    lax.fori_loop(0, groups, down_outer, 0, unroll=U[1])
    second_sem = first_sem + groups * many

    def behind(c, grad):
        cut = part(c)
        pre = nt(low, down[cut, :]) * slope[:, cut]
        bias_s[:, cut] = total(pre)
        pre = pre.astype(BF)
        pre_s[:, cut] = pre
        for i in range(groups // chunks):
            outer(pre_s, ffn_in, hold_u, c * (groups // chunks) + i, second_sem, up_to)
        return grad + nt(pre, up[:, cut])

    grad = lax.fori_loop(0, chunks, behind, res2, unroll=U[2])
    back = norm_pull(grad, n1, inv1, g1[...])
    res1[...] = back
    attn = back.astype(BF)
    half = x.shape[0] // 2
    attn_a[...] = attn[:half]
    attn_b[0:half, :] = attn[half:]
    vectors = [total(grad * n1), total(grad), total(res2), total(cotangent * n2), total(cotangent)]
    width = x.shape[1]
    vectors += [bias_s[:, width * j : width * (j + 1)] for j in range(ff // width)]
    vectors.append(jnp.zeros((attn_b.shape[0] - half - len(vectors), width), F32))
    attn_b[half:, :] = jnp.concatenate(vectors, axis=0).astype(BF)
    outer_wait(hold_d, first_sem, down_to)
    outer_wait(hold_u, second_sem, up_to)


def ffn_call(x, att, wo, g1, b1, ub, db, g2, b2, cot, up, down, n_wide, slotted):
    rows, width = x.shape
    ff = up.shape[1]
    part = ff // (4 * n_wide)
    if slotted:
        sums = [struct((2, 2, 2, part, width), BF)] * 8
    else:
        sums = [struct((ff, width), BF)] * 2
    return pl.pallas_call(
        functools.partial(ffn_kernel, slotted),
        in_specs=[HB] + [VM] * 14 + [HB] * 3,
        out_specs=[VM] * 4 + [HB] * len(sums),
        out_shape=[struct((rows, width), BF), struct((rows, width), F32)]
        + [struct((rows // 2 + more, width), BF) for more in (0, 16)]
        + sums,
        scratch_shapes=[
            pltpu.VMEM((width, ff), BF),
            pltpu.VMEM((ff, width), BF),
            pltpu.VMEM((rows, ff), BF),
            pltpu.VMEM((rows, ff), F32),
            pltpu.VMEM((rows, ff), BF),
            pltpu.VMEM((ff, width), BF),
            pltpu.VMEM((ff, width), BF),
            pltpu.VMEM((1, ff), F32),
            pltpu.VMEM((rows, width), BF),
            pltpu.VMEM((rows, width), BF),
            pltpu.SemaphoreType.DMA((10 + 64,)),
        ],
        compiler_params=pltpu.CompilerParams(vmem_limit_bytes=60 << 20),
        cost_estimate=cost(20),
        name="ffn",
    )(x, *att, *wo, g1, b1, ub, db, g2, b2, cot, up, down)


def to_slots(me, whole, n_wide):
    count = 4 * n_wide
    slot = jnp.arange(count).reshape(n_wide, 2, 2).transpose(2, 1, 0)
    picked = whole.reshape(count, -1, whole.shape[-1])[slot ^ me]
    return picked[0], picked[1]


def finish_kernel(*refs):
    pools, (input_o, output_o, taps_o, bias_o, *vec_o, vec_s) = refs[:4], refs[4:]
    nar, wide = lax.axis_index("narrow"), lax.axis_index("wide")
    local, size = output_o.shape[0], bias_o.shape[0]
    part, more = 3 * local // 8, local // 8
    for s in range(8):
        pool, w = pools[s & 3].at[s >> 2], s ^ wide
        input_o[pl.ds(pl.multiple_of(w * part, 8), part), :] = pool[0:part, :].astype(F32)
        vec_s[w] = pool[part : part + 8, :].astype(F32)
        output_o[pl.ds(pl.multiple_of(w * more, 8), more), :] = pool[part + 8 : part + 8 + more, :].astype(F32)

    def line(i):
        return vec_s[i >> 1, (i & 1) : (i & 1) + 1, :]

    for i, out in enumerate(vec_o):
        out[...] = line(i)[0]
    for h in range(taps_o.shape[0]):
        taps_o[h : h + 1, :] = line(VEC_TAPS + h)[:, 239 : 239 + KW]
    bias = jnp.zeros((1, size), F32)
    each = vec_s.shape[2] // size
    for j in range(32):
        piece = line(5 + j // each)[:, size * (j % each) : size * (j % each + 1)]
        bias = jnp.where(4 * wide + nar == j, piece, bias)
    bias_o[...] = bias[0]


def finish_call(pools, local, heads, size):
    width = pools[0].shape[2]
    return pl.pallas_call(
        finish_kernel,
        in_specs=[VM] * 4,
        out_specs=[VM] * 9,
        out_shape=[
            struct((3 * local, width), F32),
            struct((local, width), F32),
            struct((heads, KW), F32),
            struct((size,), F32),
        ]
        + [struct((width,), F32)] * 5,
        scratch_shapes=[pltpu.VMEM((8, 8, width), F32)],
        compiler_params=pltpu.CompilerParams(vmem_limit_bytes=60 << 20),
        cost_estimate=cost(3),
        name="finish",
    )(*pools)


def build(mesh):
    n_wide, n_narrow = mesh.shape["wide"], mesh.shape["narrow"]
    count = n_wide * n_narrow
    wide_bits = []
    bit = n_narrow
    while bit < count:
        wide_bits.append(bit)
        bit *= 2

    def swap(block, mask):
        return lax.ppermute(block, AXES, [(i, i ^ mask) for i in range(count)])

    def after(value, *earlier):
        return lax.optimization_barrier((value, earlier))[0]

    def gather_relative(block):
        far = swap(block, 2)
        near = swap(block, 1)
        return [block, near, far, swap(far, 1)]

    def exchange_relative(blocks):
        return [blocks[r] if r == 0 else swap(blocks[r], r) for r in range(n_narrow)]

    class Halving:
        def __init__(self, parts, masks):
            shape = [2] * len(masks) + list(parts[0].shape[-2:])
            self.masks, self.parts = list(masks), [part.reshape(shape) for part in parts]

        def split(self, mask):
            axis = self.masks.index(mask)
            self.masks.pop(axis)
            sides = [[lax.index_in_dim(part, i, axis, keepdims=False) for part in self.parts] for i in range(2)]
            self.parts = sides[0]
            self.sent = sum(part.astype(F32) for part in sides[1]).astype(BF)
            self.mask = mask

        def send(self):
            self.parts = self.parts + [swap(self.sent, self.mask)]

        def step(self, mask):
            self.split(mask)
            self.send()

        def total(self):
            return sum(part.astype(F32) for part in self.parts)

    def gather_order(masks):
        order = [0]
        for mask in masks:
            order = order + [w ^ (mask // n_narrow) for w in order]
        return order

    def double(block, mask):
        return jnp.concatenate([block, swap(block, mask)], axis=0)

    def on_device(
        tokens,
        lengths,
        input_weights,
        output_weight,
        conv_taps,
        first_gain,
        first_bias,
        up_weight,
        up_bias,
        down_weight,
        down_bias,
        second_gain,
        second_bias,
        cotangent,
    ):
        me = lax.axis_index(AXES)
        rows, width = tokens.shape
        local_width = input_weights.shape[2]
        heads = local_width // HD
        wide = lax.axis_index("wide")
        weights_t = jnp.swapaxes(input_weights, 1, 2).reshape(3 * local_width, width)
        token_blocks = gather_relative(tokens)
        weight = after(output_weight, token_blocks[2])
        far, near = swap(weight, 2), swap(weight, 1)
        *att, s0, s1, s2, s3, s4, s5 = forward_call(lengths, conv_taps, token_blocks, weights_t)
        own_att = exchange_relative(att)
        out_rel = [output_weight, near, far, swap(after(far, att[0]), 1)]
        ff_rows = up_weight.shape[1] // count
        slotted = ff_rows % 32 == 0 and n_wide == 8

        def row(vector):
            return vector[None, :]

        mixed, res1, *rest = ffn_call(
            tokens, own_att, out_rel, row(first_gain), row(first_bias), row(up_bias), row(down_bias),
            row(second_gain), row(second_bias), cotangent, up_weight, down_weight, n_wide, slotted,
        )
        attn_a, attn_b, *rest = rest
        attn = gather_relative(attn_a) + gather_relative(attn_b)
        first, *more = wide_bits
        if slotted:

            def begin(parts, lead):
                return (parts[1].astype(F32) + swap(parts[3], 1).astype(F32)).astype(BF), parts, lead

            def go_on(begun, masks):
                sent, parts, lead = begun
                return Halving([parts[0], swap(parts[2], 1), swap(sent, lead)], masks)

            down, up = begin(rest[:4], first), begin(rest[4:], 2)
            up = (after(up[0], attn[6]),) + up[1:]
            attn = list(after(tuple(attn), down[0], up[0]))
            down, up = go_on(down, [2] + more), go_on(up, wide_bits)
        else:
            masks = [2] + wide_bits[::-1]
            same, other = to_slots(me, rest[0], n_wide)
            down = Halving([same, swap(other, 1)], masks)
            down.step(first)
            same, other = to_slots(me, rest[1], n_wide)
            up = Halving([same, swap(other, 1)], masks)
            up.step(2)
        back0, back13, back2, *sums = backward_call(
            lengths, conv_taps, attn, output_weight, [s0, s1, s2, s3, s4, s5], token_blocks, weights_t, n_wide, slotted
        )
        per_wide = -(-(VEC_TAPS + heads) // n_wide)
        near = swap(back13, 1)
        far = (back2.astype(F32) + near[1].astype(F32)).astype(BF)

        def finish_tokens(far, back0):
            return (res1 + back0.astype(F32) + near[0].astype(F32) + far.astype(F32)).astype(BF)

        if slotted:
            second, third = more

            def total(*blocks):
                return sum(block.astype(F32) for block in blocks)

            near_kept, near_sent, far_kept, far_sent = after(tuple(sums), down.parts[-1], up.parts[-1])
            far_came, near_came = swap(far_sent, first), swap(near_sent, first)
            down.parts, up.parts = after((down.parts, up.parts), far_came)
            far_sum = total(far_kept, far_came).astype(BF)
            z0_came = swap(far_sum, second)
            down.split(2)
            down.sent = after(down.sent, far_sum)
            down.send()
            far = swap(after(far, far_sum), 2)
            up.split(first)
            up.sent = after(up.sent, near_came)
            up.send()
            z1_sum = total(near_kept[1], near_came[1], z0_came[1]).astype(BF)
            own = total(near_kept[0], near_came[0], z0_came[0], swap(z1_sum, third)).astype(BF)
            pair = jnp.stack([own, swap(own, third)])
            z0_pair = swap(pair, second)
            own_x, z0_x = swap(pair, first), swap(z0_pair, first)
            back0 = after(back0, z0_pair)
            tokens_grad = finish_tokens(far, back0)

            down.split(second)
            down.sent = after(down.sent, z1_sum)
            down.send()
            up.split(second)
            up.sent = after(up.sent, own)
            up.send()
            down.step(third)
            up.step(third)
            z0_x = after(z0_x, up.sent)
            input_out, output_out, taps_out, up_bias_out, *vec = finish_call(
                [pair, own_x, z0_pair, z0_x], local_width, heads, ff_rows
            )
            input_out = jnp.swapaxes(input_out.reshape(3, local_width, width), 1, 2)
        else:
            tokens_grad = finish_tokens(swap(far, 2), back0)
            vec = sums[2][: VEC_TAPS + heads]
            vec = jnp.pad(vec, ((0, per_wide * n_wide - vec.shape[0]), (0, 0)))
            pool = [block.astype(BF).reshape(n_wide, -1, width) for block in (sums[0], sums[1], vec)]
            pool = Halving([jnp.concatenate(pool, axis=1)[jnp.arange(n_wide) ^ wide]], wide_bits[::-1])
            for mask in wide_bits:
                pool.step(mask)
            pool = pool.total().astype(BF)[None]
            for mask in wide_bits[::-1]:
                pool = double(pool, mask)
            down.step(2)
            up.step(first)
            for mask in more:
                down.step(mask)
                up.step(mask)
            order = jnp.argsort(jnp.array(gather_order(wide_bits[::-1])))[jnp.arange(n_wide) ^ wide]
            pool = pool[order].astype(F32)
            part = local_width // n_wide
            input_out = pool[:, : 3 * part].reshape(3, local_width, width).transpose(0, 2, 1)
            output_out = pool[:, 3 * part : 4 * part].reshape(local_width, width)
            vec = pool[:, 4 * part :].reshape(-1, width)
            taps_out = vec[VEC_TAPS : VEC_TAPS + heads, 239 : 239 + KW]
            up_bias_out = lax.dynamic_slice_in_dim(vec[5:VEC_TAPS].reshape(-1), me * ff_rows, ff_rows)
        down_out = down.total()
        up_out = up.total().T
        return (
            mixed,
            tokens_grad,
            input_out,
            output_out,
            taps_out,
            vec[0],
            vec[1],
            up_out,
            up_bias_out,
            down_out,
            vec[2],
            vec[3],
            vec[4],
        )

    return on_device


def solution(mesh):
    spread = P(AXES, None)
    placed = (
        spread,
        P("wide"),
        P(None, None, "narrow"),
        P("narrow", None),
        P("narrow", None),
        P(),
        P(),
        P(),
        P(),
        P(),
        P(),
        P(),
        P(),
        spread,
    )
    results = (
        spread,
        spread,
        P(None, None, "narrow"),
        P("narrow", None),
        P("narrow", None),
        P(),
        P(),
        P(None, AXES),
        P(AXES),
        spread,
        P(),
        P(),
        P(),
    )
    return jax.shard_map(
        build(mesh), mesh=mesh, in_specs=placed, out_specs=results, check_vma=False
    )
```

```python
import functools
import jax
import jax.numpy as jnp
from jax import lax
from jax.experimental import pallas as pl
from jax.experimental.pallas import tpu as pltpu
from jax.sharding import PartitionSpec as P

BF = jnp.bfloat16
F32 = jnp.float32
HD = 64
LM = 64
KW = 33
NEWTON = 6
AXES = ("wide", "narrow")


def dot(a, b, ca, cb):
    return lax.dot_general(a, b, (((ca,), (cb,)), ((), ())), preferred_element_type=F32)

def nn(a, b): return dot(a, b, 1, 0)
def nt(a, b): return dot(a, b, 1, 1)
def tn(a, b): return dot(a, b, 0, 0)

def split(a):
    hi = a.astype(BF)
    return hi, (a - hi.astype(F32)).astype(BF)

def split3(a):
    hi = a.astype(BF)
    rest = a - hi.astype(F32)
    mid = rest.astype(BF)
    return hi, mid, (rest - mid.astype(F32)).astype(BF)

def m3(op, a, b):
    return op(a[0], b[0]) + (op(a[1], b[0]) + op(a[0], b[1]))

def m6(op, a, b):
    return op(a[0], b[0]) + ((op(a[1], b[0]) + op(a[0], b[1])) + (op(a[1], b[1]) + (op(a[2], b[0]) + op(a[0], b[2]))))

def m2l(op, a, b):
    return op(a[0], b) + op(a[1], b)

def m2r(op, a, b):
    return op(a, b[0]) + op(a, b[1])


def frame(length, slots, heads):
    n = heads * LM
    row = lax.broadcasted_iota(jnp.int32, (n, n), 0)
    col = lax.broadcasted_iota(jnp.int32, (n, n), 1)
    block = (row >> 6) == (col >> 6)
    place = lax.broadcasted_iota(jnp.int32, (1, slots), 1)
    live = place < length
    mark = lax.broadcasted_iota(jnp.int32, (n, 1), 0) & (LM - 1)
    begin = (mark * length) >> 6
    end = ((mark + 1) * length) >> 6
    member = jnp.where((place >= begin) & (place < end), 1.0, 0.0).astype(BF)
    mark_l = lax.broadcasted_iota(jnp.int32, (1, n), 1) & (LM - 1)
    count_l = ((((mark_l + 1) * length) >> 6) - ((mark_l * length) >> 6)).astype(F32)
    count_s = (end - begin).astype(F32)
    return block, live, member, 1.0 / count_s, 1.0 / count_l


def head_lane_max(row, heads):
    lane = lax.broadcasted_iota(jnp.int32, row.shape, 1) >> 6
    out = jnp.zeros_like(row)
    for h in range(heads):
        top = jnp.max(jnp.where(lane == h, row, -1.0), axis=1, keepdims=True)
        out = jnp.where(lane == h, top, out)
    return out


def head_lane_sum(row, heads):
    lane = lax.broadcasted_iota(jnp.int32, row.shape, 1) >> 6
    out = jnp.zeros_like(row)
    for h in range(heads):
        total = jnp.sum(jnp.where(lane == h, row, 0.0), axis=1, keepdims=True)
        out = jnp.where(lane == h, total, out)
    return out


def windows(arr, h):
    slots = arr.shape[1]
    rows = arr[HD * h : HD * (h + 1)]
    zero = jnp.zeros((HD, 128), arr.dtype)
    wide = jnp.concatenate([zero, rows, zero], axis=1)
    return jnp.concatenate([wide[:, 128 * b : 128 * b + 384] for b in range(slots // 128)], axis=0)


def bands(taps, heads, turned):
    lane = lax.broadcasted_iota(jnp.int32, (1, 384), 1) - 112
    out = []
    for h in range(heads):
        base = jnp.zeros((1, 384), F32)
        for w in range(KW):
            base = jnp.where(lane == (KW - 1 - w if turned else w), taps[h, w], base)
        out.append(split(pltpu.roll(jnp.broadcast_to(base, (128, 384)), 0, axis=1, stride=1, stride_axis=0)))
    return out


def squeeze(matrix):
    return sum(matrix[HD * h : HD * (h + 1)] for h in range(matrix.shape[0] // HD))


def times(left, right):
    both = nn(jnp.concatenate([left[0], left[1]], axis=0), right[0])
    return both[:HD] + (both[HD:] + nn(left[0], right[1]))


def blocks(pair, block_low):
    return tuple(jnp.concatenate([part] * (block_low.shape[0] // HD), axis=0) * block_low for part in pair)


def packed_eye(n):
    row = lax.broadcasted_iota(jnp.int32, (HD, n), 0)
    lane = lax.broadcasted_iota(jnp.int32, (HD, n), 1)
    return jnp.where(row == (lane & (HD - 1)), 1.0, 0.0)


def spread(packed, block):
    return jnp.where(block, jnp.concatenate([packed] * (block.shape[0] // HD), axis=0), 0.0)


def conv_apply(arr, band, heads):
    slots = arr.shape[1]
    parts = []
    for h in range(heads):
        out = m2r(nt, windows(arr, h), band[h])
        parts.append(jnp.concatenate([out[HD * b : HD * (b + 1)] for b in range(slots // 128)], axis=1))
    return jnp.concatenate(parts, axis=0)


def core_forward(q, k, v, length, band, keep):
    n, slots = q.shape
    heads = n // HD
    block, live, member, inv_s, inv_l = frame(length, slots, heads)
    k_land = jnp.where(block, nt(member, k), 0.0) * inv_s
    q_land = jnp.where(block, nt(member, q), 0.0) * inv_s
    k3, q3 = split3(k_land), split3(q_land)
    x2 = m6(nt, q3, k3) * 0.125
    x2 = jnp.where(block, x2, -1e30)
    e2 = jnp.exp(x2 - jnp.max(x2, axis=1, keepdims=True))
    mid = e2 * (1.0 / jnp.sum(e2, axis=1, keepdims=True))
    cols = jnp.sum(mid, axis=0, keepdims=True)
    inv_max = 1.0 / head_lane_max(cols, heads)
    x3 = m2l(nn, q3[:2], k) * 0.125 + jnp.where(live, 0.0, -1e9)
    e3 = jnp.exp(x3 - jnp.max(x3, axis=1, keepdims=True))
    last = e3 * (1.0 / jnp.sum(e3, axis=1, keepdims=True))
    last_s = split(last)
    keep("last", last)
    x1 = (m2l(nn, k3[:2], q) * 0.125).reshape(heads, LM, slots)
    e1 = jnp.exp(x1 - jnp.max(x1, axis=1, keepdims=True))
    first = (e1 * (1.0 / jnp.sum(e1, axis=1, keepdims=True))).reshape(n, slots)
    first_s = split(first)
    keep("first", first)
    eye = packed_eye(n)
    low = jnp.where(block, 1.0, 0.0).astype(BF)
    mid_s = split(mid)
    mid_p = tuple(squeeze(part) for part in mid_s)
    p = m3(nt, mid_p, mid_s) * inv_max

    def powers(p):
        ps = split(p)
        pb = blocks(ps, low)
        p2 = times(ps, pb)
        p2s = split(p2)
        p3 = times(p2s, pb)
        return p2, p2s, p3, 0.25 * (13.0 * eye - 15.0 * p + 7.0 * p2 - p3)

    def onward(p, p2, p2s, p3):
        return 0.25 * (13.0 * p - 15.0 * p2 + 7.0 * p3 - times(p2s, blocks(p2s, low)))

    p2, p2s, p3, root = powers(p)
    keep(0, (p, p2, p3))
    p = onward(p, p2, p2s, p3)

    def sweep(step, carry):
        p, root = carry
        p2, p2s, p3, poly = powers(p)
        keep(step, (p, p2, p3, root))
        return onward(p, p2, p2s, p3), times(split(root), blocks(split(poly), low))

    p, root = lax.fori_loop(1, NEWTON - 1, sweep, (p, root))
    p2, p2s, p3, poly = powers(p)
    keep(NEWTON - 1, (p, p2, p3, root))
    root = times(split(root), blocks(split(poly), low))
    z_t = times(split(root), mid_s) * inv_max
    sum_t = jnp.where(block, m2r(nt, v, last_s), 0.0)
    y_t = m3(nn, split(sum_t), blocks(split(z_t), low))
    out = m3(nn, split(y_t), first_s)
    out = out + conv_apply(jnp.where(live, v, jnp.zeros_like(v)), band, heads)
    att = jnp.where(live, out, 0.0).astype(BF)
    return att, first, last, mid, z_t, sum_t, y_t, root, k_land, q_land


def core_backward(g, q, k, v, parts, first, last, mid, z_t, sum_t, y_t, root, kept, k_land, q_land, band, before_newton):
    n, slots = q.shape
    heads = n // HD
    block, live, member, inv_s, inv_l = parts
    g = jnp.where(live, g, jnp.zeros_like(g))
    first_s, last_s = split(first), split(last)
    mid_s = split(mid)
    cols = jnp.sum(mid, axis=0, keepdims=True)
    top = head_lane_max(cols, heads)
    inv_max = 1.0 / top
    low = jnp.where(block, 1.0, 0.0).astype(BF)
    zt_s = blocks(split(z_t), low)
    y = y_t.T
    dfirst = m2l(nn, split(y), g)
    dy_t = jnp.where(block, m2r(nt, g, first_s), 0.0)
    dy = dy_t.T
    dy_s, dyt_s, st_s = split(dy), split(dy_t), split(sum_t)
    s_s = split(sum_t.T)
    dz = m3(nn, dy_s, st_s)
    dz_t = m3(nn, s_s, dyt_s)
    ds_t = m3(nt, dyt_s, zt_s)
    ds = ds_t.T
    dlast = m2l(nn, split(ds), v)
    dv = m3(nn, split(ds_t), last_s)
    dv = dv + jnp.where(live, conv_apply(g, band, heads), 0.0)
    dx3 = last * (dlast - jnp.sum(dlast * last, axis=1, keepdims=True)) * 0.125
    f3 = first.reshape(heads, LM, slots)
    d3 = dfirst.reshape(heads, LM, slots)
    dx1 = (f3 * (d3 - jnp.sum(d3 * f3, axis=1, keepdims=True)) * 0.125).reshape(n, slots)
    before_newton()
    eye = packed_eye(n)
    mid_p = tuple(squeeze(part) for part in mid_s)
    dmid = times(split(root), split(dz_t)) * inv_max
    droot = times(mid_p, split(dz)) * inv_max
    dtop = -jnp.sum(squeeze(dz_t) * z_t, axis=0, keepdims=True)

    def unsweep(step, dp, droot):
        p, p2, p3, before = kept(step)
        ps, p2s = split(p), split(p2)
        pb = blocks(ps, low)
        if before is None:
            dpoly = 0.25 * droot
        else:
            poly = 0.25 * (13.0 * eye - 15.0 * p + 7.0 * p2 - p3)
            droot_s = split(droot)
            dpoly = 0.25 * times(split(before), blocks(droot_s, low))
            droot = times(droot_s, blocks(split(poly), low))
        d1, d2, d3 = -15.0 * dpoly, 7.0 * dpoly, -dpoly
        if dp is not None:
            e = 0.25 * dp
            es = split(e)
            d1 = d1 + 13.0 * e
            d2 = d2 - 15.0 * e - (times(es, blocks(p2s, low)) + times(p2s, blocks(es, low)))
            d3 = d3 + 7.0 * e
        d3s = split(d3)
        d2 = d2 + times(d3s, pb)
        d1 = d1 + times(p2s, blocks(d3s, low))
        d2s = split(d2)
        return d1 + (times(d2s, pb) + times(ps, blocks(d2s, low))), droot

    dp, droot = unsweep(NEWTON - 1, None, droot)
    dp, droot = lax.fori_loop(1, NEWTON - 1, lambda i, c: unsweep(NEWTON - 1 - i, *c), (dp, droot))
    dp, droot = unsweep(0, dp, droot)
    both = spread(dp, block)
    dmid = dmid + times(split(squeeze(both + both.T)), mid_s) * inv_max
    dtop = dtop - jnp.sum(dp * kept(0)[0], axis=0, keepdims=True)
    dtop = head_lane_sum(dtop, heads) * inv_max
    hit = jnp.where(cols == top, 1.0, 0.0)
    dmid = spread(dmid + dtop * hit / head_lane_sum(hit, heads), block)
    dx2 = mid * (dmid - jnp.sum(dmid * mid, axis=1, keepdims=True)) * 0.125
    dx2_s = split(dx2)
    dx1_s, dx3_s = split(dx1), split(dx3)
    kt_s, qt_s = split(k_land.T), split(q_land.T)
    dql_t = (jnp.where(block, m2r(nt, k, dx3_s), 0.0) + m3(nt, kt_s, dx2_s)) * inv_l
    dkl_t = (jnp.where(block, m2r(nt, q, dx1_s), 0.0) + m3(nn, qt_s, dx2_s)) * inv_l
    dq = m3(nn, kt_s, dx1_s) + m2l(nn, split(dql_t), member)
    dk = m3(nn, qt_s, dx3_s) + m2l(nn, split(dkl_t), member)
    corr = []
    vm = jnp.where(live, v, jnp.zeros_like(v))
    ri = lax.broadcasted_iota(jnp.int32, (128, 128), 0)
    ci = lax.broadcasted_iota(jnp.int32, (128, 128), 1)
    flip = jnp.where(ri + ci == 127, 1.0, 0.0).astype(BF)
    for h in range(heads):
        rows = g[HD * h : HD * (h + 1)]
        stack = jnp.concatenate([rows[:, 128 * b : 128 * b + 128] for b in range(slots // 128)], axis=0)
        near = tn(nn(stack, flip).astype(BF), windows(vm, h))
        near = pltpu.roll(near, 0, axis=1, stride=1, stride_axis=0)
        corr.append(jnp.sum(near, axis=0, keepdims=True))
    return dq, dk, dv, corr


N_MATS = 7
VEC_TAPS = 9
N_KEPT = 4 * NEWTON
VM = pl.BlockSpec(memory_space=pltpu.VMEM)
SM = pl.BlockSpec(memory_space=pltpu.SMEM)
HB = pl.BlockSpec(memory_space=pltpu.HBM)


def struct(shape, kind):
    return jax.ShapeDtypeStruct(shape, kind)


def cost(micros):
    return pl.CostEstimate(flops=int(micros * 1.0e9), bytes_accessed=1 << 20, transcendentals=0)


def start(pairs, sems, first=0):
    copies = [pltpu.make_async_copy(src, dst, sems.at[first + i]) for i, (src, dst) in enumerate(pairs)]
    for copy in copies:
        copy.start()
    return copies


def finish(copies):
    for copy in copies:
        copy.wait()


def forward_kernel(lengths, taps, x0, x1, x2, x3, wt, att0, att1, att2, att3, proj_h, first_h, last_h, mats_h, kept_h, att_h,
                   att_s, proj, first_s, last_s, mats, kept_s, sems):
    nar, length = lax.axis_index("narrow"), lengths[0]
    rows = x0.shape[0]
    offs = [pl.multiple_of((nar ^ r) * rows, rows) for r in range(4)]
    for r, x in enumerate((x0, x1, x2, x3)):
        proj[:, pl.ds(offs[r], rows)] = nt(wt[...], x[...]).astype(BF)
    copies = start([(proj, proj_h)], sems)
    n = wt.shape[0] // 3
    q, k, v = proj[0:n, :], proj[n:2 * n, :], proj[2 * n:3 * n, :]

    def saved(step):
        return pltpu.make_async_copy(kept_s.at[pl.ds(4 * step, 4)], kept_h.at[pl.ds(4 * step, 4)], sems.at[4 + step])

    def keep(step, arrays):
        if step == "first":
            first_s[...] = arrays
            copies.extend(start([(first_s, first_h)], sems, 1))
        elif step == "last":
            last_s[...] = arrays
            copies.extend(start([(last_s, last_h)], sems, 2))
        else:
            for i, array in enumerate(arrays):
                kept_s[4 * step + i] = array
            saved(step).start()

    kept_s[3] = jnp.zeros(kept_s.shape[1:], F32)
    att, first, last, mid, z_t, sum_t, y_t, root, k_land, q_land = core_forward(
        q, k, v, length, bands(taps, n // HD, False), keep)
    for i, m in enumerate((mid, z_t, sum_t, y_t, root, k_land, q_land)):
        mats[i] = m if i in (1, 4) else squeeze(m)
    copies += start([(mats, mats_h)], sems, 3)
    att_s[...] = att
    copies += start([(att_s, att_h)], sems, 4 + NEWTON)
    for r, out in enumerate((att0, att1, att2, att3)):
        out[...] = att_s[:, pl.ds(offs[r], rows)]
    for step in range(NEWTON):
        saved(step).wait()
    finish(copies)


def forward_call(lengths, taps, xs, wt):
    rows, width = xs[0].shape
    n = wt.shape[0] // 3
    slots = 4 * rows
    saved = [((3 * n, slots), BF), ((n, slots), F32), ((n, slots), F32), ((N_MATS, HD, n), F32), ((N_KEPT, HD, n), F32)]
    attended = struct((n, slots), BF)
    return pl.pallas_call(
        forward_kernel,
        in_specs=[SM] * 2 + [VM] * 5,
        out_specs=[VM] * 4 + [HB] * 6,
        out_shape=[struct((n, rows), BF)] * 4 + [struct(*s) for s in saved] + [attended],
        scratch_shapes=[pltpu.VMEM((n, slots), BF)]
        + [pltpu.VMEM(*s) for s in saved]
        + [pltpu.SemaphoreType.DMA((5 + NEWTON,))],
        compiler_params=pltpu.CompilerParams(vmem_limit_bytes=60 << 20),
        cost_estimate=cost(10),
        name="core_forward",
    )(lengths, taps, *xs, wt)


def backward_kernel(slotted, lengths, taps, a0, a1, a2, a3, b0, b1, b2, b3, wo, proj_h, first_h, last_h, mats_h, kept_h, att_h, x0_h, x1_h, x2_h, x3_h, wt_h,
                    dx0, dx13, dx2, *rest):
    outs, scratch = rest[:-17], rest[-17:]
    g_s, dp_s, tot_s, vec_s, out_s, x0, x1, x2, x3, wt, proj, first_s, last_s, mats, kept_s, att_s, sems = scratch
    nar, wide, length = lax.axis_index("narrow"), lax.axis_index("wide"), lengths[0]
    copies = start([(mats_h, mats), (first_h, first_s), (proj_h, proj), (last_h, last_s), (kept_h, kept_s), (att_h, att_s)], sems)
    later = start([(wt_h, wt), (x0_h, x0), (x1_h, x1), (x2_h, x2), (x3_h, x3)], sems, 6)
    rows = x0.shape[0]
    offs = [pl.multiple_of((nar ^ r) * rows, rows) for r in range(4)]
    half = rows // 2
    for r, (a, b) in enumerate(((a0, b0), (a1, b1), (a2, b2), (a3, b3))):
        g_s[:, pl.ds(offs[r], half)] = nt(wo[...], a[...]).astype(BF)
        g_s[:, pl.ds(pl.multiple_of(offs[r] + half, half), half)] = nt(wo[...], b[0:half, :]).astype(BF)
    vectors = sum(b[half:, :].astype(F32) for b in (b0, b1, b2, b3))
    n = wt.shape[0] // 3
    heads = n // HD
    band = bands(taps, heads, True)
    parts = frame(length, 4 * rows, heads)
    block = parts[0]
    finish(copies[:4])
    q, k, v = proj[0:n, :], proj[n:2 * n, :], proj[2 * n:3 * n, :]
    mid, z_t, sum_t, y_t, root, k_land, q_land = [mats[i] if i in (1, 4) else spread(mats[i], block) for i in range(N_MATS)]

    def kept(step):
        first = isinstance(step, int) and step == 0
        got = [kept_s[4 * step + i] for i in range(3 if first else 4)]
        return got + [None] if first else got

    dq, dk, dv, corr = core_backward(g_s[...], q, k, v, parts, first_s[...], last_s[...], mid, z_t, sum_t, y_t, root,
                                     kept, k_land, q_land, band, copies[4].wait)
    dp_s[0:n, :] = dq.astype(BF)
    dp_s[n:2 * n, :] = dk.astype(BF)
    dp_s[2 * n:3 * n, :] = dv.astype(BF)
    total = None
    finish(later)
    for r, x in enumerate((x0, x1, x2, x3)):
        block = dp_s[:, pl.ds(offs[r], rows)]
        back = tn(block, wt[...]).astype(BF)
        if r & 1:
            dx13[r >> 1] = back
        else:
            (dx2 if r else dx0)[...] = back
        term = nn(block, x[...])
        total = term if total is None else total + term
    copies[5].wait()
    output = None
    for r, (a, b) in enumerate(((a0, b0), (a1, b1), (a2, b2), (a3, b3))):
        term = nn(att_s[:, pl.ds(offs[r], half)], a[...])
        term = term + nn(att_s[:, pl.ds(pl.multiple_of(offs[r] + half, half), half)], b[0:half, :])
        output = term if output is None else output + term
    vec_s[...] = jnp.zeros_like(vec_s)
    lines = [vectors[i : i + 1, :] for i in range(VEC_TAPS)]
    lines += corr
    if not slotted:
        in_grad, out_grad, vec_o = outs
        in_grad[...] = total.astype(BF)
        out_grad[...] = output.astype(BF)
        for i, line in enumerate(lines):
            vec_o[i : i + 1, 0 : line.shape[1]] = line
        return
    tot_s[...] = total
    out_s[...] = output
    for i, line in enumerate(lines):
        vec_s[i >> 1, (i & 1) : (i & 1) + 1, 0 : line.shape[1]] = line
    wides = 8
    part, more = total.shape[0] // wides, output.shape[0] // wides
    for s in range(wides):
        w = s ^ wide
        slot = outs[s & 3].at[s >> 2]
        slot[0:part, :] = tot_s[pl.ds(pl.multiple_of(w * part, 8), part), :].astype(BF)
        slot[part : part + 8, :] = vec_s[w].astype(BF)
        slot[part + 8 : part + 8 + more, :] = out_s[pl.ds(pl.multiple_of(w * more, 8), more), :].astype(BF)


def backward_call(lengths, taps, attn, wo, saved, xs, wt, n_wide, slotted):
    rows, width = xs[0].shape
    n = wt.shape[0] // 3
    slots = 4 * rows
    sums = (
        [struct((2, 4 * n // n_wide + 8, width), BF)] * 4
        if slotted
        else [struct((3 * n, width), BF), struct((n, width), BF), struct((16, width), F32)]
    )
    return pl.pallas_call(
        functools.partial(backward_kernel, slotted),
        in_specs=[SM] * 2 + [VM] * 9 + [HB] * 11,
        out_specs=[VM] * (3 + len(sums)),
        out_shape=[struct((rows, width), BF), struct((2, rows, width), BF), struct((rows, width), BF)] + sums,
        scratch_shapes=[
            pltpu.VMEM((n, slots), BF),
            pltpu.VMEM((3 * n, slots), BF),
            pltpu.VMEM((3 * n, width), F32),
            pltpu.VMEM((8, 8, width), F32),
            pltpu.VMEM((n, width), F32),
        ]
        + [pltpu.VMEM((rows, width), BF)] * 4
        + [pltpu.VMEM((3 * n, width), BF)]
        + [pltpu.VMEM(s.shape, s.dtype) for s in saved]
        + [pltpu.SemaphoreType.DMA((11,))],
        compiler_params=pltpu.CompilerParams(vmem_limit_bytes=60 << 20),
        cost_estimate=cost(19),
        name="core_backward",
    )(lengths, taps, *attn, wo, *saved, *xs, wt)


EPS = 1e-05
U = [4, 8, 4]


def norm_stats(resid):
    center = jnp.mean(resid, axis=1, keepdims=True)
    centered = resid - center
    inverse = lax.rsqrt(jnp.mean(centered * centered, axis=1, keepdims=True) + EPS)
    return centered * inverse, inverse


def norm_pull(grad, normalized, inverse, gain):
    scaled = grad * gain
    return inverse * (
        scaled
        - jnp.mean(scaled, axis=1, keepdims=True)
        - normalized * jnp.mean(scaled * normalized, axis=1, keepdims=True)
    )


def total(rows):
    return jnp.sum(rows, axis=0, keepdims=True)


def ffn_kernel(slotted, x_h, a0, a1, a2, a3, w0, w1, w2, w3, g1, b1, ub, db, g2, b2, cot_h, up_h, down_h,
               mixed, res1, attn_a, attn_b, *rest):
    outs, (up, down, hid_s, slope, pre_s, hold_d, hold_u, bias_s, x, cot, sems) = rest[:-11], rest[-11:]
    chunks = 4
    ff = up.shape[1]
    size = ff // chunks
    nar, wide = lax.axis_index("narrow"), lax.axis_index("wide")

    def part(c):
        return pl.ds(pl.multiple_of(c * size, size), size)

    def up_copy(c):
        return pltpu.make_async_copy(up_h.at[:, part(c)], up.at[:, part(c)], sems.at[2 * c])

    def down_copy(c):
        return pltpu.make_async_copy(down_h.at[part(c), :], down.at[part(c), :], sems.at[2 * c + 1])

    own = start([(x_h, x)], sems, 2 * chunks)
    for c in range(chunks):
        up_copy(c).start()
        down_copy(c).start()
    own += start([(cot_h, cot)], sems, 2 * chunks + 1)
    first_sem = 2 * chunks + 2
    if slotted:
        down_to, up_to = outs[:4], outs[4:]
        n_wide, rows = 8, down_to[0].shape[3]
        group, many = 4 * rows, 4
    else:
        down_to, up_to = outs[:1], outs[1:]
        group, many = size, 1
    groups = ff // group

    def outer(left, right, hold, w, sem, targets):
        at = pl.multiple_of(w * group, group)
        hold[pl.ds(at, group), :] = tn(left[:, pl.ds(at, group)], right).astype(BF)
        if not slotted:
            pltpu.make_async_copy(hold.at[pl.ds(at, group), :], targets[0].at[pl.ds(at, group), :], sems.at[sem + w]).start()
        for n in range(4 if slotted else 0):
            block = hold.at[pl.ds(pl.multiple_of(at + n * rows, rows), rows), :]
            slot_n, slot_w = n ^ nar, w ^ wide
            core, y, x, z0, z1 = slot_n & 1, slot_n >> 1, slot_w & 1, (slot_w >> 1) & 1, slot_w >> 2
            lead, second = (x, y) if targets is down_to else (y, x)
            for i in range(4):

                @pl.when(2 * core + lead == i)
                def _():
                    pltpu.make_async_copy(
                        block, targets[i].at[second, z0, z1, pl.ds(0, rows)], sems.at[sem + 4 * w + n]
                    ).start()

    def outer_wait(hold, sem, targets):
        def one(i, carry):
            height = group // many
            block = hold.at[pl.ds(pl.multiple_of(i * height, height), height), :]
            target = targets[0].at[0, 0, 0, pl.ds(0, rows)] if slotted else targets[0].at[pl.ds(0, group), :]
            pltpu.make_async_copy(block, target, sems.at[sem + i]).wait()
            return carry

        lax.fori_loop(0, groups * many, one, 0)

    attention = tn(a0[...], w0[...]) + tn(a1[...], w1[...]) + tn(a2[...], w2[...]) + tn(a3[...], w3[...])
    own[0].wait()
    n1, inv1 = norm_stats(x[...].astype(F32) + attention)
    normed = n1 * g1[...] + b1[...]
    ffn_in = normed.astype(BF)

    def ahead(c, out):
        cut = part(c)
        up_copy(c).wait()
        pre = nn(ffn_in, up[:, cut]) + ub[:, cut]
        below = 0.5 * (1.0 + lax.erf(pre * 0.7071067811865476))
        hid = (pre * below).astype(BF)
        slope[:, cut] = below + pre * (0.3989422804014327 * jnp.exp(-0.5 * (pre * pre)))
        hid_s[:, cut] = hid
        down_copy(c).wait()
        return out + nn(hid, down[cut, :])

    out = lax.fori_loop(0, chunks, ahead, jnp.zeros(x.shape, F32), unroll=U[0])
    n2, inv2 = norm_stats(normed + (out + db[...]))
    mixed[...] = (n2 * g2[...] + b2[...]).astype(BF)
    own[1].wait()
    cotangent = cot[...].astype(F32)
    res2 = norm_pull(cotangent, n2, inv2, g2[...])
    low = res2.astype(BF)

    def down_outer(w, carry):
        outer(hid_s, low, hold_d, w, first_sem, down_to)
        return carry

    lax.fori_loop(0, groups, down_outer, 0, unroll=U[1])
    second_sem = first_sem + groups * many

    def behind(c, grad):
        cut = part(c)
        pre = nt(low, down[cut, :]) * slope[:, cut]
        bias_s[:, cut] = total(pre)
        pre = pre.astype(BF)
        pre_s[:, cut] = pre
        for i in range(groups // chunks):
            outer(pre_s, ffn_in, hold_u, c * (groups // chunks) + i, second_sem, up_to)
        return grad + nt(pre, up[:, cut])

    grad = lax.fori_loop(0, chunks, behind, res2, unroll=U[2])
    back = norm_pull(grad, n1, inv1, g1[...])
    res1[...] = back
    attn = back.astype(BF)
    half = x.shape[0] // 2
    attn_a[...] = attn[:half]
    attn_b[0:half, :] = attn[half:]
    vectors = [total(grad * n1), total(grad), total(res2), total(cotangent * n2), total(cotangent)]
    width = x.shape[1]
    vectors += [bias_s[:, width * j : width * (j + 1)] for j in range(ff // width)]
    vectors.append(jnp.zeros((attn_b.shape[0] - half - len(vectors), width), F32))
    attn_b[half:, :] = jnp.concatenate(vectors, axis=0).astype(BF)
    outer_wait(hold_d, first_sem, down_to)
    outer_wait(hold_u, second_sem, up_to)


def ffn_call(x, att, wo, g1, b1, ub, db, g2, b2, cot, up, down, n_wide, slotted):
    rows, width = x.shape
    ff = up.shape[1]
    part = ff // (4 * n_wide)
    if slotted:
        sums = [struct((2, 2, 2, part, width), BF)] * 8
    else:
        sums = [struct((ff, width), BF)] * 2
    return pl.pallas_call(
        functools.partial(ffn_kernel, slotted),
        in_specs=[HB] + [VM] * 14 + [HB] * 3,
        out_specs=[VM] * 4 + [HB] * len(sums),
        out_shape=[struct((rows, width), BF), struct((rows, width), F32)]
        + [struct((rows // 2 + more, width), BF) for more in (0, 16)]
        + sums,
        scratch_shapes=[
            pltpu.VMEM((width, ff), BF),
            pltpu.VMEM((ff, width), BF),
            pltpu.VMEM((rows, ff), BF),
            pltpu.VMEM((rows, ff), F32),
            pltpu.VMEM((rows, ff), BF),
            pltpu.VMEM((ff, width), BF),
            pltpu.VMEM((ff, width), BF),
            pltpu.VMEM((1, ff), F32),
            pltpu.VMEM((rows, width), BF),
            pltpu.VMEM((rows, width), BF),
            pltpu.SemaphoreType.DMA((10 + 64,)),
        ],
        compiler_params=pltpu.CompilerParams(vmem_limit_bytes=60 << 20),
        cost_estimate=cost(20),
        name="ffn",
    )(x, *att, *wo, g1, b1, ub, db, g2, b2, cot, up, down)


def to_slots(me, whole, n_wide):
    count = 4 * n_wide
    slot = jnp.arange(count).reshape(n_wide, 2, 2).transpose(2, 1, 0)
    picked = whole.reshape(count, -1, whole.shape[-1])[slot ^ me]
    return picked[0], picked[1]


def finish_kernel(*refs):
    pools, (input_h, output_h, taps_o, bias_o, *vec_o, vec_s, input_o, output_o, sems) = refs[:4], refs[4:]
    nar, wide = lax.axis_index("narrow"), lax.axis_index("wide")
    local, size = output_o.shape[0], bias_o.shape[0]
    part, more = 3 * local // 8, local // 8
    copies = []
    for s in (0, 4, 1, 5, 2, 6, 3, 7):
        pool, w = pools[s & 3].at[s >> 2], s ^ wide
        here = pl.ds(pl.multiple_of(w * part, 8), part)
        input_o[here, :] = pool[0:part, :].astype(F32)
        vec_s[w] = pool[part : part + 8, :].astype(F32)
        there = pl.ds(pl.multiple_of(w * more, 8), more)
        output_o[there, :] = pool[part + 8 : part + 8 + more, :].astype(F32)
        copies += start([(input_o.at[here, :], input_h.at[here, :]), (output_o.at[there, :], output_h.at[there, :])], sems, 2 * s)

    def line(i):
        return vec_s[i >> 1, (i & 1) : (i & 1) + 1, :]

    for i, out in enumerate(vec_o):
        out[...] = line(i)[0]
    for h in range(taps_o.shape[0]):
        taps_o[h : h + 1, :] = line(VEC_TAPS + h)[:, 239 : 239 + KW]
    bias = jnp.zeros((1, size), F32)
    each = vec_s.shape[2] // size
    for j in range(32):
        piece = line(5 + j // each)[:, size * (j % each) : size * (j % each + 1)]
        bias = jnp.where(4 * wide + nar == j, piece, bias)
    bias_o[...] = bias[0]
    finish(copies)


def finish_call(pools, local, heads, size):
    width = pools[0].shape[2]
    return pl.pallas_call(
        finish_kernel,
        in_specs=[VM] * 4,
        out_specs=[HB] * 2 + [VM] * 7,
        out_shape=[
            struct((3 * local, width), F32),
            struct((local, width), F32),
            struct((heads, KW), F32),
            struct((size,), F32),
        ]
        + [struct((width,), F32)] * 5,
        scratch_shapes=[pltpu.VMEM((8, 8, width), F32)]
        + [pltpu.VMEM((3 * local, width), F32), pltpu.VMEM((local, width), F32)]
        + [pltpu.SemaphoreType.DMA((16,))],
        compiler_params=pltpu.CompilerParams(vmem_limit_bytes=12 << 20),
        cost_estimate=cost(3),
        name="finish",
    )(*pools)


def build(mesh):
    n_wide, n_narrow = mesh.shape["wide"], mesh.shape["narrow"]
    count = n_wide * n_narrow
    wide_bits = []
    bit = n_narrow
    while bit < count:
        wide_bits.append(bit)
        bit *= 2

    def swap(block, mask):
        return lax.ppermute(block, AXES, [(i, i ^ mask) for i in range(count)])

    def after(value, *earlier):
        return lax.optimization_barrier((value, earlier))[0]

    def gather_relative(block):
        far = swap(block, 2)
        near = swap(block, 1)
        return [block, near, far, swap(far, 1)]

    def exchange_relative(blocks):
        return [blocks[r] if r == 0 else swap(blocks[r], r) for r in range(n_narrow)]

    class Halving:
        def __init__(self, parts, masks):
            shape = [2] * len(masks) + list(parts[0].shape[-2:])
            self.masks, self.parts = list(masks), [part.reshape(shape) for part in parts]

        def split(self, mask):
            axis = self.masks.index(mask)
            self.masks.pop(axis)
            sides = [[lax.index_in_dim(part, i, axis, keepdims=False) for part in self.parts] for i in range(2)]
            self.parts = sides[0]
            self.sent = sum(part.astype(F32) for part in sides[1]).astype(BF)
            self.mask = mask

        def send(self):
            self.parts = self.parts + [swap(self.sent, self.mask)]

        def step(self, mask):
            self.split(mask)
            self.send()

        def total(self):
            return sum(part.astype(F32) for part in self.parts)

    def gather_order(masks):
        order = [0]
        for mask in masks:
            order = order + [w ^ (mask // n_narrow) for w in order]
        return order

    def double(block, mask):
        return jnp.concatenate([block, swap(block, mask)], axis=0)

    def on_device(
        tokens,
        lengths,
        input_weights,
        output_weight,
        conv_taps,
        first_gain,
        first_bias,
        up_weight,
        up_bias,
        down_weight,
        down_bias,
        second_gain,
        second_bias,
        cotangent,
    ):
        me = lax.axis_index(AXES)
        rows, width = tokens.shape
        local_width = input_weights.shape[2]
        heads = local_width // HD
        wide = lax.axis_index("wide")
        weights_t = jnp.swapaxes(input_weights, 1, 2).reshape(3 * local_width, width)
        token_blocks = gather_relative(tokens)
        weight = after(output_weight, token_blocks[2])
        far, near = swap(weight, 2), swap(weight, 1)
        *att, s0, s1, s2, s3, s4, s5 = forward_call(lengths, conv_taps, token_blocks, weights_t)
        own_att = exchange_relative(att)
        out_rel = [output_weight, near, far, swap(after(far, att[0]), 1)]
        ff_rows = up_weight.shape[1] // count
        slotted = ff_rows % 32 == 0 and n_wide == 8

        def row(vector):
            return vector[None, :]

        mixed, res1, *rest = ffn_call(
            tokens, own_att, out_rel, row(first_gain), row(first_bias), row(up_bias), row(down_bias),
            row(second_gain), row(second_bias), cotangent, up_weight, down_weight, n_wide, slotted,
        )
        attn_a, attn_b, *rest = rest
        attn = gather_relative(attn_a) + gather_relative(attn_b)
        first, *more = wide_bits
        if slotted:

            def begin(parts, lead):
                return (parts[1].astype(F32) + swap(parts[3], 1).astype(F32)).astype(BF), parts, lead

            def go_on(begun, masks):
                sent, parts, lead = begun
                return Halving([parts[0], swap(parts[2], 1), swap(sent, lead)], masks)

            down, up = begin(rest[:4], first), begin(rest[4:], 2)
            up = (after(up[0], attn[6]),) + up[1:]
            attn = list(after(tuple(attn), down[0], up[0]))
            down, up = go_on(down, [2] + more), go_on(up, wide_bits)
        else:
            masks = [2] + wide_bits[::-1]
            same, other = to_slots(me, rest[0], n_wide)
            down = Halving([same, swap(other, 1)], masks)
            down.step(first)
            same, other = to_slots(me, rest[1], n_wide)
            up = Halving([same, swap(other, 1)], masks)
            up.step(2)
        back0, back13, back2, *sums = backward_call(
            lengths, conv_taps, attn, output_weight, [s0, s1, s2, s3, s4, s5], token_blocks, weights_t, n_wide, slotted
        )
        per_wide = -(-(VEC_TAPS + heads) // n_wide)
        near = swap(back13, 1)
        far = (back2.astype(F32) + near[1].astype(F32)).astype(BF)

        def finish_tokens(far, back0):
            return (res1 + back0.astype(F32) + near[0].astype(F32) + far.astype(F32)).astype(BF)

        if slotted:
            second, third = more

            def total(*blocks):
                return sum(block.astype(F32) for block in blocks)

            near_kept, near_sent, far_kept, far_sent = after(tuple(sums), down.parts[-1], up.parts[-1])
            far_came, near_came = swap(far_sent, first), swap(near_sent, first)
            down.parts, up.parts = after((down.parts, up.parts), far_came)
            far_sum = total(far_kept, far_came).astype(BF)
            z0_came = swap(far_sum, second)
            down.split(2)
            down.sent = after(down.sent, far_sum)
            down.send()
            far = swap(after(far, far_sum), 2)
            up.split(first)
            up.sent = after(up.sent, near_came)
            up.send()
            z1_sum = total(near_kept[1], near_came[1], z0_came[1]).astype(BF)
            own = total(near_kept[0], near_came[0], z0_came[0], swap(z1_sum, third)).astype(BF)
            pair = jnp.stack([own, swap(own, third)])
            z0_pair = swap(pair, second)
            own_x, z0_x = swap(pair, first), swap(z0_pair, first)
            back0 = after(back0, z0_pair)
            tokens_grad = finish_tokens(far, back0)

            down.split(second)
            down.sent = after(down.sent, z1_sum)
            down.send()
            up.split(second)
            up.sent = after(up.sent, own)
            up.send()
            down.step(third)
            up.step(third)
            z0_x = after(z0_x, up.sent)
            input_out, output_out, taps_out, up_bias_out, *vec = finish_call(
                [pair, own_x, z0_pair, z0_x], local_width, heads, ff_rows
            )
            input_out = jnp.swapaxes(input_out.reshape(3, local_width, width), 1, 2)
        else:
            tokens_grad = finish_tokens(swap(far, 2), back0)
            vec = sums[2][: VEC_TAPS + heads]
            vec = jnp.pad(vec, ((0, per_wide * n_wide - vec.shape[0]), (0, 0)))
            pool = [block.astype(BF).reshape(n_wide, -1, width) for block in (sums[0], sums[1], vec)]
            pool = Halving([jnp.concatenate(pool, axis=1)[jnp.arange(n_wide) ^ wide]], wide_bits[::-1])
            for mask in wide_bits:
                pool.step(mask)
            pool = pool.total().astype(BF)[None]
            for mask in wide_bits[::-1]:
                pool = double(pool, mask)
            down.step(2)
            up.step(first)
            for mask in more:
                down.step(mask)
                up.step(mask)
            order = jnp.argsort(jnp.array(gather_order(wide_bits[::-1])))[jnp.arange(n_wide) ^ wide]
            pool = pool[order].astype(F32)
            part = local_width // n_wide
            input_out = pool[:, : 3 * part].reshape(3, local_width, width).transpose(0, 2, 1)
            output_out = pool[:, 3 * part : 4 * part].reshape(local_width, width)
            vec = pool[:, 4 * part :].reshape(-1, width)
            taps_out = vec[VEC_TAPS : VEC_TAPS + heads, 239 : 239 + KW]
            up_bias_out = lax.dynamic_slice_in_dim(vec[5:VEC_TAPS].reshape(-1), me * ff_rows, ff_rows)
        down_out = down.total()
        up_out = up.total().T
        return (
            mixed,
            tokens_grad,
            input_out,
            output_out,
            taps_out,
            vec[0],
            vec[1],
            up_out,
            up_bias_out,
            down_out,
            vec[2],
            vec[3],
            vec[4],
        )

    return on_device


def solution(mesh):
    spread = P(AXES, None)
    placed = (
        spread,
        P("wide"),
        P(None, None, "narrow"),
        P("narrow", None),
        P("narrow", None),
        P(),
        P(),
        P(),
        P(),
        P(),
        P(),
        P(),
        P(),
        spread,
    )
    results = (
        spread,
        spread,
        P(None, None, "narrow"),
        P("narrow", None),
        P("narrow", None),
        P(),
        P(),
        P(None, AXES),
        P(AXES),
        spread,
        P(),
        P(),
        P(),
    )
    return jax.shard_map(
        build(mesh), mesh=mesh, in_specs=placed, out_specs=results, check_vma=False
    )
```

```python
import functools
import jax
import jax.numpy as jnp
from jax import lax
from jax.experimental import pallas as pl
from jax.experimental.pallas import tpu as pltpu
from jax.sharding import PartitionSpec as P

BF = jnp.bfloat16
F32 = jnp.float32
HD = 64
LM = 64
KW = 33
NEWTON = 6
AXES = ("wide", "narrow")


def dot(a, b, ca, cb):
    return lax.dot_general(a, b, (((ca,), (cb,)), ((), ())), preferred_element_type=F32)

def nn(a, b): return dot(a, b, 1, 0)
def nt(a, b): return dot(a, b, 1, 1)
def tn(a, b): return dot(a, b, 0, 0)

def split(a):
    hi = a.astype(BF)
    return hi, (a - hi.astype(F32)).astype(BF)

def split3(a):
    hi = a.astype(BF)
    rest = a - hi.astype(F32)
    mid = rest.astype(BF)
    return hi, mid, (rest - mid.astype(F32)).astype(BF)

def m3(op, a, b):
    return op(a[0], b[0]) + (op(a[1], b[0]) + op(a[0], b[1]))

def m6(op, a, b):
    return op(a[0], b[0]) + ((op(a[1], b[0]) + op(a[0], b[1])) + (op(a[1], b[1]) + (op(a[2], b[0]) + op(a[0], b[2]))))

def m2l(op, a, b):
    return op(a[0], b) + op(a[1], b)

def m2r(op, a, b):
    return op(a, b[0]) + op(a, b[1])


def frame(length, slots, heads):
    n = heads * LM
    row = lax.broadcasted_iota(jnp.int32, (n, n), 0)
    col = lax.broadcasted_iota(jnp.int32, (n, n), 1)
    block = (row >> 6) == (col >> 6)
    place = lax.broadcasted_iota(jnp.int32, (1, slots), 1)
    live = place < length
    mark = lax.broadcasted_iota(jnp.int32, (n, 1), 0) & (LM - 1)
    begin = (mark * length) >> 6
    end = ((mark + 1) * length) >> 6
    member = jnp.where((place >= begin) & (place < end), 1.0, 0.0).astype(BF)
    mark_l = lax.broadcasted_iota(jnp.int32, (1, n), 1) & (LM - 1)
    count_l = ((((mark_l + 1) * length) >> 6) - ((mark_l * length) >> 6)).astype(F32)
    count_s = (end - begin).astype(F32)
    return block, live, member, 1.0 / count_s, 1.0 / count_l


def head_lane_max(row, heads):
    lane = lax.broadcasted_iota(jnp.int32, row.shape, 1) >> 6
    out = jnp.zeros_like(row)
    for h in range(heads):
        top = jnp.max(jnp.where(lane == h, row, -1.0), axis=1, keepdims=True)
        out = jnp.where(lane == h, top, out)
    return out


def head_lane_sum(row, heads):
    lane = lax.broadcasted_iota(jnp.int32, row.shape, 1) >> 6
    out = jnp.zeros_like(row)
    for h in range(heads):
        total = jnp.sum(jnp.where(lane == h, row, 0.0), axis=1, keepdims=True)
        out = jnp.where(lane == h, total, out)
    return out


def windows(arr, h):
    slots = arr.shape[1]
    rows = arr[HD * h : HD * (h + 1)]
    zero = jnp.zeros((HD, 128), arr.dtype)
    wide = jnp.concatenate([zero, rows, zero], axis=1)
    return jnp.concatenate([wide[:, 128 * b : 128 * b + 384] for b in range(slots // 128)], axis=0)


def bands(taps, heads, turned):
    lane = lax.broadcasted_iota(jnp.int32, (1, 384), 1) - 112
    out = []
    for h in range(heads):
        base = jnp.zeros((1, 384), F32)
        for w in range(KW):
            base = jnp.where(lane == (KW - 1 - w if turned else w), taps[h, w], base)
        out.append(split(pltpu.roll(jnp.broadcast_to(base, (128, 384)), 0, axis=1, stride=1, stride_axis=0)))
    return out


def squeeze(matrix):
    return sum(matrix[HD * h : HD * (h + 1)] for h in range(matrix.shape[0] // HD))


def times(left, right):
    both = nn(jnp.concatenate([left[0], left[1]], axis=0), right[0])
    return both[:HD] + (both[HD:] + nn(left[0], right[1]))


def blocks(pair, block_low):
    return tuple(jnp.concatenate([part] * (block_low.shape[0] // HD), axis=0) * block_low for part in pair)


def packed_eye(n):
    row = lax.broadcasted_iota(jnp.int32, (HD, n), 0)
    lane = lax.broadcasted_iota(jnp.int32, (HD, n), 1)
    return jnp.where(row == (lane & (HD - 1)), 1.0, 0.0)


def spread(packed, block):
    return jnp.where(block, jnp.concatenate([packed] * (block.shape[0] // HD), axis=0), 0.0)


def conv_apply(arr, band, heads):
    slots = arr.shape[1]
    parts = []
    for h in range(heads):
        out = m2r(nt, windows(arr, h), band[h])
        parts.append(jnp.concatenate([out[HD * b : HD * (b + 1)] for b in range(slots // 128)], axis=1))
    return jnp.concatenate(parts, axis=0)


def core_forward(q, k, v, length, band, keep):
    n, slots = q.shape
    heads = n // HD
    block, live, member, inv_s, inv_l = frame(length, slots, heads)
    k_land = jnp.where(block, nt(member, k), 0.0) * inv_s
    q_land = jnp.where(block, nt(member, q), 0.0) * inv_s
    k3, q3 = split3(k_land), split3(q_land)
    x2 = m6(nt, q3, k3) * 0.125
    x2 = jnp.where(block, x2, -1e30)
    e2 = jnp.exp(x2 - jnp.max(x2, axis=1, keepdims=True))
    mid = e2 * (1.0 / jnp.sum(e2, axis=1, keepdims=True))
    cols = jnp.sum(mid, axis=0, keepdims=True)
    inv_max = 1.0 / head_lane_max(cols, heads)
    x3 = m2l(nn, q3[:2], k) * 0.125 + jnp.where(live, 0.0, -1e9)
    e3 = jnp.exp(x3 - jnp.max(x3, axis=1, keepdims=True))
    last = e3 * (1.0 / jnp.sum(e3, axis=1, keepdims=True))
    last_s = split(last)
    keep("last", last)
    x1 = (m2l(nn, k3[:2], q) * 0.125).reshape(heads, LM, slots)
    e1 = jnp.exp(x1 - jnp.max(x1, axis=1, keepdims=True))
    first = (e1 * (1.0 / jnp.sum(e1, axis=1, keepdims=True))).reshape(n, slots)
    first_s = split(first)
    keep("first", first)
    eye = packed_eye(n)
    low = jnp.where(block, 1.0, 0.0).astype(BF)
    mid_s = split(mid)
    mid_p = tuple(squeeze(part) for part in mid_s)
    p = m3(nt, mid_p, mid_s) * inv_max

    def powers(p):
        ps = split(p)
        pb = blocks(ps, low)
        p2 = times(ps, pb)
        p2s = split(p2)
        p3 = times(p2s, pb)
        return p2, p2s, p3, 0.25 * (13.0 * eye - 15.0 * p + 7.0 * p2 - p3)

    def onward(p, p2, p2s, p3):
        return 0.25 * (13.0 * p - 15.0 * p2 + 7.0 * p3 - times(p2s, blocks(p2s, low)))

    p2, p2s, p3, root = powers(p)
    keep(0, (p, p2, p3))
    p = onward(p, p2, p2s, p3)

    def sweep(step, carry):
        p, root = carry
        p2, p2s, p3, poly = powers(p)
        keep(step, (p, p2, p3, root))
        return onward(p, p2, p2s, p3), times(split(root), blocks(split(poly), low))

    p, root = lax.fori_loop(1, NEWTON - 1, sweep, (p, root))
    p2, p2s, p3, poly = powers(p)
    keep(NEWTON - 1, (p, p2, p3, root))
    root = times(split(root), blocks(split(poly), low))
    z_t = times(split(root), mid_s) * inv_max
    sum_t = jnp.where(block, m2r(nt, v, last_s), 0.0)
    y_t = m3(nn, split(sum_t), blocks(split(z_t), low))
    out = m3(nn, split(y_t), first_s)
    out = out + conv_apply(jnp.where(live, v, jnp.zeros_like(v)), band, heads)
    att = jnp.where(live, out, 0.0).astype(BF)
    return att, first, last, mid, z_t, sum_t, y_t, root, k_land, q_land


def core_backward(g, q, k, v, parts, first, last, mid, z_t, sum_t, y_t, root, kept, k_land, q_land, band, before_newton):
    n, slots = q.shape
    heads = n // HD
    block, live, member, inv_s, inv_l = parts
    g = jnp.where(live, g, jnp.zeros_like(g))
    first_s, last_s = split(first), split(last)
    mid_s = split(mid)
    cols = jnp.sum(mid, axis=0, keepdims=True)
    top = head_lane_max(cols, heads)
    inv_max = 1.0 / top
    low = jnp.where(block, 1.0, 0.0).astype(BF)
    zt_s = blocks(split(z_t), low)
    y = y_t.T
    dfirst = m2l(nn, split(y), g)
    dy_t = jnp.where(block, m2r(nt, g, first_s), 0.0)
    dy = dy_t.T
    dy_s, dyt_s, st_s = split(dy), split(dy_t), split(sum_t)
    s_s = split(sum_t.T)
    dz = m3(nn, dy_s, st_s)
    dz_t = m3(nn, s_s, dyt_s)
    ds_t = m3(nt, dyt_s, zt_s)
    ds = ds_t.T
    dlast = m2l(nn, split(ds), v)
    dv = m3(nn, split(ds_t), last_s)
    dv = dv + jnp.where(live, conv_apply(g, band, heads), 0.0)
    dx3 = last * (dlast - jnp.sum(dlast * last, axis=1, keepdims=True)) * 0.125
    f3 = first.reshape(heads, LM, slots)
    d3 = dfirst.reshape(heads, LM, slots)
    dx1 = (f3 * (d3 - jnp.sum(d3 * f3, axis=1, keepdims=True)) * 0.125).reshape(n, slots)
    before_newton()
    eye = packed_eye(n)
    mid_p = tuple(squeeze(part) for part in mid_s)
    dmid = times(split(root), split(dz_t)) * inv_max
    droot = times(mid_p, split(dz)) * inv_max
    dtop = -jnp.sum(squeeze(dz_t) * z_t, axis=0, keepdims=True)

    def unsweep(step, dp, droot):
        p, p2, p3, before = kept(step)
        ps, p2s = split(p), split(p2)
        pb = blocks(ps, low)
        if before is None:
            dpoly = 0.25 * droot
        else:
            poly = 0.25 * (13.0 * eye - 15.0 * p + 7.0 * p2 - p3)
            droot_s = split(droot)
            dpoly = 0.25 * times(split(before), blocks(droot_s, low))
            droot = times(droot_s, blocks(split(poly), low))
        d1, d2, d3 = -15.0 * dpoly, 7.0 * dpoly, -dpoly
        if dp is not None:
            e = 0.25 * dp
            es = split(e)
            d1 = d1 + 13.0 * e
            d2 = d2 - 15.0 * e - (times(es, blocks(p2s, low)) + times(p2s, blocks(es, low)))
            d3 = d3 + 7.0 * e
        d3s = split(d3)
        d2 = d2 + times(d3s, pb)
        d1 = d1 + times(p2s, blocks(d3s, low))
        d2s = split(d2)
        return d1 + (times(d2s, pb) + times(ps, blocks(d2s, low))), droot

    dp, droot = unsweep(NEWTON - 1, None, droot)
    dp, droot = lax.fori_loop(1, NEWTON - 1, lambda i, c: unsweep(NEWTON - 1 - i, *c), (dp, droot))
    dp, droot = unsweep(0, dp, droot)
    both = spread(dp, block)
    dmid = dmid + times(split(squeeze(both + both.T)), mid_s) * inv_max
    dtop = dtop - jnp.sum(dp * kept(0)[0], axis=0, keepdims=True)
    dtop = head_lane_sum(dtop, heads) * inv_max
    hit = jnp.where(cols == top, 1.0, 0.0)
    dmid = spread(dmid + dtop * hit / head_lane_sum(hit, heads), block)
    dx2 = mid * (dmid - jnp.sum(dmid * mid, axis=1, keepdims=True)) * 0.125
    dx2_s = split(dx2)
    dx1_s, dx3_s = split(dx1), split(dx3)
    kt_s, qt_s = split(k_land.T), split(q_land.T)
    dql_t = (jnp.where(block, m2r(nt, k, dx3_s), 0.0) + m3(nt, kt_s, dx2_s)) * inv_l
    dkl_t = (jnp.where(block, m2r(nt, q, dx1_s), 0.0) + m3(nn, qt_s, dx2_s)) * inv_l
    dq = m3(nn, kt_s, dx1_s) + m2l(nn, split(dql_t), member)
    dk = m3(nn, qt_s, dx3_s) + m2l(nn, split(dkl_t), member)
    corr = []
    vm = jnp.where(live, v, jnp.zeros_like(v))
    ri = lax.broadcasted_iota(jnp.int32, (128, 128), 0)
    ci = lax.broadcasted_iota(jnp.int32, (128, 128), 1)
    flip = jnp.where(ri + ci == 127, 1.0, 0.0).astype(BF)
    for h in range(heads):
        rows = g[HD * h : HD * (h + 1)]
        stack = jnp.concatenate([rows[:, 128 * b : 128 * b + 128] for b in range(slots // 128)], axis=0)
        near = tn(nn(stack, flip).astype(BF), windows(vm, h))
        near = pltpu.roll(near, 0, axis=1, stride=1, stride_axis=0)
        corr.append(jnp.sum(near, axis=0, keepdims=True))
    return dq, dk, dv, corr


N_MATS = 7
VEC_TAPS = 9
N_KEPT = 4 * NEWTON
VM = pl.BlockSpec(memory_space=pltpu.VMEM)
SM = pl.BlockSpec(memory_space=pltpu.SMEM)
HB = pl.BlockSpec(memory_space=pltpu.HBM)


def struct(shape, kind):
    return jax.ShapeDtypeStruct(shape, kind)


def cost(micros):
    return pl.CostEstimate(flops=int(micros * 1.0e9), bytes_accessed=1 << 20, transcendentals=0)


def start(pairs, sems, first=0):
    copies = [pltpu.make_async_copy(src, dst, sems.at[first + i]) for i, (src, dst) in enumerate(pairs)]
    for copy in copies:
        copy.start()
    return copies


def finish(copies):
    for copy in copies:
        copy.wait()


def forward_kernel(lengths, taps, x0, x1, x2, x3, wt, att0, att1, att2, att3, proj_h, first_h, last_h, mats_h, kept_h, att_h,
                   att_s, proj, first_s, last_s, mats, kept_s, sems):
    nar, length = lax.axis_index("narrow"), lengths[0]
    rows = x0.shape[0]
    offs = [pl.multiple_of((nar ^ r) * rows, rows) for r in range(4)]
    for r, x in enumerate((x0, x1, x2, x3)):
        proj[:, pl.ds(offs[r], rows)] = nt(wt[...], x[...]).astype(BF)
    copies = start([(proj, proj_h)], sems)
    n = wt.shape[0] // 3
    q, k, v = proj[0:n, :], proj[n:2 * n, :], proj[2 * n:3 * n, :]

    def saved(step):
        return pltpu.make_async_copy(kept_s.at[pl.ds(4 * step, 4)], kept_h.at[pl.ds(4 * step, 4)], sems.at[4 + step])

    def keep(step, arrays):
        if step == "first":
            first_s[...] = arrays
            copies.extend(start([(first_s, first_h)], sems, 1))
        elif step == "last":
            last_s[...] = arrays
            copies.extend(start([(last_s, last_h)], sems, 2))
        else:
            for i, array in enumerate(arrays):
                kept_s[4 * step + i] = array
            saved(step).start()

    kept_s[3] = jnp.zeros(kept_s.shape[1:], F32)
    att, first, last, mid, z_t, sum_t, y_t, root, k_land, q_land = core_forward(
        q, k, v, length, bands(taps, n // HD, False), keep)
    for i, m in enumerate((mid, z_t, sum_t, y_t, root, k_land, q_land)):
        mats[i] = m if i in (1, 4) else squeeze(m)
    copies += start([(mats, mats_h)], sems, 3)
    att_s[...] = att
    copies += start([(att_s, att_h)], sems, 4 + NEWTON)
    for r, out in enumerate((att0, att1, att2, att3)):
        out[...] = att_s[:, pl.ds(offs[r], rows)]
    for step in range(NEWTON):
        saved(step).wait()
    finish(copies)


def forward_call(lengths, taps, xs, wt):
    rows, width = xs[0].shape
    n = wt.shape[0] // 3
    slots = 4 * rows
    saved = [((3 * n, slots), BF), ((n, slots), F32), ((n, slots), F32), ((N_MATS, HD, n), F32), ((N_KEPT, HD, n), F32)]
    attended = struct((n, slots), BF)
    return pl.pallas_call(
        forward_kernel,
        in_specs=[SM] * 2 + [VM] * 5,
        out_specs=[VM] * 4 + [HB] * 6,
        out_shape=[struct((n, rows), BF)] * 4 + [struct(*s) for s in saved] + [attended],
        scratch_shapes=[pltpu.VMEM((n, slots), BF)]
        + [pltpu.VMEM(*s) for s in saved]
        + [pltpu.SemaphoreType.DMA((5 + NEWTON,))],
        compiler_params=pltpu.CompilerParams(vmem_limit_bytes=60 << 20),
        cost_estimate=cost(10),
        name="core_forward",
    )(lengths, taps, *xs, wt)


def backward_kernel(slotted, lengths, taps, a0, a1, a2, a3, wo, proj_h, first_h, last_h, mats_h, kept_h, att_h, x0_h, x1_h, x2_h, x3_h, wt_h,
                    dx0, dx13, dx2, *rest):
    outs, scratch = rest[:-17], rest[-17:]
    g_s, dp_s, tot_s, vec_s, out_s, x0, x1, x2, x3, wt, proj, first_s, last_s, mats, kept_s, att_s, sems = scratch
    nar, wide, length = lax.axis_index("narrow"), lax.axis_index("wide"), lengths[0]
    copies = start([(mats_h, mats), (first_h, first_s), (proj_h, proj), (last_h, last_s), (kept_h, kept_s), (att_h, att_s)], sems)
    later = start([(wt_h, wt), (x0_h, x0), (x1_h, x1), (x2_h, x2), (x3_h, x3)], sems, 6)
    rows = x0.shape[0]
    offs = [pl.multiple_of((nar ^ r) * rows, rows) for r in range(4)]
    for r, a in enumerate((a0, a1, a2, a3)):
        g_s[:, pl.ds(offs[r], rows)] = nt(wo[...], a[0:rows, :]).astype(BF)
    vectors = sum(a[rows:, :].astype(F32) for a in (a0, a1, a2, a3))
    n = wt.shape[0] // 3
    heads = n // HD
    band = bands(taps, heads, True)
    parts = frame(length, 4 * rows, heads)
    block = parts[0]
    finish(copies[:4])
    q, k, v = proj[0:n, :], proj[n:2 * n, :], proj[2 * n:3 * n, :]
    mid, z_t, sum_t, y_t, root, k_land, q_land = [mats[i] if i in (1, 4) else spread(mats[i], block) for i in range(N_MATS)]

    def kept(step):
        first = isinstance(step, int) and step == 0
        got = [kept_s[4 * step + i] for i in range(3 if first else 4)]
        return got + [None] if first else got

    dq, dk, dv, corr = core_backward(g_s[...], q, k, v, parts, first_s[...], last_s[...], mid, z_t, sum_t, y_t, root,
                                     kept, k_land, q_land, band, copies[4].wait)
    dp_s[0:n, :] = dq.astype(BF)
    dp_s[n:2 * n, :] = dk.astype(BF)
    dp_s[2 * n:3 * n, :] = dv.astype(BF)
    total = None
    finish(later)
    for r, x in enumerate((x0, x1, x2, x3)):
        block = dp_s[:, pl.ds(offs[r], rows)]
        back = tn(block, wt[...]).astype(BF)
        if r & 1:
            dx13[r >> 1] = back
        else:
            (dx2 if r else dx0)[...] = back
        term = nn(block, x[...])
        total = term if total is None else total + term
    copies[5].wait()
    output = None
    for r, a in enumerate((a0, a1, a2, a3)):
        term = nn(att_s[:, pl.ds(offs[r], rows)], a[0:rows, :])
        output = term if output is None else output + term
    vec_s[...] = jnp.zeros_like(vec_s)
    lines = [vectors[i : i + 1, :] for i in range(VEC_TAPS)]
    lines += corr
    if not slotted:
        in_grad, out_grad, vec_o = outs
        in_grad[...] = total.astype(BF)
        out_grad[...] = output.astype(BF)
        for i, line in enumerate(lines):
            vec_o[i : i + 1, 0 : line.shape[1]] = line
        return
    tot_s[...] = total
    out_s[...] = output
    for i, line in enumerate(lines):
        vec_s[i >> 1, (i & 1) : (i & 1) + 1, 0 : line.shape[1]] = line
    wides = 8
    part, more = total.shape[0] // wides, output.shape[0] // wides
    for s in range(wides):
        w = s ^ wide
        slot = outs[s & 3].at[s >> 2]
        slot[0:part, :] = tot_s[pl.ds(pl.multiple_of(w * part, 8), part), :].astype(BF)
        slot[part : part + 8, :] = vec_s[w].astype(BF)
        slot[part + 8 : part + 8 + more, :] = out_s[pl.ds(pl.multiple_of(w * more, 8), more), :].astype(BF)


def backward_call(lengths, taps, attn, wo, saved, xs, wt, n_wide, slotted):
    rows, width = xs[0].shape
    n = wt.shape[0] // 3
    slots = 4 * rows
    sums = (
        [struct((2, 4 * n // n_wide + 8, width), BF)] * 4
        if slotted
        else [struct((3 * n, width), BF), struct((n, width), BF), struct((16, width), F32)]
    )
    return pl.pallas_call(
        functools.partial(backward_kernel, slotted),
        in_specs=[SM] * 2 + [VM] * 5 + [HB] * 11,
        out_specs=[VM] * (3 + len(sums)),
        out_shape=[struct((rows, width), BF), struct((2, rows, width), BF), struct((rows, width), BF)] + sums,
        scratch_shapes=[
            pltpu.VMEM((n, slots), BF),
            pltpu.VMEM((3 * n, slots), BF),
            pltpu.VMEM((3 * n, width), F32),
            pltpu.VMEM((8, 8, width), F32),
            pltpu.VMEM((n, width), F32),
        ]
        + [pltpu.VMEM((rows, width), BF)] * 4
        + [pltpu.VMEM((3 * n, width), BF)]
        + [pltpu.VMEM(s.shape, s.dtype) for s in saved]
        + [pltpu.SemaphoreType.DMA((11,))],
        compiler_params=pltpu.CompilerParams(vmem_limit_bytes=60 << 20),
        cost_estimate=cost(19),
        name="core_backward",
    )(lengths, taps, *attn, wo, *saved, *xs, wt)


EPS = 1e-05
U = [4, 8, 4]


def norm_stats(resid):
    center = jnp.mean(resid, axis=1, keepdims=True)
    centered = resid - center
    inverse = lax.rsqrt(jnp.mean(centered * centered, axis=1, keepdims=True) + EPS)
    return centered * inverse, inverse


def norm_pull(grad, normalized, inverse, gain):
    scaled = grad * gain
    return inverse * (
        scaled
        - jnp.mean(scaled, axis=1, keepdims=True)
        - normalized * jnp.mean(scaled * normalized, axis=1, keepdims=True)
    )


def total(rows):
    return jnp.sum(rows, axis=0, keepdims=True)


def ffn_kernel(slotted, x_h, a0, a1, a2, a3, w0, w1, w2, w3, g1, b1, ub, db, g2, b2, cot_h, up_h, down_h,
               mixed, res1, attn_o, *rest):
    outs, (up, down, hid_s, slope, pre_s, hold_d, hold_u, bias_s, x, cot, sems) = rest[:-11], rest[-11:]
    chunks = 4
    ff = up.shape[1]
    size = ff // chunks
    nar, wide = lax.axis_index("narrow"), lax.axis_index("wide")

    def part(c):
        return pl.ds(pl.multiple_of(c * size, size), size)

    def up_copy(c):
        return pltpu.make_async_copy(up_h.at[:, part(c)], up.at[:, part(c)], sems.at[2 * c])

    def down_copy(c):
        return pltpu.make_async_copy(down_h.at[part(c), :], down.at[part(c), :], sems.at[2 * c + 1])

    own = start([(x_h, x)], sems, 2 * chunks)
    for c in range(chunks):
        up_copy(c).start()
        down_copy(c).start()
    own += start([(cot_h, cot)], sems, 2 * chunks + 1)
    first_sem = 2 * chunks + 2
    if slotted:
        down_to, up_to = outs[:4], outs[4:]
        n_wide, rows = 8, down_to[0].shape[3]
        group, many = 4 * rows, 4
    else:
        down_to, up_to = outs[:1], outs[1:]
        group, many = size, 1
    groups = ff // group

    def outer(left, right, hold, w, sem, targets):
        at = pl.multiple_of(w * group, group)
        hold[pl.ds(at, group), :] = tn(left[:, pl.ds(at, group)], right).astype(BF)
        if not slotted:
            pltpu.make_async_copy(hold.at[pl.ds(at, group), :], targets[0].at[pl.ds(at, group), :], sems.at[sem + w]).start()
        for n in range(4 if slotted else 0):
            block = hold.at[pl.ds(pl.multiple_of(at + n * rows, rows), rows), :]
            slot_n, slot_w = n ^ nar, w ^ wide
            core, y, x, z0, z1 = slot_n & 1, slot_n >> 1, slot_w & 1, (slot_w >> 1) & 1, slot_w >> 2
            lead, second = (x, y) if targets is down_to else (y, x)
            for i in range(4):

                @pl.when(2 * core + lead == i)
                def _():
                    pltpu.make_async_copy(
                        block, targets[i].at[second, z0, z1, pl.ds(0, rows)], sems.at[sem + 4 * w + n]
                    ).start()

    def outer_wait(hold, sem, targets):
        def one(i, carry):
            height = group // many
            block = hold.at[pl.ds(pl.multiple_of(i * height, height), height), :]
            target = targets[0].at[0, 0, 0, pl.ds(0, rows)] if slotted else targets[0].at[pl.ds(0, group), :]
            pltpu.make_async_copy(block, target, sems.at[sem + i]).wait()
            return carry

        lax.fori_loop(0, groups * many, one, 0)

    attention = tn(a0[...], w0[...]) + tn(a1[...], w1[...]) + tn(a2[...], w2[...]) + tn(a3[...], w3[...])
    own[0].wait()
    n1, inv1 = norm_stats(x[...].astype(F32) + attention)
    normed = n1 * g1[...] + b1[...]
    ffn_in = normed.astype(BF)

    def ahead(c, out):
        cut = part(c)
        up_copy(c).wait()
        pre = nn(ffn_in, up[:, cut]) + ub[:, cut]
        below = 0.5 * (1.0 + lax.erf(pre * 0.7071067811865476))
        hid = (pre * below).astype(BF)
        slope[:, cut] = below + pre * (0.3989422804014327 * jnp.exp(-0.5 * (pre * pre)))
        hid_s[:, cut] = hid
        down_copy(c).wait()
        return out + nn(hid, down[cut, :])

    out = lax.fori_loop(0, chunks, ahead, jnp.zeros(x.shape, F32), unroll=U[0])
    n2, inv2 = norm_stats(normed + (out + db[...]))
    mixed[...] = (n2 * g2[...] + b2[...]).astype(BF)
    own[1].wait()
    cotangent = cot[...].astype(F32)
    res2 = norm_pull(cotangent, n2, inv2, g2[...])
    low = res2.astype(BF)

    def down_outer(w, carry):
        outer(hid_s, low, hold_d, w, first_sem, down_to)
        return carry

    lax.fori_loop(0, groups, down_outer, 0, unroll=U[1])
    second_sem = first_sem + groups * many

    def behind(c, grad):
        cut = part(c)
        pre = nt(low, down[cut, :]) * slope[:, cut]
        bias_s[:, cut] = total(pre)
        pre = pre.astype(BF)
        pre_s[:, cut] = pre
        for i in range(groups // chunks):
            outer(pre_s, ffn_in, hold_u, c * (groups // chunks) + i, second_sem, up_to)
        return grad + nt(pre, up[:, cut])

    grad = lax.fori_loop(0, chunks, behind, res2, unroll=U[2])
    back = norm_pull(grad, n1, inv1, g1[...])
    res1[...] = back
    attn = back.astype(BF)
    tokens = x.shape[0]
    attn_o[0:tokens, :] = attn
    vectors = [total(grad * n1), total(grad), total(res2), total(cotangent * n2), total(cotangent)]
    width = x.shape[1]
    vectors += [bias_s[:, width * j : width * (j + 1)] for j in range(ff // width)]
    vectors.append(jnp.zeros((attn_o.shape[0] - tokens - len(vectors), width), F32))
    attn_o[tokens:, :] = jnp.concatenate(vectors, axis=0).astype(BF)
    outer_wait(hold_d, first_sem, down_to)
    outer_wait(hold_u, second_sem, up_to)


def ffn_call(x, att, wo, g1, b1, ub, db, g2, b2, cot, up, down, n_wide, slotted):
    rows, width = x.shape
    ff = up.shape[1]
    part = ff // (4 * n_wide)
    if slotted:
        sums = [struct((2, 2, 2, part, width), BF)] * 8
    else:
        sums = [struct((ff, width), BF)] * 2
    return pl.pallas_call(
        functools.partial(ffn_kernel, slotted),
        in_specs=[HB] + [VM] * 14 + [HB] * 3,
        out_specs=[VM] * 3 + [HB] * len(sums),
        out_shape=[struct((rows, width), BF), struct((rows, width), F32)]
        + [struct((rows + 16, width), BF)]
        + sums,
        scratch_shapes=[
            pltpu.VMEM((width, ff), BF),
            pltpu.VMEM((ff, width), BF),
            pltpu.VMEM((rows, ff), BF),
            pltpu.VMEM((rows, ff), F32),
            pltpu.VMEM((rows, ff), BF),
            pltpu.VMEM((ff, width), BF),
            pltpu.VMEM((ff, width), BF),
            pltpu.VMEM((1, ff), F32),
            pltpu.VMEM((rows, width), BF),
            pltpu.VMEM((rows, width), BF),
            pltpu.SemaphoreType.DMA((10 + 64,)),
        ],
        compiler_params=pltpu.CompilerParams(vmem_limit_bytes=60 << 20),
        cost_estimate=cost(20),
        name="ffn",
    )(x, *att, *wo, g1, b1, ub, db, g2, b2, cot, up, down)


def to_slots(me, whole, n_wide):
    count = 4 * n_wide
    slot = jnp.arange(count).reshape(n_wide, 2, 2).transpose(2, 1, 0)
    picked = whole.reshape(count, -1, whole.shape[-1])[slot ^ me]
    return picked[0], picked[1]


def finish_kernel(*refs):
    pools, (input_h, output_h, taps_o, bias_o, *vec_o, vec_s, input_o, output_o, sems) = refs[:4], refs[4:]
    nar, wide = lax.axis_index("narrow"), lax.axis_index("wide")
    local, size = output_o.shape[0], bias_o.shape[0]
    part, more = 3 * local // 8, local // 8
    copies = []
    for s in (0, 4, 1, 5, 2, 6, 3, 7):
        pool, w = pools[s & 3].at[s >> 2], s ^ wide
        here = pl.ds(pl.multiple_of(w * part, 8), part)
        input_o[here, :] = pool[0:part, :].astype(F32)
        vec_s[w] = pool[part : part + 8, :].astype(F32)
        there = pl.ds(pl.multiple_of(w * more, 8), more)
        output_o[there, :] = pool[part + 8 : part + 8 + more, :].astype(F32)
        copies += start([(input_o.at[here, :], input_h.at[here, :]), (output_o.at[there, :], output_h.at[there, :])], sems, 2 * s)

    def line(i):
        return vec_s[i >> 1, (i & 1) : (i & 1) + 1, :]

    for i, out in enumerate(vec_o):
        out[...] = line(i)[0]
    for h in range(taps_o.shape[0]):
        taps_o[h : h + 1, :] = line(VEC_TAPS + h)[:, 239 : 239 + KW]
    bias = jnp.zeros((1, size), F32)
    each = vec_s.shape[2] // size
    for j in range(32):
        piece = line(5 + j // each)[:, size * (j % each) : size * (j % each + 1)]
        bias = jnp.where(4 * wide + nar == j, piece, bias)
    bias_o[...] = bias[0]
    finish(copies)


def finish_call(pools, local, heads, size):
    width = pools[0].shape[2]
    return pl.pallas_call(
        finish_kernel,
        in_specs=[VM] * 4,
        out_specs=[HB] * 2 + [VM] * 7,
        out_shape=[
            struct((3 * local, width), F32),
            struct((local, width), F32),
            struct((heads, KW), F32),
            struct((size,), F32),
        ]
        + [struct((width,), F32)] * 5,
        scratch_shapes=[pltpu.VMEM((8, 8, width), F32)]
        + [pltpu.VMEM((3 * local, width), F32), pltpu.VMEM((local, width), F32)]
        + [pltpu.SemaphoreType.DMA((16,))],
        compiler_params=pltpu.CompilerParams(vmem_limit_bytes=12 << 20),
        cost_estimate=cost(3),
        name="finish",
    )(*pools)


def build(mesh):
    n_wide, n_narrow = mesh.shape["wide"], mesh.shape["narrow"]
    count = n_wide * n_narrow
    wide_bits = []
    bit = n_narrow
    while bit < count:
        wide_bits.append(bit)
        bit *= 2

    def swap(block, mask):
        return lax.ppermute(block, AXES, [(i, i ^ mask) for i in range(count)])

    def after(value, *earlier):
        return lax.optimization_barrier((value, earlier))[0]

    def gather_relative(block):
        far = swap(block, 2)
        near = swap(block, 1)
        return [block, near, far, swap(far, 1)]

    def exchange_relative(blocks):
        return [blocks[r] if r == 0 else swap(blocks[r], r) for r in range(n_narrow)]

    class Halving:
        def __init__(self, parts, masks):
            shape = [2] * len(masks) + list(parts[0].shape[-2:])
            self.masks, self.parts = list(masks), [part.reshape(shape) for part in parts]

        def split(self, mask):
            axis = self.masks.index(mask)
            self.masks.pop(axis)
            sides = [[lax.index_in_dim(part, i, axis, keepdims=False) for part in self.parts] for i in range(2)]
            self.parts = sides[0]
            self.sent = sum(part.astype(F32) for part in sides[1]).astype(BF)
            self.mask = mask

        def send(self):
            self.parts = self.parts + [swap(self.sent, self.mask)]

        def step(self, mask):
            self.split(mask)
            self.send()

        def total(self):
            return sum(part.astype(F32) for part in self.parts)

    def gather_order(masks):
        order = [0]
        for mask in masks:
            order = order + [w ^ (mask // n_narrow) for w in order]
        return order

    def double(block, mask):
        return jnp.concatenate([block, swap(block, mask)], axis=0)

    def on_device(
        tokens,
        lengths,
        input_weights,
        output_weight,
        conv_taps,
        first_gain,
        first_bias,
        up_weight,
        up_bias,
        down_weight,
        down_bias,
        second_gain,
        second_bias,
        cotangent,
    ):
        me = lax.axis_index(AXES)
        rows, width = tokens.shape
        local_width = input_weights.shape[2]
        heads = local_width // HD
        wide = lax.axis_index("wide")
        weights_t = jnp.swapaxes(input_weights, 1, 2).reshape(3 * local_width, width)
        token_blocks = gather_relative(tokens)
        weight = after(output_weight, token_blocks[2])
        far, near = swap(weight, 2), swap(weight, 1)
        *att, s0, s1, s2, s3, s4, s5 = forward_call(lengths, conv_taps, token_blocks, weights_t)
        own_att = exchange_relative(att)
        out_rel = [output_weight, near, far, swap(after(far, att[0]), 1)]
        ff_rows = up_weight.shape[1] // count
        slotted = ff_rows % 32 == 0 and n_wide == 8

        def row(vector):
            return vector[None, :]

        mixed, res1, *rest = ffn_call(
            tokens, own_att, out_rel, row(first_gain), row(first_bias), row(up_bias), row(down_bias),
            row(second_gain), row(second_bias), cotangent, up_weight, down_weight, n_wide, slotted,
        )
        attn, *rest = rest
        attn = gather_relative(attn)
        first, *more = wide_bits
        if slotted:

            def begin(parts, lead):
                return (parts[1].astype(F32) + swap(parts[3], 1).astype(F32)).astype(BF), parts, lead

            def go_on(begun, masks):
                sent, parts, lead = begun
                return Halving([parts[0], swap(parts[2], 1), swap(sent, lead)], masks)

            down, up = begin(rest[:4], first), begin(rest[4:], 2)
            up = (after(up[0], attn[2]),) + up[1:]
            attn = list(after(tuple(attn), down[0], up[0]))
            down, up = go_on(down, [2] + more), go_on(up, wide_bits)
        else:
            masks = [2] + wide_bits[::-1]
            same, other = to_slots(me, rest[0], n_wide)
            down = Halving([same, swap(other, 1)], masks)
            down.step(first)
            same, other = to_slots(me, rest[1], n_wide)
            up = Halving([same, swap(other, 1)], masks)
            up.step(2)
        back0, back13, back2, *sums = backward_call(
            lengths, conv_taps, attn, output_weight, [s0, s1, s2, s3, s4, s5], token_blocks, weights_t, n_wide, slotted
        )
        per_wide = -(-(VEC_TAPS + heads) // n_wide)
        near = swap(back13, 1)
        far = (back2.astype(F32) + near[1].astype(F32)).astype(BF)

        def finish_tokens(far, back0):
            return (res1 + back0.astype(F32) + near[0].astype(F32) + far.astype(F32)).astype(BF)

        if slotted:
            second, third = more

            def total(*blocks):
                return sum(block.astype(F32) for block in blocks)

            near_kept, near_sent, far_kept, far_sent = after(tuple(sums), down.parts[-1], up.parts[-1])
            far_came, near_came = swap(far_sent, first), swap(near_sent, first)
            down.parts, up.parts = after((down.parts, up.parts), far_came)
            far_sum = total(far_kept, far_came).astype(BF)
            z0_came = swap(far_sum, second)
            down.split(2)
            down.sent = after(down.sent, far_sum)
            down.send()
            far = swap(after(far, far_sum), 2)
            up.split(first)
            up.sent = after(up.sent, near_came)
            up.send()
            z1_sum = total(near_kept[1], near_came[1], z0_came[1]).astype(BF)
            own = total(near_kept[0], near_came[0], z0_came[0], swap(z1_sum, third)).astype(BF)
            pair = jnp.stack([own, swap(own, third)])
            z0_pair = swap(pair, second)
            own_x, z0_x = swap(pair, first), swap(z0_pair, first)
            back0 = after(back0, z0_pair)
            tokens_grad = finish_tokens(far, back0)

            down.split(second)
            down.sent = after(down.sent, z1_sum)
            down.send()
            up.split(second)
            up.sent = after(up.sent, own)
            up.send()
            down.step(third)
            up.step(third)
            z0_x = after(z0_x, up.sent)
            input_out, output_out, taps_out, up_bias_out, *vec = finish_call(
                [pair, own_x, z0_pair, z0_x], local_width, heads, ff_rows
            )
            input_out = jnp.swapaxes(input_out.reshape(3, local_width, width), 1, 2)
        else:
            tokens_grad = finish_tokens(swap(far, 2), back0)
            vec = sums[2][: VEC_TAPS + heads]
            vec = jnp.pad(vec, ((0, per_wide * n_wide - vec.shape[0]), (0, 0)))
            pool = [block.astype(BF).reshape(n_wide, -1, width) for block in (sums[0], sums[1], vec)]
            pool = Halving([jnp.concatenate(pool, axis=1)[jnp.arange(n_wide) ^ wide]], wide_bits[::-1])
            for mask in wide_bits:
                pool.step(mask)
            pool = pool.total().astype(BF)[None]
            for mask in wide_bits[::-1]:
                pool = double(pool, mask)
            down.step(2)
            up.step(first)
            for mask in more:
                down.step(mask)
                up.step(mask)
            order = jnp.argsort(jnp.array(gather_order(wide_bits[::-1])))[jnp.arange(n_wide) ^ wide]
            pool = pool[order].astype(F32)
            part = local_width // n_wide
            input_out = pool[:, : 3 * part].reshape(3, local_width, width).transpose(0, 2, 1)
            output_out = pool[:, 3 * part : 4 * part].reshape(local_width, width)
            vec = pool[:, 4 * part :].reshape(-1, width)
            taps_out = vec[VEC_TAPS : VEC_TAPS + heads, 239 : 239 + KW]
            up_bias_out = lax.dynamic_slice_in_dim(vec[5:VEC_TAPS].reshape(-1), me * ff_rows, ff_rows)
        down_out = down.total()
        up_out = up.total().T
        return (
            mixed,
            tokens_grad,
            input_out,
            output_out,
            taps_out,
            vec[0],
            vec[1],
            up_out,
            up_bias_out,
            down_out,
            vec[2],
            vec[3],
            vec[4],
        )

    return on_device


def solution(mesh):
    spread = P(AXES, None)
    placed = (
        spread,
        P("wide"),
        P(None, None, "narrow"),
        P("narrow", None),
        P("narrow", None),
        P(),
        P(),
        P(),
        P(),
        P(),
        P(),
        P(),
        P(),
        spread,
    )
    results = (
        spread,
        spread,
        P(None, None, "narrow"),
        P("narrow", None),
        P("narrow", None),
        P(),
        P(),
        P(None, AXES),
        P(AXES),
        spread,
        P(),
        P(),
        P(),
    )
    return jax.shard_map(
        build(mesh), mesh=mesh, in_specs=placed, out_specs=results, check_vma=False
    )
```
